32 devices in a mesh: depth: 16 (over z, y, x), light: 2 (over core).
Axes of the slice: x: 2, y: 2, z: 4, core: 2. Of those that a mesh axis runs over, the one named last changes fastest.
Arguments:
- density: float32 [64, 128, 1024], P('depth', 'light'), may hold values from -6 to 6
- labels: int32 [64, 128, 1024], P('depth', 'light'), may hold values from 0 to 15
- slice_order: int32 [64], P('depth'), may hold values from 0 to 63, as said below
- extinction: float32 [16], replicated, may hold values from 0.0001 to 0.01
- albedo: float32 [3, 16], replicated, may hold values from 0.2 to 1
Outputs:
- image: float32 [4, 131072], P(None, ('light', 'depth'))
The draws below stay inside these ranges and needn't reach their ends.
Inputs may be any that keep to these rules, and one draw needn't show every extreme that they name: Within each aligned block of 4 view positions, slice_order is a permutation of that block's positions.
All inputs are finite; a program needn't handle non-finite values.
Results may differ from the reference program's by a relative error of at most 0.0003.
Values sent between devices are 32-bit elements; how exact they have to be, the bound alone decides.
A program may use at most 64 MiB of HBM per device.

```python
import math
import jax
import jax.numpy as jnp
from jax import lax

DZ = 4
IMAGE_COLUMNS = 1024
NMAT = 16
DEPTH_SLICES = 64
LIGHT_CELLS = 128


def draw_labels(key, part):
    random_keys = jax.random.split(jax.random.fold_in(key, 17), 3)
    ground_label = jax.random.randint(random_keys[0], (DEPTH_SLICES // DZ, 1, IMAGE_COLUMNS), 0, NMAT)
    ground_label = jnp.repeat(ground_label, DZ, axis=0)
    jitter_label = jax.random.randint(random_keys[1], (DEPTH_SLICES, LIGHT_CELLS, IMAGE_COLUMNS), 0, NMAT)
    flare_mask = jax.random.randint(random_keys[2], (DEPTH_SLICES, LIGHT_CELLS, IMAGE_COLUMNS), 0, 8) == 0
    return jnp.where(flare_mask, jitter_label, ground_label).astype(jnp.int32)


def draw_slice_order(key, part):
    bricks = DEPTH_SLICES // DZ
    random_keys = jax.random.split(jax.random.fold_in(key, 29), bricks)
    shuffled = jax.vmap(lambda one_key: jax.random.permutation(one_key, DZ))(random_keys)
    offsets = jnp.arange(bricks, dtype=jnp.int32)[:, None] * DZ
    return (shuffled.astype(jnp.int32) + offsets).reshape(DEPTH_SLICES).astype(jnp.int32)


def steps_of(rng, extent, cuts, least, largest):
    level = 1.0
    for dim, parts in cuts:
        steps = jax.random.uniform(jax.random.fold_in(jax.random.fold_in(rng, 6), dim), (parts,), jnp.float32, least / len(cuts), largest / len(cuts))
        level = level * jnp.repeat(jnp.exp(steps), extent[dim] // parts).reshape((-1,) + (1,) * (len(extent) - 1 - dim))
    return level


def scatter_about(own_key, extent, spread, reach, shards=(), held_as=jnp.bfloat16):
    entries = jax.random.normal(own_key, extent, jnp.float32) * spread
    if len(shards) > 0:
        entries = steps_of(own_key, extent, shards, -0.22, 0.18) * entries
    return jnp.clip(entries, min=-reach, max=reach).astype(held_as)


def setup_inputs(seed: int = 0) -> dict:
    seeds = jax.random.split(jax.random.key(seed), 6)
    return {
        "density": scatter_about(seeds[0], (DEPTH_SLICES, LIGHT_CELLS, IMAGE_COLUMNS), 1.0, 6.0, ((0, 16), (1, 2)), jnp.float32),
        "labels": draw_labels(jax.random.fold_in(seeds[5], 71), 0),
        "slice_order": draw_slice_order(jax.random.fold_in(seeds[5], 71), 0),
        "extinction": jnp.clip(jnp.exp(jax.random.uniform(seeds[3], (NMAT,), jnp.float32, math.log(0.0001), math.log(0.01))), 0.0001, 0.01),
        "albedo": jnp.clip(jax.random.uniform(seeds[4], (3, NMAT), jnp.float32, 0.2, 1.0), 0.2, 1.0),
    }


def smooth_field(padded):
    center = padded[1:-1, 1:-1, 1:-1]
    beside = padded[2:, 1:-1, 1:-1] + padded[:-2, 1:-1, 1:-1]
    beside = beside + padded[1:-1, 2:, 1:-1] + padded[1:-1, :-2, 1:-1]
    beside = beside + padded[1:-1, 1:-1, 2:] + padded[1:-1, 1:-1, :-2]
    return 0.4 * center + 0.1 * beside

def gradient_parts(padded):
    center = padded[1:-1, 1:-1, 1:-1]
    grad_z = 0.5 * (padded[2:, 1:-1, 1:-1] - padded[:-2, 1:-1, 1:-1])
    grad_x = 0.5 * (padded[1:-1, 2:, 1:-1] - padded[1:-1, :-2, 1:-1])
    grad_y = 0.5 * (padded[1:-1, 1:-1, 2:] - padded[1:-1, 1:-1, :-2])
    return (center, grad_z, grad_x, grad_y)

def material_props(materials, extinction, albedo):
    lookup_table = jnp.concatenate([extinction[None, :], albedo], axis=0)
    result = jnp.zeros((4,) + materials.shape, jnp.float32)
    for number in range(NMAT):
        result = jnp.where(materials[None] == number, lookup_table[:, number][:, None, None, None], result)
    return result

def exclusive_sum(values, axis):
    total = jnp.cumsum(values, axis=axis)
    shifted = lax.slice_in_dim(total, 0, values.shape[axis] - 1, axis=axis)
    zero_shape = list(values.shape)
    zero_shape[axis] = 1
    return jnp.concatenate([jnp.zeros(zero_shape, jnp.float32), shifted], axis=axis)

def reference(density, labels, slice_order, extinction, albedo):

    def advance(state_pair, brick_index):
        colour_sum, remaining = state_pair
        view_pos = brick_index * DZ - 2 + jnp.arange(DZ + 4, dtype=jnp.int32)
        inside = (view_pos >= 0) & (view_pos < DEPTH_SLICES)
        stored = jnp.take(slice_order, jnp.clip(view_pos, 0, DEPTH_SLICES - 1).astype(jnp.int32))
        slab_rows = jnp.take(density, stored, axis=0) * inside[:, None, None].astype(jnp.float32)
        padded = jnp.pad(slab_rows, ((0, 0), (2, 2), (2, 2)))
        smoothed = smooth_field(padded)
        x_pos = jnp.arange(LIGHT_CELLS + 2, dtype=jnp.int32)
        y_pos = jnp.arange(IMAGE_COLUMNS + 2, dtype=jnp.int32)
        inside_x = (x_pos >= 1) & (x_pos <= LIGHT_CELLS)
        inside_y = (y_pos >= 1) & (y_pos <= IMAGE_COLUMNS)
        keep_mask = inside[1:-1][:, None, None] & inside_x[None, :, None] & inside_y[None, None, :]
        smoothed = jnp.where(keep_mask, smoothed, jnp.float32(0.0))
        center, grad_z, grad_x, grad_y = gradient_parts(smoothed)
        own_pos = (brick_index * DZ + jnp.arange(DZ, dtype=jnp.int32)).astype(jnp.int32)
        materials = jnp.take(labels, jnp.take(slice_order, own_pos), axis=0)
        material = material_props(materials, extinction, albedo)
        optical = material[0] * jnp.exp(center)
        lighted = jnp.exp(-exclusive_sum(optical, 1))
        opacity = 1.0 - jnp.exp(-optical)
        facing = grad_x / jnp.sqrt(grad_z * grad_z + grad_x * grad_x + grad_y * grad_y + 0.05)
        shading = 0.2 + lighted * (0.5 + 0.5 * facing)
        weight = opacity * shading * jnp.exp(-exclusive_sum(optical, 0))
        colour = lax.optimization_barrier(jnp.sum(material[1:] * weight[None], axis=1))
        colour_sum = colour_sum + remaining[None] * colour
        remaining = remaining * jnp.exp(-lax.optimization_barrier(jnp.sum(optical, axis=0)))
        return ((colour_sum, remaining), brick_index)
    initial = (jnp.zeros((3, LIGHT_CELLS, IMAGE_COLUMNS), jnp.float32), jnp.ones((LIGHT_CELLS, IMAGE_COLUMNS), jnp.float32))
    final_pair, unused = lax.scan(advance, initial, jnp.arange(DEPTH_SLICES // DZ, dtype=jnp.int32))
    colour_sum, remaining = final_pair
    return jnp.concatenate([colour_sum, (1.0 - remaining)[None]], axis=0).reshape(4, LIGHT_CELLS * IMAGE_COLUMNS)
```

```python
import functools

import jax
import jax.numpy as jnp
from jax import lax
from jax.experimental import pallas as pl
from jax.experimental.pallas import tpu as pltpu
from jax.sharding import PartitionSpec as P

SUB, LANE = 8, 128
GROUP, PAIR = 4, 2
PARTS = GROUP * PAIR
CHUNKS = 8
EDGE = 2 * SUB
MESH = pl.DeviceIdType.MESH
FAR = pl.BlockSpec(memory_space=pltpu.HBM)
ORDER = (3, 1, 2)


def flip(value, mask):
    for bit in (1, 2):
        if mask & bit:
            value = value + bit * (1 - 2 * ((value // bit) % 2))
    return value


def lookup(table, index):
    return jnp.take_along_axis(table, index, axis=1, mode="promise_in_bounds")


def render_kernel(
    depth_count, light_count,
    density_far, labels_far, order_far, extinction_far, albedo_far,
    out,
    density, labels, order, extinction, albedo,
    bricks, strips, labels_out, column_labels, volume, halo_strips, materials,
    smooth, heat, turned, parts_out, parts_in, blended, lights_in, lights_out,
    load_sem, brick_send, brick_recv, strip_send, strip_recv, mate_sem, label_send, label_recv,
    halo_send, halo_recv, edge_send, edge_recv, light_send, light_recv, part_send, part_recv,
):
    slices, rows = density.shape[:2]
    half = slices // 2
    groups, pairs = depth_count // GROUP, light_count // PAIR
    all_rows, all_slices = PAIR * rows, GROUP * slices
    block_rows = rows // depth_count
    blocks = PAIR * depth_count
    row_tiles = rows // SUB
    d = lax.axis_index("depth")
    light = lax.axis_index("light")
    k, j = d // GROUP, d % GROUP
    p, l = light // PAIR, light % PAIR
    q = PAIR * j + l
    mine = l * depth_count + d
    has_below, has_above = k > 0, k < groups - 1
    has_before, has_after = p > 0, p < pairs - 1
    lane = lax.broadcasted_iota(jnp.int32, (SUB, LANE), 1)
    sub = lax.broadcasted_iota(jnp.int32, (SUB, LANE), 0)
    zero = jnp.zeros((SUB, LANE), jnp.float32)

    loads = [
        pltpu.make_async_copy(source, target, load_sem.at[n])
        for n, (source, target) in enumerate(
            ((order_far, order), (density_far, density), (labels_far, labels), (extinction_far, extinction), (albedo_far, albedo))
        )
    ]
    for one in loads:
        one.start()

    barrier = pltpu.get_barrier_semaphore()

    def greet(number, carry):
        to_light = PAIR * p + number // depth_count
        to_depth = number % depth_count

        @pl.when(number != mine)
        def _():
            pl.semaphore_signal(barrier, inc=1, device_id=(to_depth, to_light), device_id_type=MESH)

        return carry

    lax.fori_loop(0, blocks, greet, 0)
    greeted = blocks - 1
    if pairs > 1:
        for exists, step in ((has_before, -PAIR), (has_after, PAIR)):

            @pl.when(exists)
            def _():
                pl.semaphore_signal(barrier, inc=1, device_id=(d, light + step), device_id_type=MESH)

            greeted = greeted + jnp.where(exists, 1, 0)

    def remote(source, target, send, recv, depth, to_light):
        return pltpu.make_async_remote_copy(
            src_ref=source, dst_ref=target, send_sem=send, recv_sem=recv,
            device_id=(depth, to_light), device_id_type=MESH,
        )

    loads[0].wait()
    loads[1].wait()

    def pack(i, packed):
        z, g = i // row_tiles, i % row_tiles
        at = lax.rem(order[z], slices)
        base = pl.multiple_of(g * SUB, SUB)
        tiles = [density[at, pl.ds(base, SUB), t * LANE : (t + 1) * LANE] for t in range(PARTS)]
        result = []
        for t in range(PARTS):
            bricks[t, z, pl.ds(base, SUB), :] = tiles[t]
            left = tiles[t - 1] if t > 0 else zero
            right = tiles[t + 1] if t < PARTS - 1 else zero
            rims = pltpu.roll(jnp.where(lane < LANE // 2, right, left), lax.rem(4 * i + 2, LANE), 1)
            result.append(jnp.where(lane // 4 == i, rims, packed[t]))
        return tuple(result)

    packed = lax.fori_loop(0, slices * row_tiles, pack, (zero,) * PARTS)
    for t in range(PARTS):
        strips[t] = packed[t]

    @pl.when(jnp.logical_not(has_below))
    def _():
        volume[half : slices, 0] = jnp.zeros((half,) + volume.shape[2:], jnp.float32)
        halo_strips[0] = jnp.zeros(halo_strips.shape[1:], jnp.float32)

    @pl.when(jnp.logical_not(has_above))
    def _():
        volume[slices + all_slices : slices + all_slices + half, 0] = jnp.zeros((half,) + volume.shape[2:], jnp.float32)
        halo_strips[GROUP + 1] = jnp.zeros(halo_strips.shape[1:], jnp.float32)

    pl.semaphore_wait(barrier, greeted)

    def brick_spot(from_j, from_l, part):
        return volume.at[
            pl.ds(slices + slices * from_j + half * part, half), 0, pl.ds(EDGE + rows * from_l, rows)
        ]

    def brick_copy(m, e, part):
        to_q = PAIR * flip(j, m) + (l if e == 0 else 1 - l)
        source = bricks.at[to_q, pl.ds(half * part, half)]
        slot = PAIR * m + e
        if slot == 0:
            return pltpu.make_async_copy(source, brick_spot(j, l, part), brick_recv.at[part, 0])
        return remote(
            source, brick_spot(j, l, part), brick_send.at[part, slot], brick_recv.at[part, slot],
            GROUP * k + flip(j, m), PAIR * p + to_q % PAIR,
        )

    def strip_copy(m, e):
        to_q = PAIR * flip(j, m) + (l if e == 0 else 1 - l)
        target = halo_strips.at[1 + j, l]
        slot = PAIR * m + e
        if slot == 0:
            return pltpu.make_async_copy(strips.at[to_q], target, strip_recv.at[0])
        return remote(
            strips.at[to_q], target, strip_send.at[slot], strip_recv.at[slot],
            GROUP * k + flip(j, m), PAIR * p + to_q % PAIR,
        )

    every = [(m, e) for m in ORDER + (0,) for e in range(PAIR)]
    early = jnp.where(j == GROUP - 1, 1, 0)
    for m, e in every:
        brick_copy(m, e, early).start()
    for m, e in every:
        strip_copy(m, e).start()
    for m, e in every:
        brick_copy(m, e, 1 - early).start()

    loads[2].wait()

    def pack_labels(i, carry):
        z, g = i // row_tiles, i % row_tiles
        at = lax.rem(order[z], slices)
        base = pl.multiple_of(g * SUB, SUB)
        for t in range(PARTS):
            labels_out[t % PAIR, t // PAIR, z, pl.ds(base, SUB), :] = labels[at, pl.ds(base, SUB), t * LANE : (t + 1) * LANE]
        return carry

    lax.fori_loop(0, slices * row_tiles, pack_labels, 0)
    own_rows = column_labels.at[:, :, pl.ds(rows * l, rows)]
    keep_labels = pltpu.make_async_copy(labels_out.at[l], own_rows, mate_sem.at[0])
    mate_labels = remote(labels_out.at[1 - l], own_rows, mate_sem.at[1], mate_sem.at[2], d, PAIR * p + 1 - l)
    keep_labels.start()
    mate_labels.start()

    def wait_brick(m, e, part):
        to_q = PAIR * flip(j, m) + (l if e == 0 else 1 - l)
        if isinstance(m, int) and PAIR * m + e == 0:
            brick_copy(0, 0, part).wait()
        else:
            spot = brick_spot(flip(j, m), to_q % PAIR, part)
            remote(spot, spot, brick_send.at[part, PAIR * m + e], brick_recv.at[part, PAIR * m + e], d, light).wait_recv()

    def wait_strip(m, e):
        if PAIR * m + e == 0:
            strip_copy(0, 0).wait()
        else:
            strip_copy(m, e).wait_recv()

    halos = []
    for n, (step, own, part, target) in enumerate(
        ((-1, 0, 0, slices + all_slices), (1, GROUP - 1, 1, half))
    ):
        start = slices + slices * own + half * part
        depth = d + GROUP * step
        strip_target = GROUP + 1 if step < 0 else 0
        halos.append((
            remote(
                volume.at[pl.ds(start, half), 0, pl.ds(EDGE, all_rows)],
                volume.at[pl.ds(target, half), 0, pl.ds(EDGE, all_rows)],
                halo_send.at[n], halo_recv.at[n], depth, light,
            ),
            remote(halo_strips.at[1 + own], halo_strips.at[strip_target], halo_send.at[2 + n], halo_recv.at[2 + n], depth, light),
        ))
    for part in range(2):
        first_j = 0 if part == 0 else GROUP - 1
        for m in range(GROUP):

            @pl.when(flip(j, m) == first_j)
            def _():
                for e in range(PAIR):
                    wait_brick(m, e, part)

    for m, e in every:
        wait_strip(m, e)
    for (bulk, thin), exists in zip(halos, (has_below, has_above)):

        @pl.when(exists)
        def _():
            bulk.start()
            thin.start()

    keep_labels.wait()
    mate_labels.wait_recv()
    chunk_rows = all_rows // CHUNKS

    def label_copy(c, m):
        at = pl.ds(pl.multiple_of(c * chunk_rows, SUB), chunk_rows)
        return remote(
            column_labels.at[flip(j, m), :, at], materials.at[pl.ds(slices * j, slices), at],
            label_send.at[c, m - 1], label_recv.at[c, m - 1], GROUP * k + flip(j, m), light,
        )

    def send_labels(c, carry):
        for m in ORDER:
            label_copy(c, m).start()
        return carry

    lax.fori_loop(0, CHUNKS, send_labels, 0)
    own_labels = pltpu.make_async_copy(column_labels.at[j], materials.at[pl.ds(slices * j, slices)], mate_sem.at[0])
    own_labels.start()

    for part in range(2):
        first_j = 0 if part == 0 else GROUP - 1
        for m in range(GROUP):

            @pl.when(flip(j, m) != first_j)
            def _():
                for e in range(PAIR):
                    wait_brick(m, e, part)

    for n, exists in ((1, has_below), (0, has_above)):

        @pl.when(exists)
        def _():
            halos[n][0].wait_recv()
            halos[n][1].wait_recv()

    def unpack(b, carry):
        for l_from in range(PAIR):
            strip = halo_strips[b, l_from]
            for z in range(slices):
                for g in range(row_tiles):
                    i = z * row_tiles + g
                    at = EDGE + rows * l_from + SUB * g
                    volume[slices * b + z, 1, at : at + SUB] = pltpu.roll(strip, (2 * LANE - 4 * i - 2) % LANE, 1)
        return carry

    lax.fori_loop(0, GROUP + 2, unpack, 0)

    edges = []
    if pairs > 1:
        for n, (step, source, target, exists) in enumerate(
            ((-PAIR, EDGE, EDGE + all_rows, has_before), (PAIR, EDGE + all_rows - SUB, EDGE - SUB, has_after))
        ):
            edges.append((
                remote(
                    volume.at[:, :, pl.ds(source, SUB)], volume.at[:, :, pl.ds(target, SUB)],
                    edge_send.at[n], edge_recv.at[n], d, light + step,
                ),
                exists,
            ))
        for one, exists in edges:
            pl.when(exists)(one.start)

    def zero_edge(at):
        for t in range(2):
            for z in range(half, all_slices + slices + half):
                volume[z, t, at : at + SUB] = zero

    if pairs > 1:
        for n, exists in ((0, has_after), (1, has_before)):
            pl.when(exists)(edges[n][0].wait_recv)
    pl.when(jnp.logical_not(has_before))(lambda: zero_edge(EDGE - SUB))
    pl.when(jnp.logical_not(has_after))(lambda: zero_edge(EDGE + all_rows))

    below = jnp.where(has_below, 1.0, 0.0)
    above = jnp.where(has_above, 1.0, 0.0)
    inside = jnp.where(lane < LANE // 2, jnp.where(q < PARTS - 1, 1.0, 0.0), jnp.where(q > 0, 1.0, 0.0))
    lane_first, lane_last = lane == 0, lane == LANE - 1

    def smooth_tile(g, carry):
        base = pl.multiple_of(EDGE + g * SUB, SUB)
        target = pl.multiple_of(SUB + g * SUB, SUB)
        at = pl.ds(base, SUB)

        def both(z):
            return [volume[z, t, at] for t in range(2)]

        first = slices - 1
        before, center = both(first - 1), both(first)
        for s in range(all_slices + 2):
            z = first + s
            after = both(z + 1)
            for t in range(2):
                own, other = center[t], center[1 - t]
                low = pltpu.roll(jnp.where(lane_last, other, own), 1, 1)
                high = pltpu.roll(jnp.where(lane_first, other, own), LANE - 1, 1)
                up = volume[z, t, pl.ds(base - 1, SUB)]
                down = volume[z, t, pl.ds(base + 1, SUB)]
                value = 0.4 * own + 0.1 * ((before[t] + after[t]) + (up + down) + (low + high))
                if s == 0:
                    value = value * below
                if s == all_slices + 1:
                    value = value * above
                if t == 1:
                    value = value * inside
                smooth[s, t, pl.ds(target, SUB)] = value
            before, center = center, after
        return carry

    ends = 1 if pairs > 1 else 0
    lax.fori_loop(-ends, all_rows // SUB + ends, smooth_tile, 0)

    def clear_rim(at):
        for s in range(1, all_slices + 1):
            smooth[s, 0, at : at + SUB] = zero

    pl.when(jnp.logical_not(has_before))(lambda: clear_rim(0))
    pl.when(jnp.logical_not(has_after))(lambda: clear_rim(SUB + all_rows))

    def slope_tile(g, carry):
        base = pl.multiple_of(SUB + g * SUB, SUB)
        target = pl.ds(pl.multiple_of(g * SUB, SUB), SUB)
        at = pl.ds(base, SUB)
        before, center = smooth[0, 0, at], smooth[1, 0, at]
        for z in range(all_slices):
            after = smooth[z + 2, 0, at]
            beside = smooth[z + 1, 1, at]
            low = pltpu.roll(jnp.where(lane_last, beside, center), 1, 1)
            high = pltpu.roll(jnp.where(lane_first, beside, center), LANE - 1, 1)
            up = smooth[z + 1, 0, pl.ds(base - 1, SUB)]
            down = smooth[z + 1, 0, pl.ds(base + 1, SUB)]
            grad_z, grad_x, grad_y = after - before, down - up, high - low
            facing = grad_x * lax.rsqrt(grad_z * grad_z + grad_x * grad_x + grad_y * grad_y + 0.2)
            heat[z, target] = jnp.exp(center)
            turned[z, target] = 0.5 + 0.5 * facing
            before, center = center, after
        return carry

    lax.fori_loop(0, all_rows // SUB, slope_tile, 0)

    loads[3].wait()
    loads[4].wait()
    tables = [zero for _ in range(4)]
    for n in range(extinction.shape[0]):
        tables[0] = jnp.where(lane == n, extinction[n], tables[0])
        for c in range(3):
            tables[c + 1] = jnp.where(lane == n, albedo[c, n], tables[c + 1])

    def part_spot():
        return parts_in.at[k, q]

    def send_part(o):
        to_depth, to_light = o % depth_count, PAIR * p + o // depth_count

        @pl.when(o != mine)
        def _():
            remote(parts_out.at[o], part_spot(), part_send, part_recv, to_depth, to_light).start()

        @pl.when(o == mine)
        def _():
            pltpu.make_async_copy(parts_out.at[o], part_spot(), part_recv).start()

    per_tile = SUB // block_rows

    def shade_tile(g, lights):
        at = pl.ds(pl.multiple_of(g * SUB, SUB), SUB)
        lights = list(lights)
        remaining = jnp.ones((SUB, LANE), jnp.float32)
        colours = [zero] * 3
        for z in range(all_slices):
            index = materials[z, at]
            passed = jnp.exp(-(lookup(tables[0], index) * heat[z, at]))
            ahead = jnp.where(sub >= 1, pltpu.roll(passed, 1, 0), lights[z])
            for step in (1, 2, 4):
                ahead = ahead * jnp.where(sub >= step, pltpu.roll(ahead, step, 0), 1.0)
            lights[z] = jnp.broadcast_to((ahead * passed)[SUB - 1 :], (SUB, LANE))
            weight = (1.0 - passed) * remaining * (0.2 + ahead * turned[z, at])
            for c in range(3):
                colours[c] = colours[c] + lookup(tables[c + 1], index) * weight
            remaining = remaining * passed
        for b in range(per_tile):
            for c, value in enumerate(colours + [remaining]):
                parts_out[g * per_tile + b, c * block_rows : (c + 1) * block_rows] = value[b * block_rows : (b + 1) * block_rows]
        for b in range(per_tile):
            send_part(g * per_tile + b)
        return tuple(lights)

    lights = (jnp.ones((SUB, LANE), jnp.float32),) * all_slices
    if pairs > 1:
        light_copy = remote(lights_out, lights_in, light_send, light_recv, d, light + PAIR)

        @pl.when(has_before)
        def _():
            light_copy.wait_recv()

        @pl.when(jnp.logical_not(has_before))
        def _():
            for z in range(all_slices):
                lights_in[z] = jnp.ones((SUB, LANE), jnp.float32)

        lights = tuple(lights_in[z] for z in range(all_slices))

    own_labels.wait()
    tiles_per_chunk = chunk_rows // SUB

    def shade_chunk(c, lights):
        for m in ORDER:
            label_copy(c, m).wait_recv()
        for n in range(tiles_per_chunk):
            lights = shade_tile(c * tiles_per_chunk + n, lights)
        return lights

    lights = lax.fori_loop(0, CHUNKS, shade_chunk, lights)
    if pairs > 1:
        for z in range(all_slices):
            lights_out[z] = lights[z]
        pl.when(has_after)(light_copy.start)

    pltpu.make_async_copy(parts_in, parts_in, part_recv).wait()

    for n in range(PARTS):
        through = parts_in[groups - 1, n, 3 * block_rows :]
        back = [parts_in[groups - 1, n, c * block_rows : (c + 1) * block_rows] for c in range(3)]
        for front in reversed(range(groups - 1)):
            clear = parts_in[front, n, 3 * block_rows :]
            through = through * clear
            back = [parts_in[front, n, c * block_rows : (c + 1) * block_rows] + clear * back[c] for c in range(3)]
        for c, value in enumerate(back + [1.0 - through]):
            blended[n, c * block_rows : (c + 1) * block_rows] = value
        for r in range(block_rows):
            at = r * PARTS * LANE + n * LANE
            out[:, at : at + LANE] = blended[n, pl.ds(r, 4, stride=block_rows), :]

    for part in range(2):
        for m, e in every:
            if (m, e) != (0, 0):
                brick_copy(m, e, part).wait_send()
    for m, e in every:
        if (m, e) != (0, 0):
            strip_copy(m, e).wait_send()
    mate_labels.wait_send()
    for (bulk, thin), exists in zip(halos, (has_below, has_above)):

        @pl.when(exists)
        def _():
            bulk.wait_send()
            thin.wait_send()

    def sent_labels(c, carry):
        for m in ORDER:
            label_copy(c, m).wait_send()
        return carry

    lax.fori_loop(0, CHUNKS, sent_labels, 0)
    sent = parts_out.at[pl.ds(0, blocks - 1)]
    pltpu.make_async_copy(sent, sent, part_send).wait()
    for one, exists in edges:
        pl.when(exists)(one.wait_send)
    if pairs > 1:
        pl.when(has_after)(light_copy.wait_send)


def shards(density, labels, slice_order, extinction, albedo):
    depth_count = lax.axis_size("depth")
    light_count = lax.axis_size("light")
    slices, rows, columns = density.shape
    groups = depth_count // GROUP
    block_rows = rows // depth_count
    all_rows, all_slices = PAIR * rows, GROUP * slices
    f32, i32 = jnp.float32, jnp.int32
    vmem, smem, dma = pltpu.VMEM, pltpu.SMEM, pltpu.SemaphoreType.DMA
    scratch = [
        vmem(density.shape, f32),
        vmem(labels.shape, i32),
        smem(slice_order.shape, i32),
        smem(extinction.shape, f32),
        smem(albedo.shape, f32),
        vmem((PARTS, slices, rows, LANE), f32),
        vmem((PARTS, SUB, LANE), f32),
        vmem((PAIR, GROUP, slices, rows, LANE), i32),
        vmem((GROUP, slices, all_rows, LANE), i32),
        vmem((all_slices + 2 * slices, 2, all_rows + 2 * EDGE, LANE), f32),
        vmem((GROUP + 2, PAIR, SUB, LANE), f32),
        vmem((all_slices, all_rows, LANE), i32),
        vmem((all_slices + 2, 2, all_rows + 2 * SUB, LANE), f32),
        vmem((all_slices, all_rows, LANE), f32),
        vmem((all_slices, all_rows, LANE), f32),
        vmem((PAIR * depth_count, 4 * block_rows, LANE), f32),
        vmem((groups, PARTS, 4 * block_rows, LANE), f32),
        vmem((PARTS, 4 * block_rows, LANE), f32),
        vmem((all_slices, SUB, LANE), f32),
        vmem((all_slices, SUB, LANE), f32),
        dma((5,)),
        dma((2, PARTS)),
        dma((2, PARTS)),
        dma((PARTS,)),
        dma((PARTS,)),
        dma((3,)),
        dma((CHUNKS, GROUP - 1)),
        dma((CHUNKS, GROUP - 1)),
        dma((4,)),
        dma((4,)),
        dma((2,)),
        dma((2,)),
        dma(()),
        dma(()),
        dma(()),
        dma(()),
    ]
    image = pl.pallas_call(
        functools.partial(render_kernel, depth_count, light_count),
        in_specs=[FAR] * 5,
        out_specs=pl.BlockSpec(memory_space=pltpu.VMEM),
        out_shape=jax.ShapeDtypeStruct((4, block_rows * columns), f32),
        scratch_shapes=scratch,
        compiler_params=pltpu.CompilerParams(
            collective_id=0, has_side_effects=True, vmem_limit_bytes=40 * 1024 * 1024
        ),
    )(*(pltpu.with_memory_space_constraint(one, pltpu.HBM) for one in (density, labels, slice_order, extinction, albedo)))
    return image


def solution(mesh):
    return jax.shard_map(
        shards,
        mesh=mesh,
        in_specs=(P("depth", "light", None), P("depth", "light", None), P("depth"), P(), P()),
        out_specs=P(None, ("light", "depth")),
        check_vma=False,
    )
```

```python
import functools

import jax
import jax.numpy as jnp
from jax import lax
from jax.experimental import pallas as pl
from jax.experimental.pallas import tpu as pltpu
from jax.sharding import PartitionSpec as P

SUB, LANE = 8, 128
GROUP, PAIR = 4, 2
PARTS = GROUP * PAIR
DIRECT = 1
EDGE = 2 * SUB
MESH = pl.DeviceIdType.MESH
FAR = pl.BlockSpec(memory_space=pltpu.HBM)
ORDER = (3, 1, 2)


def flip(value, mask):
    for bit in (1, 2):
        if mask & bit:
            value = value + bit * (1 - 2 * ((value // bit) % 2))
    return value


def far_reaches(groups):
    reaches, known = [], 1
    while known < groups - 1:
        reaches.append(known)
        known *= 2
    return reaches


def lookup(table, index):
    return jnp.take_along_axis(table, index, axis=1, mode="promise_in_bounds")


def render_kernel(
    depth_count, light_count,
    density_far, labels_far, order_far, extinction_far, albedo_far,
    out,
    density, labels, order, extinction, albedo,
    bricks, strips, labels_out, column_labels, volume, halo_strips, materials,
    smooth, heat, turned, parts_out, parts_mid, parts_merged, parts_last, direct_last, blended, lights_in, lights_out,
    load_sem, brick_send, brick_recv, strip_send, strip_recv, mate_sem, label_send, label_recv,
    halo_send, halo_recv, edge_send, edge_recv, light_send, light_recv, ready_sem,
    mid_send, mid_recv, last_send, last_recv, direct_send, direct_recv,
):
    slices, rows = density.shape[:2]
    half = slices // 2
    groups, pairs = depth_count // GROUP, light_count // PAIR
    all_rows, all_slices = PAIR * rows, GROUP * slices
    block_rows = rows // depth_count
    row_tiles = rows // SUB
    unit_rows = GROUP * block_rows
    units = PAIR * groups
    chunk_rows = max(2 * SUB, unit_rows)
    chunks = all_rows // chunk_rows
    chunk_units = chunk_rows // unit_rows
    direct_from = units - DIRECT * chunk_units
    d = lax.axis_index("depth")
    light = lax.axis_index("light")
    k, j = d // GROUP, d % GROUP
    p, l = light // PAIR, light % PAIR
    q = PAIR * j + l
    has_below, has_above = k > 0, k < groups - 1
    has_before, has_after = p > 0, p < pairs - 1
    lane = lax.broadcasted_iota(jnp.int32, (SUB, LANE), 1)
    sub = lax.broadcasted_iota(jnp.int32, (SUB, LANE), 0)
    zero = jnp.zeros((SUB, LANE), jnp.float32)

    loads = [
        pltpu.make_async_copy(source, target, load_sem.at[n])
        for n, (source, target) in enumerate(
            ((order_far, order), (density_far, density), (labels_far, labels), (extinction_far, extinction), (albedo_far, albedo))
        )
    ]
    for one in loads:
        one.start()

    barrier = pltpu.get_barrier_semaphore()

    for m in range(GROUP):
        for e in range(PAIR):
            if (m, e) != (0, 0):
                mate = (GROUP * k + flip(j, m), PAIR * p + (l if e == 0 else 1 - l))
                pl.semaphore_signal(barrier, inc=1, device_id=mate, device_id_type=MESH)
    greeted = PARTS - 1
    for exists, step in ((has_below, -GROUP), (has_above, GROUP)):

        @pl.when(exists)
        def _():
            pl.semaphore_signal(barrier, inc=1, device_id=(d + step, light), device_id_type=MESH)

        greeted = greeted + jnp.where(exists, 1, 0)
    if pairs > 1:
        for exists, step in ((has_before, -PAIR), (has_after, PAIR)):

            @pl.when(exists)
            def _():
                pl.semaphore_signal(barrier, inc=1, device_id=(d, light + step), device_id_type=MESH)

            greeted = greeted + jnp.where(exists, 1, 0)

    def remote(source, target, send, recv, depth, to_light):
        return pltpu.make_async_remote_copy(
            src_ref=source, dst_ref=target, send_sem=send, recv_sem=recv,
            device_id=(depth, to_light), device_id_type=MESH,
        )

    loads[0].wait()
    loads[1].wait()

    def pack(i, packed):
        z, g = i // row_tiles, i % row_tiles
        at = lax.rem(order[z], slices)
        base = pl.multiple_of(g * SUB, SUB)
        tiles = [density[at, pl.ds(base, SUB), t * LANE : (t + 1) * LANE] for t in range(PARTS)]
        result = []
        for t in range(PARTS):
            bricks[t, z, pl.ds(base, SUB), :] = tiles[t]
            left = tiles[t - 1] if t > 0 else zero
            right = tiles[t + 1] if t < PARTS - 1 else zero
            rims = pltpu.roll(jnp.where(lane < LANE // 2, right, left), lax.rem(4 * i + 2, LANE), 1)
            result.append(jnp.where(lane // 4 == i, rims, packed[t]))
        return tuple(result)

    packed = lax.fori_loop(0, slices * row_tiles, pack, (zero,) * PARTS)
    for t in range(PARTS):
        strips[t] = packed[t]

    @pl.when(jnp.logical_not(has_below))
    def _():
        volume[half : slices, 0] = jnp.zeros((half,) + volume.shape[2:], jnp.float32)
        halo_strips[0] = jnp.zeros(halo_strips.shape[1:], jnp.float32)

    @pl.when(jnp.logical_not(has_above))
    def _():
        volume[slices + all_slices : slices + all_slices + half, 0] = jnp.zeros((half,) + volume.shape[2:], jnp.float32)
        halo_strips[GROUP + 1] = jnp.zeros(halo_strips.shape[1:], jnp.float32)

    pl.semaphore_wait(barrier, greeted)

    def brick_spot(from_j, from_l, part):
        return volume.at[
            pl.ds(slices + slices * from_j + half * part, half), 0, pl.ds(EDGE + rows * from_l, rows)
        ]

    def brick_copy(m, e, part):
        to_q = PAIR * flip(j, m) + (l if e == 0 else 1 - l)
        source = bricks.at[to_q, pl.ds(half * part, half)]
        slot = PAIR * m + e
        if slot == 0:
            return pltpu.make_async_copy(source, brick_spot(j, l, part), brick_recv.at[part, 0])
        return remote(
            source, brick_spot(j, l, part), brick_send.at[part, slot], brick_recv.at[part, slot],
            GROUP * k + flip(j, m), PAIR * p + to_q % PAIR,
        )

    def strip_copy(m, e):
        to_q = PAIR * flip(j, m) + (l if e == 0 else 1 - l)
        target = halo_strips.at[1 + j, l]
        slot = PAIR * m + e
        if slot == 0:
            return pltpu.make_async_copy(strips.at[to_q], target, strip_recv.at[0])
        return remote(
            strips.at[to_q], target, strip_send.at[slot], strip_recv.at[slot],
            GROUP * k + flip(j, m), PAIR * p + to_q % PAIR,
        )

    every = [(m, e) for m in ORDER + (0,) for e in range(PAIR)]
    early = jnp.where(j == GROUP - 1, 1, 0)
    for m, e in every:
        brick_copy(m, e, early).start()
    for m, e in every:
        strip_copy(m, e).start()
    for m, e in every:
        brick_copy(m, e, 1 - early).start()

    def signal_far(number, reach):
        for exists, step in ((k >= reach, -reach), (k + reach < groups, reach)):

            @pl.when(exists)
            def _():
                pl.semaphore_signal(
                    ready_sem.at[number], inc=1, device_id=(d + GROUP * step, light), device_id_type=MESH
                )

    def wait_far(number, reach):
        count = jnp.where(k >= reach, 1, 0) + jnp.where(k + reach < groups, 1, 0)
        pl.semaphore_wait(ready_sem.at[number], count)

    reaches = far_reaches(groups)
    if reaches:
        signal_far(0, reaches[0])

    loads[2].wait()

    def pack_labels(i, carry):
        z, g = i // row_tiles, i % row_tiles
        at = lax.rem(order[z], slices)
        base = pl.multiple_of(g * SUB, SUB)
        for t in range(PARTS):
            labels_out[t % PAIR, t // PAIR, z, pl.ds(base, SUB), :] = labels[at, pl.ds(base, SUB), t * LANE : (t + 1) * LANE]
        return carry

    lax.fori_loop(0, slices * row_tiles, pack_labels, 0)
    own_rows = column_labels.at[:, :, pl.ds(rows * l, rows)]
    keep_labels = pltpu.make_async_copy(labels_out.at[l], own_rows, mate_sem.at[0])
    mate_labels = remote(labels_out.at[1 - l], own_rows, mate_sem.at[1], mate_sem.at[2], d, PAIR * p + 1 - l)
    keep_labels.start()
    mate_labels.start()

    def wait_brick(m, e, part):
        to_q = PAIR * flip(j, m) + (l if e == 0 else 1 - l)
        if isinstance(m, int) and PAIR * m + e == 0:
            brick_copy(0, 0, part).wait()
        else:
            spot = brick_spot(flip(j, m), to_q % PAIR, part)
            remote(spot, spot, brick_send.at[part, PAIR * m + e], brick_recv.at[part, PAIR * m + e], d, light).wait_recv()

    def wait_strip(m, e):
        if PAIR * m + e == 0:
            strip_copy(0, 0).wait()
        else:
            strip_copy(m, e).wait_recv()

    halos = []
    for n, (step, own, part, target) in enumerate(
        ((-1, 0, 0, slices + all_slices), (1, GROUP - 1, 1, half))
    ):
        start = slices + slices * own + half * part
        depth = d + GROUP * step
        strip_target = GROUP + 1 if step < 0 else 0
        halos.append((
            remote(
                volume.at[pl.ds(start, half), 0, pl.ds(EDGE, all_rows)],
                volume.at[pl.ds(target, half), 0, pl.ds(EDGE, all_rows)],
                halo_send.at[n], halo_recv.at[n], depth, light,
            ),
            remote(halo_strips.at[1 + own], halo_strips.at[strip_target], halo_send.at[2 + n], halo_recv.at[2 + n], depth, light),
        ))
    for part in range(2):
        first_j = 0 if part == 0 else GROUP - 1
        for m in range(GROUP):

            @pl.when(flip(j, m) == first_j)
            def _():
                for e in range(PAIR):
                    wait_brick(m, e, part)

    for m, e in every:
        wait_strip(m, e)
    for (bulk, thin), exists in zip(halos, (has_below, has_above)):

        @pl.when(exists)
        def _():
            bulk.start()
            thin.start()

    keep_labels.wait()
    mate_labels.wait_recv()
    def label_copy(c, m):
        at = pl.ds(pl.multiple_of(c * chunk_rows, SUB), chunk_rows)
        return remote(
            column_labels.at[flip(j, m), :, at], materials.at[pl.ds(slices * j, slices), at],
            label_send.at[c, m - 1], label_recv.at[c, m - 1], GROUP * k + flip(j, m), light,
        )

    def send_labels(c, carry):
        for m in ORDER:
            label_copy(c, m).start()
        return carry

    lax.fori_loop(0, chunks, send_labels, 0)
    own_labels = pltpu.make_async_copy(column_labels.at[j], materials.at[pl.ds(slices * j, slices)], mate_sem.at[0])
    own_labels.start()

    for part in range(2):
        first_j = 0 if part == 0 else GROUP - 1
        for m in range(GROUP):

            @pl.when(flip(j, m) != first_j)
            def _():
                for e in range(PAIR):
                    wait_brick(m, e, part)

    for n, exists in ((1, has_below), (0, has_above)):

        @pl.when(exists)
        def _():
            halos[n][0].wait_recv()
            halos[n][1].wait_recv()

    for number, reach in enumerate(reaches):
        wait_far(number, reach)
        if number + 1 < len(reaches):
            signal_far(number + 1, reaches[number + 1])

    def unpack(b, carry):
        for l_from in range(PAIR):
            strip = halo_strips[b, l_from]
            for z in range(slices):
                for g in range(row_tiles):
                    i = z * row_tiles + g
                    at = EDGE + rows * l_from + SUB * g
                    volume[slices * b + z, 1, at : at + SUB] = pltpu.roll(strip, (2 * LANE - 4 * i - 2) % LANE, 1)
        return carry

    lax.fori_loop(0, GROUP + 2, unpack, 0)

    edges = []
    if pairs > 1:
        for n, (step, source, target, exists) in enumerate(
            ((-PAIR, EDGE, EDGE + all_rows, has_before), (PAIR, EDGE + all_rows - SUB, EDGE - SUB, has_after))
        ):
            edges.append((
                remote(
                    volume.at[:, :, pl.ds(source, SUB)], volume.at[:, :, pl.ds(target, SUB)],
                    edge_send.at[n], edge_recv.at[n], d, light + step,
                ),
                exists,
            ))
        for one, exists in edges:
            pl.when(exists)(one.start)

    def zero_edge(at):
        for t in range(2):
            for z in range(half, all_slices + slices + half):
                volume[z, t, at : at + SUB] = zero

    if pairs > 1:
        for n, exists in ((0, has_after), (1, has_before)):
            pl.when(exists)(edges[n][0].wait_recv)
    pl.when(jnp.logical_not(has_before))(lambda: zero_edge(EDGE - SUB))
    pl.when(jnp.logical_not(has_after))(lambda: zero_edge(EDGE + all_rows))

    below = jnp.where(has_below, 1.0, 0.0)
    above = jnp.where(has_above, 1.0, 0.0)
    inside = jnp.where(lane < LANE // 2, jnp.where(q < PARTS - 1, 1.0, 0.0), jnp.where(q > 0, 1.0, 0.0))
    lane_first, lane_last = lane == 0, lane == LANE - 1

    def smooth_tile(g, carry):
        base = pl.multiple_of(EDGE + g * SUB, SUB)
        target = pl.multiple_of(SUB + g * SUB, SUB)
        at = pl.ds(base, SUB)

        def both(z):
            return [volume[z, t, at] for t in range(2)]

        first = slices - 1
        before, center = both(first - 1), both(first)
        for s in range(all_slices + 2):
            z = first + s
            after = both(z + 1)
            for t in range(2):
                own, other = center[t], center[1 - t]
                low = pltpu.roll(jnp.where(lane_last, other, own), 1, 1)
                high = pltpu.roll(jnp.where(lane_first, other, own), LANE - 1, 1)
                up = volume[z, t, pl.ds(base - 1, SUB)]
                down = volume[z, t, pl.ds(base + 1, SUB)]
                value = 0.4 * own + 0.1 * ((before[t] + after[t]) + (up + down) + (low + high))
                if s == 0:
                    value = value * below
                if s == all_slices + 1:
                    value = value * above
                if t == 1:
                    value = value * inside
                smooth[s, t, pl.ds(target, SUB)] = value
            before, center = center, after
        return carry

    ends = 1 if pairs > 1 else 0
    lax.fori_loop(-ends, all_rows // SUB + ends, smooth_tile, 0)

    def clear_rim(at):
        for s in range(1, all_slices + 1):
            smooth[s, 0, at : at + SUB] = zero

    pl.when(jnp.logical_not(has_before))(lambda: clear_rim(0))
    pl.when(jnp.logical_not(has_after))(lambda: clear_rim(SUB + all_rows))

    def slope_tile(g, carry):
        base = pl.multiple_of(SUB + g * SUB, SUB)
        target = pl.ds(pl.multiple_of(g * SUB, SUB), SUB)
        at = pl.ds(base, SUB)
        before, center = smooth[0, 0, at], smooth[1, 0, at]
        for z in range(all_slices):
            after = smooth[z + 2, 0, at]
            beside = smooth[z + 1, 1, at]
            low = pltpu.roll(jnp.where(lane_last, beside, center), 1, 1)
            high = pltpu.roll(jnp.where(lane_first, beside, center), LANE - 1, 1)
            up = smooth[z + 1, 0, pl.ds(base - 1, SUB)]
            down = smooth[z + 1, 0, pl.ds(base + 1, SUB)]
            grad_z, grad_x, grad_y = after - before, down - up, high - low
            facing = grad_x * lax.rsqrt(grad_z * grad_z + grad_x * grad_x + grad_y * grad_y + 0.2)
            heat[z, target] = jnp.exp(center)
            turned[z, target] = 0.5 + 0.5 * facing
            before, center = center, after
        return carry

    lax.fori_loop(0, all_rows // SUB, slope_tile, 0)

    loads[3].wait()
    loads[4].wait()
    tables = [zero for _ in range(4)]
    for n in range(extinction.shape[0]):
        tables[0] = jnp.where(lane == n, extinction[n], tables[0])
        for c in range(3):
            tables[c + 1] = jnp.where(lane == n, albedo[c, n], tables[c + 1])

    def unit_copy(u):
        return remote(
            parts_out.at[pl.ds(GROUP * u, GROUP)], parts_mid.at[u // groups, k],
            mid_send.at[u], mid_recv.at[u // groups], GROUP * (u % groups) + j, light,
        )

    def send_unit(u):
        @pl.when(u % groups != k)
        def _():
            unit_copy(u).start()

        @pl.when(u % groups == k)
        def _():
            pltpu.make_async_copy(
                parts_out.at[pl.ds(GROUP * u, GROUP)], parts_mid.at[u // groups, k], mid_recv.at[u // groups]
            ).start()

    def owned_here(u, i):
        return (u % groups == k) & (u // groups == l) & (j == i)

    def owner_copy(source, target, send, recv, u, i):
        return remote(source, target, send, recv, GROUP * (u % groups) + i, PAIR * p + u // groups)

    def send_owner(source, target, send, recv, u, i):
        own = owned_here(u, i)

        @pl.when(jnp.logical_not(own))
        def _():
            owner_copy(source, target, send, recv, u, i).start()

        @pl.when(own)
        def _():
            pltpu.make_async_copy(source, target, recv).start()

    def direct_parts(u, i):
        send = direct_send.at[u - direct_from, i]
        return parts_out.at[GROUP * u + i], direct_last.at[k, q], send, direct_recv, u, i

    def merged_parts(to_l, i):
        send = last_send.at[to_l, i]
        return parts_merged.at[to_l, i], parts_last.at[q], send, last_recv, to_l * groups + k, i

    def over(fronts):
        through = fronts[-1][3]
        back = fronts[-1][:3]
        for front in reversed(fronts[:-1]):
            through = through * front[3]
            back = [front[c] + front[3] * back[c] for c in range(3)]
        return back, through

    def channels(ref, at):
        return [ref[at + (pl.ds(c * block_rows, block_rows),)] for c in range(4)]

    per_tile = SUB // block_rows

    def shade_tile(g, lights):
        at = pl.ds(pl.multiple_of(g * SUB, SUB), SUB)
        lights = list(lights)
        remaining = jnp.ones((SUB, LANE), jnp.float32)
        colours = [zero] * 3
        for z in range(all_slices):
            index = materials[z, at]
            passed = jnp.exp(-(lookup(tables[0], index) * heat[z, at]))
            ahead = jnp.where(sub >= 1, pltpu.roll(passed, 1, 0), lights[z])
            for step in (1, 2, 4):
                ahead = ahead * jnp.where(sub >= step, pltpu.roll(ahead, step, 0), 1.0)
            lights[z] = jnp.broadcast_to((ahead * passed)[SUB - 1 :], (SUB, LANE))
            weight = (1.0 - passed) * remaining * (0.2 + ahead * turned[z, at])
            for c in range(3):
                colours[c] = colours[c] + lookup(tables[c + 1], index) * weight
            remaining = remaining * passed
        for b in range(per_tile):
            for c, value in enumerate(colours + [remaining]):
                parts_out[g * per_tile + b, c * block_rows : (c + 1) * block_rows] = value[b * block_rows : (b + 1) * block_rows]
        return tuple(lights)

    lights = (jnp.ones((SUB, LANE), jnp.float32),) * all_slices
    if pairs > 1:
        light_copy = remote(lights_out, lights_in, light_send, light_recv, d, light + PAIR)

        @pl.when(has_before)
        def _():
            light_copy.wait_recv()

        @pl.when(jnp.logical_not(has_before))
        def _():
            for z in range(all_slices):
                lights_in[z] = jnp.ones((SUB, LANE), jnp.float32)

        lights = tuple(lights_in[z] for z in range(all_slices))

    own_labels.wait()
    tiles_per_chunk = chunk_rows // SUB

    def shade_chunk(c, lights):
        for m in ORDER:
            label_copy(c, m).wait_recv()
        for n in range(tiles_per_chunk):
            lights = shade_tile(c * tiles_per_chunk + n, lights)
        return lights

    def merged_chunk(c, lights):
        lights = shade_chunk(c, lights)
        for n in range(chunk_units):
            send_unit(c * chunk_units + n)
        return lights

    def direct_chunk(c, lights):
        lights = shade_chunk(c, lights)
        for n in range(chunk_units):
            u = c * chunk_units + n
            for i in range(GROUP):
                send_owner(*direct_parts(u, i))
        return lights

    lights = lax.fori_loop(0, chunks - DIRECT, merged_chunk, lights)
    lights = lax.fori_loop(chunks - DIRECT, chunks, direct_chunk, lights)
    if pairs > 1:
        for z in range(all_slices):
            lights_out[z] = lights[z]
        pl.when(has_after)(light_copy.start)

    def bytes_of(ref, sem):
        pltpu.make_async_copy(ref, ref, sem).wait()

    def merge(to_l):
        bytes_of(parts_mid.at[to_l], mid_recv.at[to_l])
        for i in range(GROUP):
            back, through = over([channels(parts_mid, (to_l, front, i)) for front in range(groups)])
            for c, value in enumerate(back + [through]):
                parts_merged[to_l, i, c * block_rows : (c + 1) * block_rows] = value
            send_owner(*merged_parts(to_l, i))

    def merges_far(to_l):
        return to_l * groups + k < direct_from

    for to_l in range(PAIR):
        pl.when(merges_far(to_l))(functools.partial(merge, to_l))

    def finish(n, back, through):
        for c, value in enumerate(back + [1.0 - through]):
            blended[n, c * block_rows : (c + 1) * block_rows] = value
        for r in range(block_rows):
            at = r * PARTS * LANE + n * LANE
            out[:, at : at + LANE] = blended[n, pl.ds(r, 4, stride=block_rows), :]

    own_far = l * groups + k < direct_from

    @pl.when(own_far)
    def _():
        bytes_of(parts_last, last_recv)
        for n in range(PARTS):
            *back, through = channels(parts_last, (n,))
            finish(n, back, through)

    @pl.when(jnp.logical_not(own_far))
    def _():
        bytes_of(direct_last, direct_recv)
        for n in range(PARTS):
            finish(n, *over([channels(direct_last, (front, n)) for front in range(groups)]))

    for part in range(2):
        for m, e in every:
            if (m, e) != (0, 0):
                brick_copy(m, e, part).wait_send()
    for m, e in every:
        if (m, e) != (0, 0):
            strip_copy(m, e).wait_send()
    mate_labels.wait_send()
    for (bulk, thin), exists in zip(halos, (has_below, has_above)):

        @pl.when(exists)
        def _():
            bulk.wait_send()
            thin.wait_send()

    def sent_labels(c, carry):
        for m in ORDER:
            label_copy(c, m).wait_send()
        return carry

    lax.fori_loop(0, chunks, sent_labels, 0)

    def sent_unit(u, carry):
        @pl.when(u % groups != k)
        def _():
            unit_copy(u).wait_send()

        return carry

    lax.fori_loop(0, direct_from, sent_unit, 0)

    def sent_direct(u, carry):
        for i in range(GROUP):

            @pl.when(jnp.logical_not(owned_here(u, i)))
            def _():
                owner_copy(*direct_parts(u, i)).wait_send()

        return carry

    lax.fori_loop(direct_from, units, sent_direct, 0)
    for to_l in range(PAIR):
        for i in range(GROUP):

            @pl.when(merges_far(to_l) & jnp.logical_not(owned_here(to_l * groups + k, i)))
            def _():
                owner_copy(*merged_parts(to_l, i)).wait_send()

    for one, exists in edges:
        pl.when(exists)(one.wait_send)
    if pairs > 1:
        pl.when(has_after)(light_copy.wait_send)


def shards(density, labels, slice_order, extinction, albedo):
    depth_count = lax.axis_size("depth")
    light_count = lax.axis_size("light")
    slices, rows, columns = density.shape
    groups = depth_count // GROUP
    block_rows = rows // depth_count
    all_rows, all_slices = PAIR * rows, GROUP * slices
    units = PAIR * groups
    chunks = all_rows // max(2 * SUB, GROUP * block_rows)
    f32, i32 = jnp.float32, jnp.int32
    vmem, smem, dma = pltpu.VMEM, pltpu.SMEM, pltpu.SemaphoreType.DMA
    scratch = [
        vmem(density.shape, f32),
        vmem(labels.shape, i32),
        smem(slice_order.shape, i32),
        smem(extinction.shape, f32),
        smem(albedo.shape, f32),
        vmem((PARTS, slices, rows, LANE), f32),
        vmem((PARTS, SUB, LANE), f32),
        vmem((PAIR, GROUP, slices, rows, LANE), i32),
        vmem((GROUP, slices, all_rows, LANE), i32),
        vmem((all_slices + 2 * slices, 2, all_rows + 2 * EDGE, LANE), f32),
        vmem((GROUP + 2, PAIR, SUB, LANE), f32),
        vmem((all_slices, all_rows, LANE), i32),
        vmem((all_slices + 2, 2, all_rows + 2 * SUB, LANE), f32),
        vmem((all_slices, all_rows, LANE), f32),
        vmem((all_slices, all_rows, LANE), f32),
        vmem((PAIR * depth_count, 4 * block_rows, LANE), f32),
        vmem((PAIR, groups, GROUP, 4 * block_rows, LANE), f32),
        vmem((PAIR, GROUP, 4 * block_rows, LANE), f32),
        vmem((PARTS, 4 * block_rows, LANE), f32),
        vmem((groups, PARTS, 4 * block_rows, LANE), f32),
        vmem((PARTS, 4 * block_rows, LANE), f32),
        vmem((all_slices, SUB, LANE), f32),
        vmem((all_slices, SUB, LANE), f32),
        dma((5,)),
        dma((2, PARTS)),
        dma((2, PARTS)),
        dma((PARTS,)),
        dma((PARTS,)),
        dma((3,)),
        dma((chunks, GROUP - 1)),
        dma((chunks, GROUP - 1)),
        dma((4,)),
        dma((4,)),
        dma((2,)),
        dma((2,)),
        dma(()),
        dma(()),
        pltpu.SemaphoreType.REGULAR((max(1, len(far_reaches(groups))),)),
        dma((units,)),
        dma((PAIR,)),
        dma((PAIR, GROUP)),
        dma(()),
        dma((units, GROUP)),
        dma(()),
    ]
    image = pl.pallas_call(
        functools.partial(render_kernel, depth_count, light_count),
        in_specs=[FAR] * 5,
        out_specs=pl.BlockSpec(memory_space=pltpu.VMEM),
        out_shape=jax.ShapeDtypeStruct((4, block_rows * columns), f32),
        scratch_shapes=scratch,
        compiler_params=pltpu.CompilerParams(
            collective_id=0, has_side_effects=True, vmem_limit_bytes=40 * 1024 * 1024
        ),
    )(*(pltpu.with_memory_space_constraint(one, pltpu.HBM) for one in (density, labels, slice_order, extinction, albedo)))
    return image


def solution(mesh):
    return jax.shard_map(
        shards,
        mesh=mesh,
        in_specs=(P("depth", "light", None), P("depth", "light", None), P("depth"), P(), P()),
        out_specs=P(None, ("light", "depth")),
        check_vma=False,
    )
```

```python
import functools

import jax
import jax.numpy as jnp
from jax import lax
from jax.experimental import pallas as pl
from jax.experimental.pallas import tpu as pltpu
from jax.sharding import PartitionSpec as P

SUB, LANE = 8, 128
GROUP, PAIR = 4, 2
PARTS = GROUP * PAIR
DIRECT = 8
EDGE = 2 * SUB
MESH = pl.DeviceIdType.MESH
FAR = pl.BlockSpec(memory_space=pltpu.HBM)
ORDER = (3, 1, 2)


def flip(value, mask):
    for bit in (1, 2):
        if mask & bit:
            value = value + bit * (1 - 2 * ((value // bit) % 2))
    return value


def far_reaches(groups):
    reaches, known = [], 1
    while known < groups - 1:
        reaches.append(known)
        known *= 2
    return reaches


def lookup(table, index):
    return jnp.take_along_axis(table, index, axis=1, mode="promise_in_bounds")


def render_kernel(
    depth_count, light_count,
    density_far, labels_far, order_far, extinction_far, albedo_far,
    out,
    density, labels, order, extinction, albedo,
    bricks, strips, labels_out, column_labels, volume, halo_strips, materials,
    smooth, heat, turned, parts_out, parts_mid, parts_merged, parts_last, direct_last, blended, lights_in, lights_out,
    load_sem, brick_send, brick_recv, strip_send, strip_recv, mate_sem, label_send, label_recv,
    halo_send, halo_recv, edge_send, edge_recv, light_send, light_recv, ready_sem,
    mid_send, mid_recv, last_send, last_recv, direct_send, direct_recv,
):
    slices, rows = density.shape[:2]
    half = slices // 2
    groups, pairs = depth_count // GROUP, light_count // PAIR
    all_rows, all_slices = PAIR * rows, GROUP * slices
    block_rows = rows // depth_count
    row_tiles = rows // SUB
    unit_rows = GROUP * block_rows
    units = PAIR * groups
    chunk_rows = max(2 * SUB, unit_rows)
    chunks = all_rows // chunk_rows
    chunk_units = chunk_rows // unit_rows
    direct_from = units - DIRECT * chunk_units
    d = lax.axis_index("depth")
    light = lax.axis_index("light")
    k, j = d // GROUP, d % GROUP
    p, l = light // PAIR, light % PAIR
    q = PAIR * j + l
    has_below, has_above = k > 0, k < groups - 1
    has_before, has_after = p > 0, p < pairs - 1
    lane = lax.broadcasted_iota(jnp.int32, (SUB, LANE), 1)
    sub = lax.broadcasted_iota(jnp.int32, (SUB, LANE), 0)
    zero = jnp.zeros((SUB, LANE), jnp.float32)

    loads = [
        pltpu.make_async_copy(source, target, load_sem.at[n])
        for n, (source, target) in enumerate(
            ((order_far, order), (density_far, density), (labels_far, labels), (extinction_far, extinction), (albedo_far, albedo))
        )
    ]
    for one in loads:
        one.start()

    barrier = pltpu.get_barrier_semaphore()

    for m in range(GROUP):
        for e in range(PAIR):
            if (m, e) != (0, 0):
                mate = (GROUP * k + flip(j, m), PAIR * p + (l if e == 0 else 1 - l))
                pl.semaphore_signal(barrier, inc=1, device_id=mate, device_id_type=MESH)
    greeted = PARTS - 1
    for exists, step in ((has_below, -GROUP), (has_above, GROUP)):

        @pl.when(exists)
        def _():
            pl.semaphore_signal(barrier, inc=1, device_id=(d + step, light), device_id_type=MESH)

        greeted = greeted + jnp.where(exists, 1, 0)
    if pairs > 1:
        for exists, step in ((has_before, -PAIR), (has_after, PAIR)):

            @pl.when(exists)
            def _():
                pl.semaphore_signal(barrier, inc=1, device_id=(d, light + step), device_id_type=MESH)

            greeted = greeted + jnp.where(exists, 1, 0)

    def remote(source, target, send, recv, depth, to_light):
        return pltpu.make_async_remote_copy(
            src_ref=source, dst_ref=target, send_sem=send, recv_sem=recv,
            device_id=(depth, to_light), device_id_type=MESH,
        )

    loads[0].wait()
    loads[1].wait()

    def pack_bricks(part):
        for z in range(half):
            z = half * part + z
            at = lax.rem(order[z], slices)
            for g in range(row_tiles):
                for t in range(PARTS):
                    tile = density[at, g * SUB : (g + 1) * SUB, t * LANE : (t + 1) * LANE]
                    bricks[t, z, g * SUB : (g + 1) * SUB, :] = tile

    pack_bricks(jnp.where(j == GROUP - 1, 1, 0))

    def brick_spot(from_j, from_l, part):
        return volume.at[
            pl.ds(slices + slices * from_j + half * part, half), 0, pl.ds(EDGE + rows * from_l, rows)
        ]

    def brick_copy(m, e, part):
        to_q = PAIR * flip(j, m) + (l if e == 0 else 1 - l)
        source = bricks.at[to_q, pl.ds(half * part, half)]
        slot = PAIR * m + e
        if slot == 0:
            return pltpu.make_async_copy(source, brick_spot(j, l, part), brick_recv.at[part, 0])
        return remote(
            source, brick_spot(j, l, part), brick_send.at[part, slot], brick_recv.at[part, slot],
            GROUP * k + flip(j, m), PAIR * p + to_q % PAIR,
        )

    def strip_copy(m, e):
        to_q = PAIR * flip(j, m) + (l if e == 0 else 1 - l)
        target = halo_strips.at[1 + j, l]
        slot = PAIR * m + e
        if slot == 0:
            return pltpu.make_async_copy(strips.at[to_q], target, strip_recv.at[0])
        return remote(
            strips.at[to_q], target, strip_send.at[slot], strip_recv.at[slot],
            GROUP * k + flip(j, m), PAIR * p + to_q % PAIR,
        )

    every = [(m, e) for m in ORDER + (0,) for e in range(PAIR)]
    early = jnp.where(j == GROUP - 1, 1, 0)
    pl.semaphore_wait(barrier, greeted)
    for m, e in every:
        brick_copy(m, e, early).start()
    pack_bricks(1 - early)

    def pack_strips(z, packed):
        packed = list(packed)
        for g in range(row_tiles):
            i = z * row_tiles + g
            rows_at = slice(g * SUB, (g + 1) * SUB)
            for t in range(PARTS):
                left = bricks[t - 1, z, rows_at, :] if t > 0 else zero
                right = bricks[t + 1, z, rows_at, :] if t < PARTS - 1 else zero
                rims = pltpu.roll(jnp.where(lane < LANE // 2, right, left), lax.rem(4 * i + 2, LANE), 1)
                packed[t] = jnp.where(lane // 4 == i, rims, packed[t])
        return tuple(packed)

    packed = lax.fori_loop(0, slices, pack_strips, (zero,) * PARTS)
    for t in range(PARTS):
        strips[t] = packed[t]
    for m, e in every:
        strip_copy(m, e).start()
    for m, e in every:
        brick_copy(m, e, 1 - early).start()

    @pl.when(jnp.logical_not(has_below))
    def _():
        volume[half : slices, 0] = jnp.zeros((half,) + volume.shape[2:], jnp.float32)
        halo_strips[0] = jnp.zeros(halo_strips.shape[1:], jnp.float32)

    @pl.when(jnp.logical_not(has_above))
    def _():
        volume[slices + all_slices : slices + all_slices + half, 0] = jnp.zeros((half,) + volume.shape[2:], jnp.float32)
        halo_strips[GROUP + 1] = jnp.zeros(halo_strips.shape[1:], jnp.float32)


    def signal_far(number, reach):
        for exists, step in ((k >= reach, -reach), (k + reach < groups, reach)):

            @pl.when(exists)
            def _():
                pl.semaphore_signal(
                    ready_sem.at[number], inc=1, device_id=(d + GROUP * step, light), device_id_type=MESH
                )

    def wait_far(number, reach):
        count = jnp.where(k >= reach, 1, 0) + jnp.where(k + reach < groups, 1, 0)
        pl.semaphore_wait(ready_sem.at[number], count)

    reaches = far_reaches(groups)
    if reaches:
        signal_far(0, reaches[0])

    loads[2].wait()

    def pack_labels(i, carry):
        z, g = i // row_tiles, i % row_tiles
        at = lax.rem(order[z], slices)
        base = pl.multiple_of(g * SUB, SUB)
        for t in range(PARTS):
            labels_out[t % PAIR, t // PAIR, z, pl.ds(base, SUB), :] = labels[at, pl.ds(base, SUB), t * LANE : (t + 1) * LANE]
        return carry

    lax.fori_loop(0, slices * row_tiles, pack_labels, 0)
    own_rows = column_labels.at[:, :, pl.ds(rows * l, rows)]
    keep_labels = pltpu.make_async_copy(labels_out.at[l], own_rows, mate_sem.at[0])
    mate_labels = remote(labels_out.at[1 - l], own_rows, mate_sem.at[1], mate_sem.at[2], d, PAIR * p + 1 - l)
    keep_labels.start()
    mate_labels.start()

    def wait_brick(m, e, part):
        to_q = PAIR * flip(j, m) + (l if e == 0 else 1 - l)
        if isinstance(m, int) and PAIR * m + e == 0:
            brick_copy(0, 0, part).wait()
        else:
            spot = brick_spot(flip(j, m), to_q % PAIR, part)
            remote(spot, spot, brick_send.at[part, PAIR * m + e], brick_recv.at[part, PAIR * m + e], d, light).wait_recv()

    def wait_strip(m, e):
        if PAIR * m + e == 0:
            strip_copy(0, 0).wait()
        else:
            strip_copy(m, e).wait_recv()

    halos = []
    for n, (step, own, part, target) in enumerate(
        ((-1, 0, 0, slices + all_slices), (1, GROUP - 1, 1, half))
    ):
        start = slices + slices * own + half * part
        depth = d + GROUP * step
        strip_target = GROUP + 1 if step < 0 else 0
        halos.append((
            remote(
                volume.at[pl.ds(start, half), 0, pl.ds(EDGE, all_rows)],
                volume.at[pl.ds(target, half), 0, pl.ds(EDGE, all_rows)],
                halo_send.at[n], halo_recv.at[n], depth, light,
            ),
            remote(halo_strips.at[1 + own], halo_strips.at[strip_target], halo_send.at[2 + n], halo_recv.at[2 + n], depth, light),
        ))
    for part in range(2):
        first_j = 0 if part == 0 else GROUP - 1
        for m in range(GROUP):

            @pl.when(flip(j, m) == first_j)
            def _():
                for e in range(PAIR):
                    wait_brick(m, e, part)

    for (bulk, thin), exists in zip(halos, (has_below, has_above)):
        pl.when(exists)(bulk.start)
    for m, e in every:
        wait_strip(m, e)
    for (bulk, thin), exists in zip(halos, (has_below, has_above)):
        pl.when(exists)(thin.start)

    keep_labels.wait()
    mate_labels.wait_recv()
    def label_copy(c, m):
        at = pl.ds(pl.multiple_of(c * chunk_rows, SUB), chunk_rows)
        return remote(
            column_labels.at[flip(j, m), :, at], materials.at[pl.ds(slices * j, slices), at],
            label_send.at[c, m - 1], label_recv.at[c, m - 1], GROUP * k + flip(j, m), light,
        )

    def send_labels(c, carry):
        for m in ORDER:
            label_copy(c, m).start()
        return carry

    lax.fori_loop(0, chunks, send_labels, 0)
    own_labels = pltpu.make_async_copy(column_labels.at[j], materials.at[pl.ds(slices * j, slices)], mate_sem.at[0])
    own_labels.start()

    for part in range(2):
        first_j = 0 if part == 0 else GROUP - 1
        for m in range(GROUP):

            @pl.when(flip(j, m) != first_j)
            def _():
                for e in range(PAIR):
                    wait_brick(m, e, part)

    for n, exists in ((1, has_below), (0, has_above)):

        @pl.when(exists)
        def _():
            halos[n][0].wait_recv()
            halos[n][1].wait_recv()

    for number, reach in enumerate(reaches):
        wait_far(number, reach)
        if number + 1 < len(reaches):
            signal_far(number + 1, reaches[number + 1])

    def unpack(b, carry):
        for l_from in range(PAIR):
            strip = halo_strips[b, l_from]
            for z in range(slices):
                for g in range(row_tiles):
                    i = z * row_tiles + g
                    at = EDGE + rows * l_from + SUB * g
                    volume[slices * b + z, 1, at : at + SUB] = pltpu.roll(strip, (2 * LANE - 4 * i - 2) % LANE, 1)
        return carry

    lax.fori_loop(0, GROUP + 2, unpack, 0)

    edges = []
    if pairs > 1:
        for n, (step, source, target, exists) in enumerate(
            ((-PAIR, EDGE, EDGE + all_rows, has_before), (PAIR, EDGE + all_rows - SUB, EDGE - SUB, has_after))
        ):
            edges.append((
                remote(
                    volume.at[:, :, pl.ds(source, SUB)], volume.at[:, :, pl.ds(target, SUB)],
                    edge_send.at[n], edge_recv.at[n], d, light + step,
                ),
                exists,
            ))
        for one, exists in edges:
            pl.when(exists)(one.start)

    def zero_edge(at):
        for t in range(2):
            for z in range(half, all_slices + slices + half):
                volume[z, t, at : at + SUB] = zero

    if pairs > 1:
        for n, exists in ((0, has_after), (1, has_before)):
            pl.when(exists)(edges[n][0].wait_recv)
    pl.when(jnp.logical_not(has_before))(lambda: zero_edge(EDGE - SUB))
    pl.when(jnp.logical_not(has_after))(lambda: zero_edge(EDGE + all_rows))

    below = jnp.where(has_below, 1.0, 0.0)
    above = jnp.where(has_above, 1.0, 0.0)
    inside = jnp.where(lane < LANE // 2, jnp.where(q < PARTS - 1, 1.0, 0.0), jnp.where(q > 0, 1.0, 0.0))
    lane_first, lane_last = lane == 0, lane == LANE - 1

    def smooth_tile(g, carry):
        base = pl.multiple_of(EDGE + g * SUB, SUB)
        target = pl.multiple_of(SUB + g * SUB, SUB)
        at = pl.ds(base, SUB)

        def both(z):
            return [volume[z, t, at] for t in range(2)]

        first = slices - 1
        before, center = both(first - 1), both(first)
        for s in range(all_slices + 2):
            z = first + s
            after = both(z + 1)
            for t in range(2):
                own, other = center[t], center[1 - t]
                low = pltpu.roll(jnp.where(lane_last, other, own), 1, 1)
                high = pltpu.roll(jnp.where(lane_first, other, own), LANE - 1, 1)
                up = volume[z, t, pl.ds(base - 1, SUB)]
                down = volume[z, t, pl.ds(base + 1, SUB)]
                value = 0.4 * own + 0.1 * ((before[t] + after[t]) + (up + down) + (low + high))
                if s == 0:
                    value = value * below
                if s == all_slices + 1:
                    value = value * above
                if t == 1:
                    value = value * inside
                smooth[s, t, pl.ds(target, SUB)] = value
            before, center = center, after
        return carry

    ends = 1 if pairs > 1 else 0
    lax.fori_loop(-ends, all_rows // SUB + ends, smooth_tile, 0)

    def clear_rim(at):
        for s in range(1, all_slices + 1):
            smooth[s, 0, at : at + SUB] = zero

    pl.when(jnp.logical_not(has_before))(lambda: clear_rim(0))
    pl.when(jnp.logical_not(has_after))(lambda: clear_rim(SUB + all_rows))

    def slope_tile(g, carry):
        base = pl.multiple_of(SUB + g * SUB, SUB)
        target = pl.ds(pl.multiple_of(g * SUB, SUB), SUB)
        at = pl.ds(base, SUB)
        before, center = smooth[0, 0, at], smooth[1, 0, at]
        for z in range(all_slices):
            after = smooth[z + 2, 0, at]
            beside = smooth[z + 1, 1, at]
            low = pltpu.roll(jnp.where(lane_last, beside, center), 1, 1)
            high = pltpu.roll(jnp.where(lane_first, beside, center), LANE - 1, 1)
            up = smooth[z + 1, 0, pl.ds(base - 1, SUB)]
            down = smooth[z + 1, 0, pl.ds(base + 1, SUB)]
            grad_z, grad_x, grad_y = after - before, down - up, high - low
            facing = grad_x * lax.rsqrt(grad_z * grad_z + grad_x * grad_x + grad_y * grad_y + 0.2)
            heat[z, target] = jnp.exp(center)
            turned[z, target] = 0.5 + 0.5 * facing
            before, center = center, after
        return carry

    lax.fori_loop(0, all_rows // SUB, slope_tile, 0)

    loads[3].wait()
    loads[4].wait()
    tables = [zero for _ in range(4)]
    for n in range(extinction.shape[0]):
        tables[0] = jnp.where(lane == n, extinction[n], tables[0])
        for c in range(3):
            tables[c + 1] = jnp.where(lane == n, albedo[c, n], tables[c + 1])

    def unit_copy(u):
        return remote(
            parts_out.at[pl.ds(GROUP * u, GROUP)], parts_mid.at[u // groups, k],
            mid_send.at[u], mid_recv.at[u // groups], GROUP * (u % groups) + j, light,
        )

    def send_unit(u):
        @pl.when(u % groups != k)
        def _():
            unit_copy(u).start()

        @pl.when(u % groups == k)
        def _():
            pltpu.make_async_copy(
                parts_out.at[pl.ds(GROUP * u, GROUP)], parts_mid.at[u // groups, k], mid_recv.at[u // groups]
            ).start()

    def owned_here(u, i):
        return (u % groups == k) & (u // groups == l) & (j == i)

    def owner_copy(source, target, send, recv, u, i):
        return remote(source, target, send, recv, GROUP * (u % groups) + i, PAIR * p + u // groups)

    def send_owner(source, target, send, recv, u, i):
        own = owned_here(u, i)

        @pl.when(jnp.logical_not(own))
        def _():
            owner_copy(source, target, send, recv, u, i).start()

        @pl.when(own)
        def _():
            pltpu.make_async_copy(source, target, recv).start()

    def direct_parts(u, i):
        send = direct_send.at[u - direct_from, i]
        return parts_out.at[GROUP * u + i], direct_last.at[k, q], send, direct_recv, u, i

    def merged_parts(to_l, i):
        send = last_send.at[to_l, i]
        return parts_merged.at[to_l, i], parts_last.at[q], send, last_recv, to_l * groups + k, i

    def over(fronts):
        through = fronts[-1][3]
        back = fronts[-1][:3]
        for front in reversed(fronts[:-1]):
            through = through * front[3]
            back = [front[c] + front[3] * back[c] for c in range(3)]
        return back, through

    def channels(ref, at):
        return [ref[at + (pl.ds(c * block_rows, block_rows),)] for c in range(4)]

    per_tile = SUB // block_rows

    def shade_tile(g, lights):
        at = pl.ds(pl.multiple_of(g * SUB, SUB), SUB)
        lights = list(lights)
        remaining = jnp.ones((SUB, LANE), jnp.float32)
        colours = [zero] * 3
        for z in range(all_slices):
            index = materials[z, at]
            passed = jnp.exp(-(lookup(tables[0], index) * heat[z, at]))
            ahead = jnp.where(sub >= 1, pltpu.roll(passed, 1, 0), lights[z])
            for step in (1, 2, 4):
                ahead = ahead * jnp.where(sub >= step, pltpu.roll(ahead, step, 0), 1.0)
            lights[z] = jnp.broadcast_to((ahead * passed)[SUB - 1 :], (SUB, LANE))
            weight = (1.0 - passed) * remaining * (0.2 + ahead * turned[z, at])
            for c in range(3):
                colours[c] = colours[c] + lookup(tables[c + 1], index) * weight
            remaining = remaining * passed
        for b in range(per_tile):
            for c, value in enumerate(colours + [remaining]):
                parts_out[g * per_tile + b, c * block_rows : (c + 1) * block_rows] = value[b * block_rows : (b + 1) * block_rows]
        return tuple(lights)

    lights = (jnp.ones((SUB, LANE), jnp.float32),) * all_slices
    if pairs > 1:
        light_copy = remote(lights_out, lights_in, light_send, light_recv, d, light + PAIR)

        @pl.when(has_before)
        def _():
            light_copy.wait_recv()

        @pl.when(jnp.logical_not(has_before))
        def _():
            for z in range(all_slices):
                lights_in[z] = jnp.ones((SUB, LANE), jnp.float32)

        lights = tuple(lights_in[z] for z in range(all_slices))

    own_labels.wait()
    tiles_per_chunk = chunk_rows // SUB

    def shade_chunk(c, lights):
        for m in ORDER:
            label_copy(c, m).wait_recv()
        for n in range(tiles_per_chunk):
            lights = shade_tile(c * tiles_per_chunk + n, lights)
        return lights

    def merged_chunk(c, lights):
        lights = shade_chunk(c, lights)
        for n in range(chunk_units):
            send_unit(c * chunk_units + n)
        return lights

    def direct_chunk(c, lights):
        lights = shade_chunk(c, lights)
        for n in range(chunk_units):
            u = c * chunk_units + n
            for i in range(GROUP):
                send_owner(*direct_parts(u, i))
        return lights

    lights = lax.fori_loop(0, chunks - DIRECT, merged_chunk, lights)
    lights = lax.fori_loop(chunks - DIRECT, chunks, direct_chunk, lights)
    if pairs > 1:
        for z in range(all_slices):
            lights_out[z] = lights[z]
        pl.when(has_after)(light_copy.start)

    def bytes_of(ref, sem):
        pltpu.make_async_copy(ref, ref, sem).wait()

    def merge(to_l):
        bytes_of(parts_mid.at[to_l], mid_recv.at[to_l])
        for i in range(GROUP):
            back, through = over([channels(parts_mid, (to_l, front, i)) for front in range(groups)])
            for c, value in enumerate(back + [through]):
                parts_merged[to_l, i, c * block_rows : (c + 1) * block_rows] = value
            send_owner(*merged_parts(to_l, i))

    def merges_far(to_l):
        return to_l * groups + k < direct_from

    for to_l in range(PAIR):
        pl.when(merges_far(to_l))(functools.partial(merge, to_l))

    def finish(n, back, through):
        for c, value in enumerate(back + [1.0 - through]):
            blended[n, c * block_rows : (c + 1) * block_rows] = value
        for r in range(block_rows):
            at = r * PARTS * LANE + n * LANE
            out[:, at : at + LANE] = blended[n, pl.ds(r, 4, stride=block_rows), :]

    own_far = l * groups + k < direct_from

    @pl.when(own_far)
    def _():
        bytes_of(parts_last, last_recv)
        for n in range(PARTS):
            *back, through = channels(parts_last, (n,))
            finish(n, back, through)

    @pl.when(jnp.logical_not(own_far))
    def _():
        bytes_of(direct_last, direct_recv)
        for n in range(PARTS):
            finish(n, *over([channels(direct_last, (front, n)) for front in range(groups)]))

    for part in range(2):
        for m, e in every:
            if (m, e) != (0, 0):
                brick_copy(m, e, part).wait_send()
    for m, e in every:
        if (m, e) != (0, 0):
            strip_copy(m, e).wait_send()
    mate_labels.wait_send()
    for (bulk, thin), exists in zip(halos, (has_below, has_above)):

        @pl.when(exists)
        def _():
            bulk.wait_send()
            thin.wait_send()

    def sent_labels(c, carry):
        for m in ORDER:
            label_copy(c, m).wait_send()
        return carry

    lax.fori_loop(0, chunks, sent_labels, 0)

    def sent_unit(u, carry):
        @pl.when(u % groups != k)
        def _():
            unit_copy(u).wait_send()

        return carry

    lax.fori_loop(0, direct_from, sent_unit, 0)

    def sent_direct(u, carry):
        for i in range(GROUP):

            @pl.when(jnp.logical_not(owned_here(u, i)))
            def _():
                owner_copy(*direct_parts(u, i)).wait_send()

        return carry

    lax.fori_loop(direct_from, units, sent_direct, 0)
    for to_l in range(PAIR):
        for i in range(GROUP):

            @pl.when(merges_far(to_l) & jnp.logical_not(owned_here(to_l * groups + k, i)))
            def _():
                owner_copy(*merged_parts(to_l, i)).wait_send()

    for one, exists in edges:
        pl.when(exists)(one.wait_send)
    if pairs > 1:
        pl.when(has_after)(light_copy.wait_send)


def shards(density, labels, slice_order, extinction, albedo):
    depth_count = lax.axis_size("depth")
    light_count = lax.axis_size("light")
    slices, rows, columns = density.shape
    groups = depth_count // GROUP
    block_rows = rows // depth_count
    all_rows, all_slices = PAIR * rows, GROUP * slices
    units = PAIR * groups
    chunks = all_rows // max(2 * SUB, GROUP * block_rows)
    f32, i32 = jnp.float32, jnp.int32
    vmem, smem, dma = pltpu.VMEM, pltpu.SMEM, pltpu.SemaphoreType.DMA
    scratch = [
        vmem(density.shape, f32),
        vmem(labels.shape, i32),
        smem(slice_order.shape, i32),
        smem(extinction.shape, f32),
        smem(albedo.shape, f32),
        vmem((PARTS, slices, rows, LANE), f32),
        vmem((PARTS, SUB, LANE), f32),
        vmem((PAIR, GROUP, slices, rows, LANE), i32),
        vmem((GROUP, slices, all_rows, LANE), i32),
        vmem((all_slices + 2 * slices, 2, all_rows + 2 * EDGE, LANE), f32),
        vmem((GROUP + 2, PAIR, SUB, LANE), f32),
        vmem((all_slices, all_rows, LANE), i32),
        vmem((all_slices + 2, 2, all_rows + 2 * SUB, LANE), f32),
        vmem((all_slices, all_rows, LANE), f32),
        vmem((all_slices, all_rows, LANE), f32),
        vmem((PAIR * depth_count, 4 * block_rows, LANE), f32),
        vmem((PAIR, groups, GROUP, 4 * block_rows, LANE), f32),
        vmem((PAIR, GROUP, 4 * block_rows, LANE), f32),
        vmem((PARTS, 4 * block_rows, LANE), f32),
        vmem((groups, PARTS, 4 * block_rows, LANE), f32),
        vmem((PARTS, 4 * block_rows, LANE), f32),
        vmem((all_slices, SUB, LANE), f32),
        vmem((all_slices, SUB, LANE), f32),
        dma((5,)),
        dma((2, PARTS)),
        dma((2, PARTS)),
        dma((PARTS,)),
        dma((PARTS,)),
        dma((3,)),
        dma((chunks, GROUP - 1)),
        dma((chunks, GROUP - 1)),
        dma((4,)),
        dma((4,)),
        dma((2,)),
        dma((2,)),
        dma(()),
        dma(()),
        pltpu.SemaphoreType.REGULAR((max(1, len(far_reaches(groups))),)),
        dma((units,)),
        dma((PAIR,)),
        dma((PAIR, GROUP)),
        dma(()),
        dma((units, GROUP)),
        dma(()),
    ]
    image = pl.pallas_call(
        functools.partial(render_kernel, depth_count, light_count),
        in_specs=[FAR] * 5,
        out_specs=pl.BlockSpec(memory_space=pltpu.VMEM),
        out_shape=jax.ShapeDtypeStruct((4, block_rows * columns), f32),
        scratch_shapes=scratch,
        compiler_params=pltpu.CompilerParams(
            collective_id=0, has_side_effects=True, vmem_limit_bytes=40 * 1024 * 1024
        ),
    )(*(pltpu.with_memory_space_constraint(one, pltpu.HBM) for one in (density, labels, slice_order, extinction, albedo)))
    return image


def solution(mesh):
    return jax.shard_map(
        shards,
        mesh=mesh,
        in_specs=(P("depth", "light", None), P("depth", "light", None), P("depth"), P(), P()),
        out_specs=P(None, ("light", "depth")),
        check_vma=False,
    )
```

```python
import functools

import jax
import jax.numpy as jnp
from jax import lax
from jax.experimental import pallas as pl
from jax.experimental.pallas import tpu as pltpu
from jax.sharding import PartitionSpec as P

SUB, LANE = 8, 128
GROUP, PAIR = 4, 2
PARTS = GROUP * PAIR
MERGE_AFTER = 7
EDGE = 2 * SUB
MESH = pl.DeviceIdType.MESH
FAR = pl.BlockSpec(memory_space=pltpu.HBM)
ORDER = (3, 1, 2)


def flip(value, mask):
    for bit in (1, 2):
        if mask & bit:
            value = value + bit * (1 - 2 * ((value // bit) % 2))
    return value


def far_reaches(groups):
    reaches, known = [], 1
    while known < groups - 1:
        reaches.append(known)
        known *= 2
    return reaches


def lookup(table, index):
    return jnp.take_along_axis(table, index, axis=1, mode="promise_in_bounds")


def render_kernel(
    depth_count, light_count,
    density_far, labels_far, order_far, extinction_far, albedo_far,
    out,
    density, labels, order, extinction, albedo,
    bricks, strips, labels_out, column_labels, volume, halo_strips, materials,
    smooth, heat, turned, parts_out, parts_mid, parts_merged, parts_last, direct_last, blended, lights_in, lights_out,
    load_sem, brick_send, brick_recv, strip_send, strip_recv, mate_sem, label_send, label_recv,
    halo_send, halo_recv, edge_send, edge_recv, light_send, light_recv, ready_sem,
    mid_send, mid_recv, last_send, last_recv, direct_send, direct_recv,
):
    slices, rows = density.shape[:2]
    half = slices // 2
    groups, pairs = depth_count // GROUP, light_count // PAIR
    all_rows, all_slices = PAIR * rows, GROUP * slices
    block_rows = rows // depth_count
    row_tiles = rows // SUB
    unit_rows = GROUP * block_rows
    units = PAIR * groups
    chunk_rows = max(2 * SUB, unit_rows)
    chunks = all_rows // chunk_rows
    chunk_units = chunk_rows // unit_rows
    direct_from = units // 2
    merged_chunks = direct_from // chunk_units
    merge_at = min(MERGE_AFTER, chunks)
    d = lax.axis_index("depth")
    light = lax.axis_index("light")
    k, j = d // GROUP, d % GROUP
    p, l = light // PAIR, light % PAIR
    q = PAIR * j + l
    has_below, has_above = k > 0, k < groups - 1
    has_before, has_after = p > 0, p < pairs - 1
    lane = lax.broadcasted_iota(jnp.int32, (SUB, LANE), 1)
    sub = lax.broadcasted_iota(jnp.int32, (SUB, LANE), 0)
    zero = jnp.zeros((SUB, LANE), jnp.float32)

    loads = [
        pltpu.make_async_copy(source, target, load_sem.at[n])
        for n, (source, target) in enumerate(
            ((order_far, order), (density_far, density), (labels_far, labels), (extinction_far, extinction), (albedo_far, albedo))
        )
    ]
    for one in loads:
        one.start()

    barrier = pltpu.get_barrier_semaphore()

    for m in range(GROUP):
        for e in range(PAIR):
            if (m, e) != (0, 0):
                mate = (GROUP * k + flip(j, m), PAIR * p + (l if e == 0 else 1 - l))
                pl.semaphore_signal(barrier, inc=1, device_id=mate, device_id_type=MESH)
    greeted = PARTS - 1
    for exists, step in ((has_below, -GROUP), (has_above, GROUP)):

        @pl.when(exists)
        def _():
            pl.semaphore_signal(barrier, inc=1, device_id=(d + step, light), device_id_type=MESH)

        greeted = greeted + jnp.where(exists, 1, 0)
    if pairs > 1:
        for exists, step in ((has_before, -PAIR), (has_after, PAIR)):

            @pl.when(exists)
            def _():
                pl.semaphore_signal(barrier, inc=1, device_id=(d, light + step), device_id_type=MESH)

            greeted = greeted + jnp.where(exists, 1, 0)

    def remote(source, target, send, recv, depth, to_light):
        return pltpu.make_async_remote_copy(
            src_ref=source, dst_ref=target, send_sem=send, recv_sem=recv,
            device_id=(depth, to_light), device_id_type=MESH,
        )

    loads[0].wait()
    loads[1].wait()

    def pack_bricks(part):
        for z in range(half):
            z = half * part + z
            at = lax.rem(order[z], slices)
            for g in range(row_tiles):
                for t in range(PARTS):
                    tile = density[at, g * SUB : (g + 1) * SUB, t * LANE : (t + 1) * LANE]
                    bricks[t, z, g * SUB : (g + 1) * SUB, :] = tile

    pack_bricks(jnp.where(j == GROUP - 1, 1, 0))

    def brick_spot(from_j, from_l, part):
        return volume.at[
            pl.ds(slices + slices * from_j + half * part, half), 0, pl.ds(EDGE + rows * from_l, rows)
        ]

    def brick_copy(m, e, part):
        to_q = PAIR * flip(j, m) + (l if e == 0 else 1 - l)
        source = bricks.at[to_q, pl.ds(half * part, half)]
        slot = PAIR * m + e
        if slot == 0:
            return pltpu.make_async_copy(source, brick_spot(j, l, part), brick_recv.at[part, 0])
        return remote(
            source, brick_spot(j, l, part), brick_send.at[part, slot], brick_recv.at[part, slot],
            GROUP * k + flip(j, m), PAIR * p + to_q % PAIR,
        )

    def strip_copy(m, e):
        to_q = PAIR * flip(j, m) + (l if e == 0 else 1 - l)
        target = halo_strips.at[1 + j, l]
        slot = PAIR * m + e
        if slot == 0:
            return pltpu.make_async_copy(strips.at[to_q], target, strip_recv.at[0])
        return remote(
            strips.at[to_q], target, strip_send.at[slot], strip_recv.at[slot],
            GROUP * k + flip(j, m), PAIR * p + to_q % PAIR,
        )

    every = [(m, e) for m in ORDER + (0,) for e in range(PAIR)]
    early = jnp.where(j == GROUP - 1, 1, 0)
    pl.semaphore_wait(barrier, greeted)
    for m, e in every:
        brick_copy(m, e, early).start()
    pack_bricks(1 - early)

    def pack_strips(z, packed):
        packed = list(packed)
        for g in range(row_tiles):
            i = z * row_tiles + g
            rows_at = slice(g * SUB, (g + 1) * SUB)
            for t in range(PARTS):
                left = bricks[t - 1, z, rows_at, :] if t > 0 else zero
                right = bricks[t + 1, z, rows_at, :] if t < PARTS - 1 else zero
                rims = pltpu.roll(jnp.where(lane < LANE // 2, right, left), lax.rem(4 * i + 2, LANE), 1)
                packed[t] = jnp.where(lane // 4 == i, rims, packed[t])
        return tuple(packed)

    packed = lax.fori_loop(0, slices, pack_strips, (zero,) * PARTS)
    for t in range(PARTS):
        strips[t] = packed[t]
    for m, e in every:
        strip_copy(m, e).start()
    for m, e in every:
        brick_copy(m, e, 1 - early).start()

    @pl.when(jnp.logical_not(has_below))
    def _():
        volume[half : slices, 0] = jnp.zeros((half,) + volume.shape[2:], jnp.float32)
        halo_strips[0] = jnp.zeros(halo_strips.shape[1:], jnp.float32)

    @pl.when(jnp.logical_not(has_above))
    def _():
        volume[slices + all_slices : slices + all_slices + half, 0] = jnp.zeros((half,) + volume.shape[2:], jnp.float32)
        halo_strips[GROUP + 1] = jnp.zeros(halo_strips.shape[1:], jnp.float32)


    def signal_far(number, reach):
        for exists, step in ((k >= reach, -reach), (k + reach < groups, reach)):

            @pl.when(exists)
            def _():
                pl.semaphore_signal(
                    ready_sem.at[number], inc=1, device_id=(d + GROUP * step, light), device_id_type=MESH
                )

    def wait_far(number, reach):
        count = jnp.where(k >= reach, 1, 0) + jnp.where(k + reach < groups, 1, 0)
        pl.semaphore_wait(ready_sem.at[number], count)

    reaches = far_reaches(groups)
    if reaches:
        signal_far(0, reaches[0])

    loads[2].wait()

    def pack_labels(i, carry):
        z, g = i // row_tiles, i % row_tiles
        at = lax.rem(order[z], slices)
        base = pl.multiple_of(g * SUB, SUB)
        for t in range(PARTS):
            labels_out[t % PAIR, t // PAIR, z, pl.ds(base, SUB), :] = labels[at, pl.ds(base, SUB), t * LANE : (t + 1) * LANE]
        return carry

    lax.fori_loop(0, slices * row_tiles, pack_labels, 0)
    own_rows = column_labels.at[:, :, pl.ds(rows * l, rows)]
    keep_labels = pltpu.make_async_copy(labels_out.at[l], own_rows, mate_sem.at[0])
    mate_labels = remote(labels_out.at[1 - l], own_rows, mate_sem.at[1], mate_sem.at[2], d, PAIR * p + 1 - l)
    keep_labels.start()
    mate_labels.start()

    def wait_brick(m, e, part):
        to_q = PAIR * flip(j, m) + (l if e == 0 else 1 - l)
        if isinstance(m, int) and PAIR * m + e == 0:
            brick_copy(0, 0, part).wait()
        else:
            spot = brick_spot(flip(j, m), to_q % PAIR, part)
            remote(spot, spot, brick_send.at[part, PAIR * m + e], brick_recv.at[part, PAIR * m + e], d, light).wait_recv()

    def wait_strip(m, e):
        if PAIR * m + e == 0:
            strip_copy(0, 0).wait()
        else:
            strip_copy(m, e).wait_recv()

    halos = []
    for n, (step, own, part, target) in enumerate(
        ((-1, 0, 0, slices + all_slices), (1, GROUP - 1, 1, half))
    ):
        start = slices + slices * own + half * part
        depth = d + GROUP * step
        strip_target = GROUP + 1 if step < 0 else 0
        halos.append((
            remote(
                volume.at[pl.ds(start, half), 0, pl.ds(EDGE, all_rows)],
                volume.at[pl.ds(target, half), 0, pl.ds(EDGE, all_rows)],
                halo_send.at[n], halo_recv.at[n], depth, light,
            ),
            remote(halo_strips.at[1 + own], halo_strips.at[strip_target], halo_send.at[2 + n], halo_recv.at[2 + n], depth, light),
        ))
    for part in range(2):
        first_j = 0 if part == 0 else GROUP - 1
        for m in range(GROUP):

            @pl.when(flip(j, m) == first_j)
            def _():
                for e in range(PAIR):
                    wait_brick(m, e, part)

    for (bulk, thin), exists in zip(halos, (has_below, has_above)):
        pl.when(exists)(bulk.start)
    for number in range(len(reaches) - 1):
        wait_far(number, reaches[number])
        signal_far(number + 1, reaches[number + 1])
    for m, e in every:
        wait_strip(m, e)
    for (bulk, thin), exists in zip(halos, (has_below, has_above)):
        pl.when(exists)(thin.start)

    keep_labels.wait()
    mate_labels.wait_recv()
    def label_copy(c, m):
        at = pl.ds(pl.multiple_of(c * chunk_rows, SUB), chunk_rows)
        return remote(
            column_labels.at[flip(j, m), :, at], materials.at[pl.ds(slices * j, slices), at],
            label_send.at[c, m - 1], label_recv.at[c, m - 1], GROUP * k + flip(j, m), light,
        )

    def send_labels(c, carry):
        for m in ORDER:
            label_copy(c, m).start()
        return carry

    lax.fori_loop(0, chunks, send_labels, 0)
    own_labels = pltpu.make_async_copy(column_labels.at[j], materials.at[pl.ds(slices * j, slices)], mate_sem.at[0])
    own_labels.start()

    for part in range(2):
        first_j = 0 if part == 0 else GROUP - 1
        for m in range(GROUP):

            @pl.when(flip(j, m) != first_j)
            def _():
                for e in range(PAIR):
                    wait_brick(m, e, part)

    for n, exists in ((1, has_below), (0, has_above)):

        @pl.when(exists)
        def _():
            halos[n][0].wait_recv()
            halos[n][1].wait_recv()

    def unpack(b, carry):
        for l_from in range(PAIR):
            strip = halo_strips[b, l_from]
            for z in range(slices):
                for g in range(row_tiles):
                    i = z * row_tiles + g
                    at = EDGE + rows * l_from + SUB * g
                    volume[slices * b + z, 1, at : at + SUB] = pltpu.roll(strip, (2 * LANE - 4 * i - 2) % LANE, 1)
        return carry

    lax.fori_loop(0, GROUP + 2, unpack, 0)

    edges = []
    if pairs > 1:
        for n, (step, source, target, exists) in enumerate(
            ((-PAIR, EDGE, EDGE + all_rows, has_before), (PAIR, EDGE + all_rows - SUB, EDGE - SUB, has_after))
        ):
            edges.append((
                remote(
                    volume.at[:, :, pl.ds(source, SUB)], volume.at[:, :, pl.ds(target, SUB)],
                    edge_send.at[n], edge_recv.at[n], d, light + step,
                ),
                exists,
            ))
        for one, exists in edges:
            pl.when(exists)(one.start)

    def zero_edge(at):
        for t in range(2):
            for z in range(half, all_slices + slices + half):
                volume[z, t, at : at + SUB] = zero

    if pairs > 1:
        for n, exists in ((0, has_after), (1, has_before)):
            pl.when(exists)(edges[n][0].wait_recv)
    pl.when(jnp.logical_not(has_before))(lambda: zero_edge(EDGE - SUB))
    pl.when(jnp.logical_not(has_after))(lambda: zero_edge(EDGE + all_rows))

    below = jnp.where(has_below, 1.0, 0.0)
    above = jnp.where(has_above, 1.0, 0.0)
    inside = jnp.where(lane < LANE // 2, jnp.where(q < PARTS - 1, 1.0, 0.0), jnp.where(q > 0, 1.0, 0.0))
    lane_first, lane_last = lane == 0, lane == LANE - 1

    def smooth_tile(g, carry):
        base = pl.multiple_of(EDGE + g * SUB, SUB)
        target = pl.multiple_of(SUB + g * SUB, SUB)
        at = pl.ds(base, SUB)

        def both(z):
            return [volume[z, t, at] for t in range(2)]

        first = slices - 1
        before, center = both(first - 1), both(first)
        for s in range(all_slices + 2):
            z = first + s
            after = both(z + 1)
            for t in range(2):
                own, other = center[t], center[1 - t]
                low = pltpu.roll(jnp.where(lane_last, other, own), 1, 1)
                high = pltpu.roll(jnp.where(lane_first, other, own), LANE - 1, 1)
                up = volume[z, t, pl.ds(base - 1, SUB)]
                down = volume[z, t, pl.ds(base + 1, SUB)]
                value = 0.4 * own + 0.1 * ((before[t] + after[t]) + (up + down) + (low + high))
                if s == 0:
                    value = value * below
                if s == all_slices + 1:
                    value = value * above
                if t == 1:
                    value = value * inside
                smooth[s, t, pl.ds(target, SUB)] = value
            before, center = center, after
        return carry

    ends = 1 if pairs > 1 else 0
    lax.fori_loop(-ends, all_rows // SUB + ends, smooth_tile, 0)

    def clear_rim(at):
        for s in range(1, all_slices + 1):
            smooth[s, 0, at : at + SUB] = zero

    pl.when(jnp.logical_not(has_before))(lambda: clear_rim(0))
    pl.when(jnp.logical_not(has_after))(lambda: clear_rim(SUB + all_rows))

    def slope_tile(g, carry):
        base = pl.multiple_of(SUB + g * SUB, SUB)
        target = pl.ds(pl.multiple_of(g * SUB, SUB), SUB)
        at = pl.ds(base, SUB)
        before, center = smooth[0, 0, at], smooth[1, 0, at]
        for z in range(all_slices):
            after = smooth[z + 2, 0, at]
            beside = smooth[z + 1, 1, at]
            low = pltpu.roll(jnp.where(lane_last, beside, center), 1, 1)
            high = pltpu.roll(jnp.where(lane_first, beside, center), LANE - 1, 1)
            up = smooth[z + 1, 0, pl.ds(base - 1, SUB)]
            down = smooth[z + 1, 0, pl.ds(base + 1, SUB)]
            grad_z, grad_x, grad_y = after - before, down - up, high - low
            facing = grad_x * lax.rsqrt(grad_z * grad_z + grad_x * grad_x + grad_y * grad_y + 0.2)
            heat[z, target] = jnp.exp(center)
            turned[z, target] = 0.5 + 0.5 * facing
            before, center = center, after
        return carry

    lax.fori_loop(0, all_rows // SUB, slope_tile, 0)

    loads[3].wait()
    loads[4].wait()
    tables = [zero for _ in range(4)]
    for n in range(extinction.shape[0]):
        tables[0] = jnp.where(lane == n, extinction[n], tables[0])
        for c in range(3):
            tables[c + 1] = jnp.where(lane == n, albedo[c, n], tables[c + 1])

    def unit_copy(u):
        return remote(
            parts_out.at[pl.ds(GROUP * u, GROUP)], parts_mid.at[u // groups, k],
            mid_send.at[u], mid_recv.at[u // groups], GROUP * (u % groups) + j, light,
        )

    def send_unit(u):
        @pl.when(u % groups != k)
        def _():
            unit_copy(u).start()

        @pl.when(u % groups == k)
        def _():
            pltpu.make_async_copy(
                parts_out.at[pl.ds(GROUP * u, GROUP)], parts_mid.at[u // groups, k], mid_recv.at[u // groups]
            ).start()

    def owned_here(u, i):
        return (u % groups == k) & (u // groups == l) & (j == i)

    def owner_copy(source, target, send, recv, u, i):
        return remote(source, target, send, recv, GROUP * (u % groups) + i, PAIR * p + u // groups)

    def send_owner(source, target, send, recv, u, i):
        own = owned_here(u, i)

        @pl.when(jnp.logical_not(own))
        def _():
            owner_copy(source, target, send, recv, u, i).start()

        @pl.when(own)
        def _():
            pltpu.make_async_copy(source, target, recv).start()

    def direct_parts(u, i):
        send = direct_send.at[u - direct_from, i]
        return parts_out.at[GROUP * u + i], direct_last.at[k, q], send, direct_recv, u, i

    def merged_parts(to_l, i):
        send = last_send.at[to_l, i]
        return parts_merged.at[to_l, i], parts_last.at[q], send, last_recv, to_l * groups + k, i

    paired = 2 * block_rows == SUB
    top = sub < SUB // 2

    def turn(value):
        return pltpu.roll(value, SUB // 2, 0)

    def fetch(ref, at):
        if paired:
            return [ref[at + (pl.ds(SUB * n, SUB),)] for n in range(2)]
        return [ref[at + (pl.ds(block_rows * c, block_rows),)] for c in range(4)]

    def keep(ref, at, values):
        size = SUB if paired else block_rows
        for n, value in enumerate(values):
            ref[at + (pl.ds(size * n, size),)] = value

    def over(fronts):
        back = fronts[-1]
        for front in reversed(fronts[:-1]):
            shade = jnp.where(top, turn(front[-1]), front[-1]) if paired else front[-1]
            clear = 1.0 - shade
            back = [one + clear * other for one, other in zip(front, back)]
        return back

    per_tile = SUB // block_rows

    def shade_tile(g, lights):
        at = pl.ds(pl.multiple_of(g * SUB, SUB), SUB)
        lights = list(lights)
        remaining = jnp.ones((SUB, LANE), jnp.float32)
        colours = [zero] * 3
        for z in range(all_slices):
            index = materials[z, at]
            passed = jnp.exp(-(lookup(tables[0], index) * heat[z, at]))
            ahead = jnp.where(sub >= 1, pltpu.roll(passed, 1, 0), lights[z])
            for step in (1, 2, 4):
                ahead = ahead * jnp.where(sub >= step, pltpu.roll(ahead, step, 0), 1.0)
            lights[z] = jnp.broadcast_to((ahead * passed)[SUB - 1 :], (SUB, LANE))
            weight = (1.0 - passed) * remaining * (0.2 + ahead * turned[z, at])
            for c in range(3):
                colours[c] = colours[c] + lookup(tables[c + 1], index) * weight
            remaining = remaining * passed
        values = colours + [1.0 - remaining]
        for b in range(per_tile):
            if paired and b == 0:
                block = [jnp.where(top, values[n], turn(values[n + 1])) for n in (0, 2)]
            elif paired:
                block = [jnp.where(top, turn(values[n]), values[n + 1]) for n in (0, 2)]
            else:
                block = [value[b * block_rows : (b + 1) * block_rows] for value in values]
            keep(parts_out, (g * per_tile + b,), block)
        return tuple(lights)

    lights = (jnp.ones((SUB, LANE), jnp.float32),) * all_slices
    if pairs > 1:
        light_copy = remote(lights_out, lights_in, light_send, light_recv, d, light + PAIR)

        @pl.when(has_before)
        def _():
            light_copy.wait_recv()

        @pl.when(jnp.logical_not(has_before))
        def _():
            for z in range(all_slices):
                lights_in[z] = jnp.ones((SUB, LANE), jnp.float32)

        lights = tuple(lights_in[z] for z in range(all_slices))

    if reaches:
        wait_far(len(reaches) - 1, reaches[-1])
    own_labels.wait()
    tiles_per_chunk = chunk_rows // SUB

    def shade_chunk(c, lights):
        for m in ORDER:
            label_copy(c, m).wait_recv()
        for n in range(tiles_per_chunk):
            lights = shade_tile(c * tiles_per_chunk + n, lights)
        return lights

    def merged_chunk(c, lights):
        lights = shade_chunk(c, lights)
        for n in range(chunk_units):
            send_unit(c * chunk_units + n)
        return lights

    def direct_chunk(c, lights):
        lights = shade_chunk(c, lights)
        for n in range(chunk_units):
            u = c * chunk_units + n
            for i in range(GROUP):
                send_owner(*direct_parts(u, i))
        return lights

    def bytes_of(ref, sem):
        pltpu.make_async_copy(ref, ref, sem).wait()

    def merge(to_l):
        bytes_of(parts_mid.at[to_l], mid_recv.at[to_l])
        for i in range(GROUP):
            keep(parts_merged, (to_l, i), over([fetch(parts_mid, (to_l, front, i)) for front in range(groups)]))
        for i in range(GROUP):
            send_owner(*merged_parts(to_l, i))

    def merges_far(to_l):
        return to_l * groups + k < direct_from

    lights = lax.fori_loop(0, merged_chunks, merged_chunk, lights)
    lights = lax.fori_loop(merged_chunks, merge_at, direct_chunk, lights)
    merge(0)
    lights = lax.fori_loop(merge_at, chunks, direct_chunk, lights)
    if pairs > 1:
        for z in range(all_slices):
            lights_out[z] = lights[z]
        pl.when(has_after)(light_copy.start)

    own_far = l * groups + k < direct_from

    @pl.when(own_far)
    def _():
        bytes_of(parts_last, last_recv)
        for n in range(PARTS):
            keep(blended, (n,), fetch(parts_last, (n,)))

    @pl.when(jnp.logical_not(own_far))
    def _():
        bytes_of(direct_last, direct_recv)
        for n in range(PARTS):
            keep(blended, (n,), over([fetch(direct_last, (front, n)) for front in range(groups)]))

    for n in range(PARTS):
        for r in range(block_rows):
            at = r * PARTS * LANE + n * LANE
            out[:, at : at + LANE] = blended[n, pl.ds(r, 4, stride=block_rows), :]

    for part in range(2):
        for m, e in every:
            if (m, e) != (0, 0):
                brick_copy(m, e, part).wait_send()
    for m, e in every:
        if (m, e) != (0, 0):
            strip_copy(m, e).wait_send()
    mate_labels.wait_send()
    for (bulk, thin), exists in zip(halos, (has_below, has_above)):

        @pl.when(exists)
        def _():
            bulk.wait_send()
            thin.wait_send()

    def sent_labels(c, carry):
        for m in ORDER:
            label_copy(c, m).wait_send()
        return carry

    lax.fori_loop(0, chunks, sent_labels, 0)

    def sent_unit(u, carry):
        @pl.when(u % groups != k)
        def _():
            unit_copy(u).wait_send()

        return carry

    lax.fori_loop(0, direct_from, sent_unit, 0)

    def sent_direct(u, carry):
        for i in range(GROUP):

            @pl.when(jnp.logical_not(owned_here(u, i)))
            def _():
                owner_copy(*direct_parts(u, i)).wait_send()

        return carry

    lax.fori_loop(direct_from, units, sent_direct, 0)
    for to_l in range(PAIR):
        for i in range(GROUP):

            @pl.when(merges_far(to_l) & jnp.logical_not(owned_here(to_l * groups + k, i)))
            def _():
                owner_copy(*merged_parts(to_l, i)).wait_send()

    for one, exists in edges:
        pl.when(exists)(one.wait_send)
    if pairs > 1:
        pl.when(has_after)(light_copy.wait_send)


def shards(density, labels, slice_order, extinction, albedo):
    depth_count = lax.axis_size("depth")
    light_count = lax.axis_size("light")
    slices, rows, columns = density.shape
    groups = depth_count // GROUP
    block_rows = rows // depth_count
    all_rows, all_slices = PAIR * rows, GROUP * slices
    units = PAIR * groups
    chunks = all_rows // max(2 * SUB, GROUP * block_rows)
    f32, i32 = jnp.float32, jnp.int32
    vmem, smem, dma = pltpu.VMEM, pltpu.SMEM, pltpu.SemaphoreType.DMA
    scratch = [
        vmem(density.shape, f32),
        vmem(labels.shape, i32),
        smem(slice_order.shape, i32),
        smem(extinction.shape, f32),
        smem(albedo.shape, f32),
        vmem((PARTS, slices, rows, LANE), f32),
        vmem((PARTS, SUB, LANE), f32),
        vmem((PAIR, GROUP, slices, rows, LANE), i32),
        vmem((GROUP, slices, all_rows, LANE), i32),
        vmem((all_slices + 2 * slices, 2, all_rows + 2 * EDGE, LANE), f32),
        vmem((GROUP + 2, PAIR, SUB, LANE), f32),
        vmem((all_slices, all_rows, LANE), i32),
        vmem((all_slices + 2, 2, all_rows + 2 * SUB, LANE), f32),
        vmem((all_slices, all_rows, LANE), f32),
        vmem((all_slices, all_rows, LANE), f32),
        vmem((PAIR * depth_count, 4 * block_rows, LANE), f32),
        vmem((PAIR, groups, GROUP, 4 * block_rows, LANE), f32),
        vmem((PAIR, GROUP, 4 * block_rows, LANE), f32),
        vmem((PARTS, 4 * block_rows, LANE), f32),
        vmem((groups, PARTS, 4 * block_rows, LANE), f32),
        vmem((PARTS, 4 * block_rows, LANE), f32),
        vmem((all_slices, SUB, LANE), f32),
        vmem((all_slices, SUB, LANE), f32),
        dma((5,)),
        dma((2, PARTS)),
        dma((2, PARTS)),
        dma((PARTS,)),
        dma((PARTS,)),
        dma((3,)),
        dma((chunks, GROUP - 1)),
        dma((chunks, GROUP - 1)),
        dma((4,)),
        dma((4,)),
        dma((2,)),
        dma((2,)),
        dma(()),
        dma(()),
        pltpu.SemaphoreType.REGULAR((max(1, len(far_reaches(groups))),)),
        dma((units,)),
        dma((PAIR,)),
        dma((PAIR, GROUP)),
        dma(()),
        dma((units, GROUP)),
        dma(()),
    ]
    image = pl.pallas_call(
        functools.partial(render_kernel, depth_count, light_count),
        in_specs=[FAR] * 5,
        out_specs=pl.BlockSpec(memory_space=pltpu.VMEM),
        out_shape=jax.ShapeDtypeStruct((4, block_rows * columns), f32),
        scratch_shapes=scratch,
        compiler_params=pltpu.CompilerParams(
            collective_id=0, has_side_effects=True, vmem_limit_bytes=40 * 1024 * 1024
        ),
    )(*(pltpu.with_memory_space_constraint(one, pltpu.HBM) for one in (density, labels, slice_order, extinction, albedo)))
    return image


def solution(mesh):
    return jax.shard_map(
        shards,
        mesh=mesh,
        in_specs=(P("depth", "light", None), P("depth", "light", None), P("depth"), P(), P()),
        out_specs=P(None, ("light", "depth")),
        check_vma=False,
    )
```

```python
import functools

import jax
import jax.numpy as jnp
from jax import lax
from jax.experimental import pallas as pl
from jax.experimental.pallas import tpu as pltpu
from jax.sharding import PartitionSpec as P

SUB, LANE = 8, 128
GROUP, PAIR = 4, 2
PARTS = GROUP * PAIR
CHUNK_TILES = 2
MERGE_AFTER = 12
EDGE = 2 * SUB
MESH = pl.DeviceIdType.MESH
FAR = pl.BlockSpec(memory_space=pltpu.HBM)
ORDER = (3, 1, 2)


def flip(value, mask):
    for bit in (1, 2):
        if mask & bit:
            value = value + bit * (1 - 2 * ((value // bit) % 2))
    return value


def far_reaches(groups):
    reaches, known = [], 1
    while known < groups - 1:
        reaches.append(known)
        known *= 2
    return reaches


def lookup(table, index):
    return jnp.take_along_axis(table, index, axis=1, mode="promise_in_bounds")


def render_kernel(
    depth_count, light_count,
    density_far, labels_far, order_far, extinction_far, albedo_far,
    out,
    density, labels, order, extinction, albedo,
    bricks, strips, labels_out, column_labels, volume, halo_strips, materials,
    smooth, heat, turned, parts_out, parts_mid, parts_merged, parts_last, direct_last, blended, lights_in, lights_out,
    load_sem, brick_send, brick_recv, strip_send, strip_recv, mate_sem, label_send, label_recv,
    halo_send, halo_recv, edge_send, edge_recv, light_send, light_recv, ready_sem,
    mid_send, mid_recv, last_send, last_recv, direct_send, direct_recv,
):
    slices, rows = density.shape[:2]
    half = slices // 2
    groups, pairs = depth_count // GROUP, light_count // PAIR
    all_rows, all_slices = PAIR * rows, GROUP * slices
    block_rows = rows // depth_count
    row_tiles = rows // SUB
    unit_rows = GROUP * block_rows
    units = PAIR * groups
    chunk_tiles = CHUNK_TILES
    chunk_rows = chunk_tiles * SUB
    chunks = all_rows // chunk_rows
    step_rows = max(chunk_rows, unit_rows)
    step_units, step_tiles = step_rows // unit_rows, step_rows // SUB
    direct_from = units // 2
    merged_steps = direct_from // step_units
    merge_at = min(MERGE_AFTER // step_tiles, all_rows // step_rows)
    d = lax.axis_index("depth")
    light = lax.axis_index("light")
    k, j = d // GROUP, d % GROUP
    p, l = light // PAIR, light % PAIR
    q = PAIR * j + l
    has_below, has_above = k > 0, k < groups - 1
    has_before, has_after = p > 0, p < pairs - 1
    lane = lax.broadcasted_iota(jnp.int32, (SUB, LANE), 1)
    sub = lax.broadcasted_iota(jnp.int32, (SUB, LANE), 0)
    zero = jnp.zeros((SUB, LANE), jnp.float32)

    loads = [
        pltpu.make_async_copy(source, target, load_sem.at[n])
        for n, (source, target) in enumerate(
            ((order_far, order), (density_far, density), (labels_far, labels), (extinction_far, extinction), (albedo_far, albedo))
        )
    ]
    for one in loads:
        one.start()

    barrier = pltpu.get_barrier_semaphore()

    for m in range(GROUP):
        for e in range(PAIR):
            if (m, e) != (0, 0):
                mate = (GROUP * k + flip(j, m), PAIR * p + (l if e == 0 else 1 - l))
                pl.semaphore_signal(barrier, inc=1, device_id=mate, device_id_type=MESH)
    greeted = PARTS - 1
    for exists, step in ((has_below, -GROUP), (has_above, GROUP)):

        @pl.when(exists)
        def _():
            pl.semaphore_signal(barrier, inc=1, device_id=(d + step, light), device_id_type=MESH)

        greeted = greeted + jnp.where(exists, 1, 0)
    if pairs > 1:
        for exists, step in ((has_before, -PAIR), (has_after, PAIR)):

            @pl.when(exists)
            def _():
                pl.semaphore_signal(barrier, inc=1, device_id=(d, light + step), device_id_type=MESH)

            greeted = greeted + jnp.where(exists, 1, 0)

    def remote(source, target, send, recv, depth, to_light):
        return pltpu.make_async_remote_copy(
            src_ref=source, dst_ref=target, send_sem=send, recv_sem=recv,
            device_id=(depth, to_light), device_id_type=MESH,
        )

    loads[0].wait()
    loads[1].wait()

    def pack_bricks(part):
        for z in range(half):
            z = half * part + z
            at = lax.rem(order[z], slices)
            for g in range(row_tiles):
                for t in range(PARTS):
                    tile = density[at, g * SUB : (g + 1) * SUB, t * LANE : (t + 1) * LANE]
                    bricks[t, z, g * SUB : (g + 1) * SUB, :] = tile

    pack_bricks(jnp.where(j == GROUP - 1, 1, 0))

    def brick_spot(from_j, from_l, part):
        return volume.at[
            pl.ds(slices + slices * from_j + half * part, half), 0, pl.ds(EDGE + rows * from_l, rows)
        ]

    def brick_copy(m, e, part):
        to_q = PAIR * flip(j, m) + (l if e == 0 else 1 - l)
        source = bricks.at[to_q, pl.ds(half * part, half)]
        slot = PAIR * m + e
        if slot == 0:
            return pltpu.make_async_copy(source, brick_spot(j, l, part), brick_recv.at[part, 0])
        return remote(
            source, brick_spot(j, l, part), brick_send.at[part, slot], brick_recv.at[part, slot],
            GROUP * k + flip(j, m), PAIR * p + to_q % PAIR,
        )

    def strip_copy(m, e):
        to_q = PAIR * flip(j, m) + (l if e == 0 else 1 - l)
        target = halo_strips.at[1 + j, l]
        slot = PAIR * m + e
        if slot == 0:
            return pltpu.make_async_copy(strips.at[to_q], target, strip_recv.at[0])
        return remote(
            strips.at[to_q], target, strip_send.at[slot], strip_recv.at[slot],
            GROUP * k + flip(j, m), PAIR * p + to_q % PAIR,
        )

    every = [(m, e) for m in ORDER + (0,) for e in range(PAIR)]
    early = jnp.where(j == GROUP - 1, 1, 0)
    pl.semaphore_wait(barrier, greeted)
    for m, e in every:
        brick_copy(m, e, early).start()
    pack_bricks(1 - early)

    def pack_strips(z, packed):
        packed = list(packed)
        for g in range(row_tiles):
            i = z * row_tiles + g
            rows_at = slice(g * SUB, (g + 1) * SUB)
            for t in range(PARTS):
                left = bricks[t - 1, z, rows_at, :] if t > 0 else zero
                right = bricks[t + 1, z, rows_at, :] if t < PARTS - 1 else zero
                rims = pltpu.roll(jnp.where(lane < LANE // 2, right, left), lax.rem(4 * i + 2, LANE), 1)
                packed[t] = jnp.where(lane // 4 == i, rims, packed[t])
        return tuple(packed)

    packed = lax.fori_loop(0, slices, pack_strips, (zero,) * PARTS)
    for t in range(PARTS):
        strips[t] = packed[t]
    for m, e in every:
        strip_copy(m, e).start()
    for m, e in every:
        brick_copy(m, e, 1 - early).start()

    @pl.when(jnp.logical_not(has_below))
    def _():
        volume[half : slices, 0] = jnp.zeros((half,) + volume.shape[2:], jnp.float32)
        halo_strips[0] = jnp.zeros(halo_strips.shape[1:], jnp.float32)

    @pl.when(jnp.logical_not(has_above))
    def _():
        volume[slices + all_slices : slices + all_slices + half, 0] = jnp.zeros((half,) + volume.shape[2:], jnp.float32)
        halo_strips[GROUP + 1] = jnp.zeros(halo_strips.shape[1:], jnp.float32)


    def signal_far(number, reach):
        for exists, step in ((k >= reach, -reach), (k + reach < groups, reach)):

            @pl.when(exists)
            def _():
                pl.semaphore_signal(
                    ready_sem.at[number], inc=1, device_id=(d + GROUP * step, light), device_id_type=MESH
                )

    def wait_far(number, reach):
        count = jnp.where(k >= reach, 1, 0) + jnp.where(k + reach < groups, 1, 0)
        pl.semaphore_wait(ready_sem.at[number], count)

    reaches = far_reaches(groups)
    if reaches:
        signal_far(0, reaches[0])

    loads[2].wait()

    def pack_labels(i, carry):
        z, g = i // row_tiles, i % row_tiles
        at = lax.rem(order[z], slices)
        base = pl.multiple_of(g * SUB, SUB)
        spot = pl.multiple_of(g % chunk_tiles * SUB, SUB)
        for t in range(PARTS):
            labels_out[t % PAIR, t // PAIR, g // chunk_tiles, z, pl.ds(spot, SUB), :] = labels[at, pl.ds(base, SUB), t * LANE : (t + 1) * LANE]
        return carry

    lax.fori_loop(0, slices * row_tiles, pack_labels, 0)
    own_rows = column_labels.at[:, pl.ds(chunks // PAIR * l, chunks // PAIR)]
    keep_labels = pltpu.make_async_copy(labels_out.at[l], own_rows, mate_sem.at[0])
    mate_labels = remote(labels_out.at[1 - l], own_rows, mate_sem.at[1], mate_sem.at[2], d, PAIR * p + 1 - l)
    keep_labels.start()
    mate_labels.start()

    def wait_brick(m, e, part):
        to_q = PAIR * flip(j, m) + (l if e == 0 else 1 - l)
        if isinstance(m, int) and PAIR * m + e == 0:
            brick_copy(0, 0, part).wait()
        else:
            spot = brick_spot(flip(j, m), to_q % PAIR, part)
            remote(spot, spot, brick_send.at[part, PAIR * m + e], brick_recv.at[part, PAIR * m + e], d, light).wait_recv()

    def wait_strip(m, e):
        if PAIR * m + e == 0:
            strip_copy(0, 0).wait()
        else:
            strip_copy(m, e).wait_recv()

    halos = []
    for n, (step, own, part, target) in enumerate(
        ((-1, 0, 0, slices + all_slices), (1, GROUP - 1, 1, half))
    ):
        start = slices + slices * own + half * part
        depth = d + GROUP * step
        strip_target = GROUP + 1 if step < 0 else 0
        halos.append((
            remote(
                volume.at[pl.ds(start, half), 0, pl.ds(EDGE, all_rows)],
                volume.at[pl.ds(target, half), 0, pl.ds(EDGE, all_rows)],
                halo_send.at[n], halo_recv.at[n], depth, light,
            ),
            remote(halo_strips.at[1 + own], halo_strips.at[strip_target], halo_send.at[2 + n], halo_recv.at[2 + n], depth, light),
        ))
    for part in range(2):
        first_j = 0 if part == 0 else GROUP - 1
        for m in range(GROUP):

            @pl.when(flip(j, m) == first_j)
            def _():
                for e in range(PAIR):
                    wait_brick(m, e, part)

    for (bulk, thin), exists in zip(halos, (has_below, has_above)):
        pl.when(exists)(bulk.start)
    for number in range(len(reaches) - 1):
        wait_far(number, reaches[number])
        signal_far(number + 1, reaches[number + 1])
    for m, e in every:
        wait_strip(m, e)
    for (bulk, thin), exists in zip(halos, (has_below, has_above)):
        pl.when(exists)(thin.start)

    keep_labels.wait()
    mate_labels.wait_recv()
    def label_copy(c, m):
        return remote(
            column_labels.at[flip(j, m), c], materials.at[c, pl.ds(slices * j, slices)],
            label_send.at[c, m - 1], label_recv.at[c, m - 1], GROUP * k + flip(j, m), light,
        )

    def send_labels(c, carry):
        for m in ORDER:
            label_copy(c, m).start()
        return carry

    lax.fori_loop(0, chunks, send_labels, 0)
    own_labels = pltpu.make_async_copy(column_labels.at[j], materials.at[:, pl.ds(slices * j, slices)], mate_sem.at[0])
    own_labels.start()

    def unpack(b, carry):
        for l_from in range(PAIR):
            strip = halo_strips[b, l_from]
            for z in range(slices):
                for g in range(row_tiles):
                    i = z * row_tiles + g
                    at = EDGE + rows * l_from + SUB * g
                    volume[slices * b + z, 1, at : at + SUB] = pltpu.roll(strip, (2 * LANE - 4 * i - 2) % LANE, 1)
        return carry

    lax.fori_loop(1, GROUP + 1, unpack, 0)

    def zero_edge(at):
        for t in range(2):
            for z in range(half, all_slices + slices + half):
                volume[z, t, at : at + SUB] = zero

    pl.when(jnp.logical_not(has_before))(lambda: zero_edge(EDGE - SUB))
    pl.when(jnp.logical_not(has_after))(lambda: zero_edge(EDGE + all_rows))

    def clear_rim(at):
        for s in range(1, all_slices + 1):
            smooth[s, 0, at : at + SUB] = zero

    def clear_rims():
        pl.when(jnp.logical_not(has_before))(lambda: clear_rim(0))
        pl.when(jnp.logical_not(has_after))(lambda: clear_rim(SUB + all_rows))

    if pairs == 1:
        clear_rims()

    loads[3].wait()
    loads[4].wait()
    tables = [zero for _ in range(4)]
    for n in range(extinction.shape[0]):
        tables[0] = jnp.where(lane == n, extinction[n], tables[0])
        for c in range(3):
            tables[c + 1] = jnp.where(lane == n, albedo[c, n], tables[c + 1])


    for part in range(2):
        first_j = 0 if part == 0 else GROUP - 1
        for m in range(GROUP):

            @pl.when(flip(j, m) != first_j)
            def _():
                for e in range(PAIR):
                    wait_brick(m, e, part)

    for n, exists in ((1, has_below), (0, has_above)):

        @pl.when(exists)
        def _():
            halos[n][0].wait_recv()
            halos[n][1].wait_recv()

    for b in (0, GROUP + 1):
        unpack(b, 0)

    edges = []
    if pairs > 1:
        for n, (step, source, target, exists) in enumerate(
            ((-PAIR, EDGE, EDGE + all_rows, has_before), (PAIR, EDGE + all_rows - SUB, EDGE - SUB, has_after))
        ):
            edges.append((
                remote(
                    volume.at[:, :, pl.ds(source, SUB)], volume.at[:, :, pl.ds(target, SUB)],
                    edge_send.at[n], edge_recv.at[n], d, light + step,
                ),
                exists,
            ))
        for one, exists in edges:
            pl.when(exists)(one.start)

    if pairs > 1:
        for n, exists in ((0, has_after), (1, has_before)):
            pl.when(exists)(edges[n][0].wait_recv)
    below = jnp.where(has_below, 1.0, 0.0)
    above = jnp.where(has_above, 1.0, 0.0)
    inside = jnp.where(lane < LANE // 2, jnp.where(q < PARTS - 1, 1.0, 0.0), jnp.where(q > 0, 1.0, 0.0))
    lane_first, lane_last = lane == 0, lane == LANE - 1

    def smooth_tile(g, carry):
        base = pl.multiple_of(EDGE + g * SUB, SUB)
        target = pl.multiple_of(SUB + g * SUB, SUB)
        at = pl.ds(base, SUB)

        def both(z):
            return [volume[z, t, at] for t in range(2)]

        first = slices - 1
        before, center = both(first - 1), both(first)
        for s in range(all_slices + 2):
            z = first + s
            after = both(z + 1)
            for t in range(2 if 0 < s <= all_slices else 1):
                own, other = center[t], center[1 - t]
                low = pltpu.roll(jnp.where(lane_last, other, own), 1, 1)
                high = pltpu.roll(jnp.where(lane_first, other, own), LANE - 1, 1)
                up = volume[z, t, pl.ds(base - 1, SUB)]
                down = volume[z, t, pl.ds(base + 1, SUB)]
                value = 0.4 * own + 0.1 * ((before[t] + after[t]) + (up + down) + (low + high))
                if s == 0:
                    value = value * below
                if s == all_slices + 1:
                    value = value * above
                if t == 1:
                    value = value * inside
                smooth[s, t, pl.ds(target, SUB)] = value
            before, center = center, after
        return carry

    ends = 1 if pairs > 1 else 0
    lax.fori_loop(-ends, all_rows // SUB + ends, smooth_tile, 0)

    if pairs > 1:
        clear_rims()

    def slope_tile(g, carry):
        base = pl.multiple_of(SUB + g * SUB, SUB)
        target = pl.ds(pl.multiple_of(g * SUB, SUB), SUB)
        at = pl.ds(base, SUB)
        before, center = smooth[0, 0, at], smooth[1, 0, at]
        for z in range(all_slices):
            after = smooth[z + 2, 0, at]
            beside = smooth[z + 1, 1, at]
            low = pltpu.roll(jnp.where(lane_last, beside, center), 1, 1)
            high = pltpu.roll(jnp.where(lane_first, beside, center), LANE - 1, 1)
            up = smooth[z + 1, 0, pl.ds(base - 1, SUB)]
            down = smooth[z + 1, 0, pl.ds(base + 1, SUB)]
            grad_z, grad_x, grad_y = after - before, down - up, high - low
            facing = grad_x * lax.rsqrt(grad_z * grad_z + grad_x * grad_x + grad_y * grad_y + 0.2)
            heat[z, target] = jnp.exp(center)
            turned[z, target] = 0.5 + 0.5 * facing
            before, center = center, after
        return carry

    lax.fori_loop(0, all_rows // SUB, slope_tile, 0)

    def unit_copy(u):
        return remote(
            parts_out.at[pl.ds(GROUP * u, GROUP)], parts_mid.at[u // groups, k],
            mid_send.at[u], mid_recv.at[u // groups], GROUP * (u % groups) + j, light,
        )

    def send_unit(u):
        @pl.when(u % groups != k)
        def _():
            unit_copy(u).start()

        @pl.when(u % groups == k)
        def _():
            pltpu.make_async_copy(
                parts_out.at[pl.ds(GROUP * u, GROUP)], parts_mid.at[u // groups, k], mid_recv.at[u // groups]
            ).start()

    def owned_here(u, i):
        return (u % groups == k) & (u // groups == l) & (j == i)

    def owner_copy(source, target, send, recv, u, i):
        return remote(source, target, send, recv, GROUP * (u % groups) + i, PAIR * p + u // groups)

    def send_owner(source, target, send, recv, u, i):
        own = owned_here(u, i)

        @pl.when(jnp.logical_not(own))
        def _():
            owner_copy(source, target, send, recv, u, i).start()

        @pl.when(own)
        def _():
            pltpu.make_async_copy(source, target, recv).start()

    def direct_parts(u, i):
        send = direct_send.at[u - direct_from, i]
        return parts_out.at[GROUP * u + i], direct_last.at[k, q], send, direct_recv, u, i

    def merged_parts(to_l, i):
        send = last_send.at[to_l, i]
        return parts_merged.at[to_l, i], parts_last.at[q], send, last_recv, to_l * groups + k, i

    paired = 2 * block_rows == SUB
    top = sub < SUB // 2

    def turn(value):
        return pltpu.roll(value, SUB // 2, 0)

    def fetch(ref, at):
        if paired:
            return [ref[at + (pl.ds(SUB * n, SUB),)] for n in range(2)]
        return [ref[at + (pl.ds(block_rows * c, block_rows),)] for c in range(4)]

    def keep(ref, at, values):
        size = SUB if paired else block_rows
        for n, value in enumerate(values):
            ref[at + (pl.ds(size * n, size),)] = value

    def over(fronts):
        back = fronts[-1]
        for front in reversed(fronts[:-1]):
            shade = jnp.where(top, turn(front[-1]), front[-1]) if paired else front[-1]
            clear = 1.0 - shade
            back = [one + clear * other for one, other in zip(front, back)]
        return back

    per_tile = SUB // block_rows

    def shade_tile(g, lights):
        at = pl.ds(pl.multiple_of(g * SUB, SUB), SUB)
        spot = pl.ds(pl.multiple_of(g % chunk_tiles * SUB, SUB), SUB)
        lights = list(lights)
        remaining = jnp.ones((SUB, LANE), jnp.float32)
        colours = [zero] * 3
        for z in range(all_slices):
            index = materials[g // chunk_tiles, z, spot]
            passed = jnp.exp(-(lookup(tables[0], index) * heat[z, at]))
            ahead = jnp.where(sub >= 1, pltpu.roll(passed, 1, 0), lights[z])
            for step in (1, 2, 4):
                ahead = ahead * jnp.where(sub >= step, pltpu.roll(ahead, step, 0), 1.0)
            lights[z] = jnp.broadcast_to((ahead * passed)[SUB - 1 :], (SUB, LANE))
            weight = (1.0 - passed) * remaining * (0.2 + ahead * turned[z, at])
            for c in range(3):
                colours[c] = colours[c] + lookup(tables[c + 1], index) * weight
            remaining = remaining * passed
        values = colours + [1.0 - remaining]
        for b in range(per_tile):
            if paired and b == 0:
                block = [jnp.where(top, values[n], turn(values[n + 1])) for n in (0, 2)]
            elif paired:
                block = [jnp.where(top, turn(values[n]), values[n + 1]) for n in (0, 2)]
            else:
                block = [value[b * block_rows : (b + 1) * block_rows] for value in values]
            keep(parts_out, (g * per_tile + b,), block)
        return tuple(lights)

    lights = (jnp.ones((SUB, LANE), jnp.float32),) * all_slices
    if pairs > 1:
        light_copy = remote(lights_out, lights_in, light_send, light_recv, d, light + PAIR)

        @pl.when(has_before)
        def _():
            light_copy.wait_recv()

        @pl.when(jnp.logical_not(has_before))
        def _():
            for z in range(all_slices):
                lights_in[z] = jnp.ones((SUB, LANE), jnp.float32)

        lights = tuple(lights_in[z] for z in range(all_slices))

    if reaches:
        wait_far(len(reaches) - 1, reaches[-1])
    own_labels.wait()

    def shade_wait(g, n, lights):
        if n % chunk_tiles == 0:
            for m in ORDER:
                label_copy(g // chunk_tiles, m).wait_recv()
        return shade_tile(g, lights)

    def merged_step(step, lights):
        for n in range(step_tiles):
            lights = shade_wait(step * step_tiles + n, n, lights)
        for n in range(step_units):
            send_unit(step * step_units + n)
        return lights

    def direct_step(step, lights):
        for n in range(step_tiles):
            g = step * step_tiles + n
            lights = shade_wait(g, n, lights)
            for b in range(per_tile):
                block = g * per_tile + b
                send_owner(*direct_parts(block // GROUP, block % GROUP))
        return lights

    def bytes_of(ref, sem):
        pltpu.make_async_copy(ref, ref, sem).wait()

    def merge(to_l):
        bytes_of(parts_mid.at[to_l], mid_recv.at[to_l])
        for i in range(GROUP):
            keep(parts_merged, (to_l, i), over([fetch(parts_mid, (to_l, front, i)) for front in range(groups)]))
        for i in range(GROUP):
            send_owner(*merged_parts(to_l, i))

    def merges_far(to_l):
        return to_l * groups + k < direct_from

    lights = lax.fori_loop(0, merged_steps, merged_step, lights)
    lights = lax.fori_loop(merged_steps, merge_at, direct_step, lights)
    merge(0)
    lights = lax.fori_loop(merge_at, all_rows // step_rows, direct_step, lights)
    if pairs > 1:
        for z in range(all_slices):
            lights_out[z] = lights[z]
        pl.when(has_after)(light_copy.start)

    for part in range(2):
        for m, e in every:
            if (m, e) != (0, 0):
                brick_copy(m, e, part).wait_send()
    for m, e in every:
        if (m, e) != (0, 0):
            strip_copy(m, e).wait_send()
    mate_labels.wait_send()
    for (bulk, thin), exists in zip(halos, (has_below, has_above)):

        @pl.when(exists)
        def _():
            bulk.wait_send()
            thin.wait_send()

    def sent_labels(c, carry):
        for m in ORDER:
            label_copy(c, m).wait_send()
        return carry

    lax.fori_loop(0, chunks, sent_labels, 0)

    def sent_unit(u, carry):
        @pl.when(u % groups != k)
        def _():
            unit_copy(u).wait_send()

        return carry

    lax.fori_loop(0, direct_from, sent_unit, 0)

    def sent_direct(u, carry):
        for i in range(GROUP):

            @pl.when(jnp.logical_not(owned_here(u, i)))
            def _():
                owner_copy(*direct_parts(u, i)).wait_send()

        return carry

    lax.fori_loop(direct_from, units, sent_direct, 0)
    for to_l in range(PAIR):
        for i in range(GROUP):

            @pl.when(merges_far(to_l) & jnp.logical_not(owned_here(to_l * groups + k, i)))
            def _():
                owner_copy(*merged_parts(to_l, i)).wait_send()

    for one, exists in edges:
        pl.when(exists)(one.wait_send)
    if pairs > 1:
        pl.when(has_after)(light_copy.wait_send)

    own_far = l * groups + k < direct_from

    @pl.when(own_far)
    def _():
        bytes_of(parts_last, last_recv)
        for n in range(PARTS):
            keep(blended, (n,), fetch(parts_last, (n,)))

    @pl.when(jnp.logical_not(own_far))
    def _():
        bytes_of(direct_last, direct_recv)
        for n in range(PARTS):
            keep(blended, (n,), over([fetch(direct_last, (front, n)) for front in range(groups)]))

    for n in range(PARTS):
        for r in range(block_rows):
            at = r * PARTS * LANE + n * LANE
            out[:, at : at + LANE] = blended[n, pl.ds(r, 4, stride=block_rows), :]


def shards(density, labels, slice_order, extinction, albedo):
    depth_count = lax.axis_size("depth")
    light_count = lax.axis_size("light")
    slices, rows, columns = density.shape
    groups = depth_count // GROUP
    block_rows = rows // depth_count
    all_rows, all_slices = PAIR * rows, GROUP * slices
    units = PAIR * groups
    chunk_rows = CHUNK_TILES * SUB
    chunks = all_rows // chunk_rows
    f32, i32 = jnp.float32, jnp.int32
    vmem, smem, dma = pltpu.VMEM, pltpu.SMEM, pltpu.SemaphoreType.DMA
    scratch = [
        vmem(density.shape, f32),
        vmem(labels.shape, i32),
        smem(slice_order.shape, i32),
        smem(extinction.shape, f32),
        smem(albedo.shape, f32),
        vmem((PARTS, slices, rows, LANE), f32),
        vmem((PARTS, SUB, LANE), f32),
        vmem((PAIR, GROUP, chunks // PAIR, slices, chunk_rows, LANE), i32),
        vmem((GROUP, chunks, slices, chunk_rows, LANE), i32),
        vmem((all_slices + 2 * slices, 2, all_rows + 2 * EDGE, LANE), f32),
        vmem((GROUP + 2, PAIR, SUB, LANE), f32),
        vmem((chunks, all_slices, chunk_rows, LANE), i32),
        vmem((all_slices + 2, 2, all_rows + 2 * SUB, LANE), f32),
        vmem((all_slices, all_rows, LANE), f32),
        vmem((all_slices, all_rows, LANE), f32),
        vmem((PAIR * depth_count, 4 * block_rows, LANE), f32),
        vmem((PAIR, groups, GROUP, 4 * block_rows, LANE), f32),
        vmem((PAIR, GROUP, 4 * block_rows, LANE), f32),
        vmem((PARTS, 4 * block_rows, LANE), f32),
        vmem((groups, PARTS, 4 * block_rows, LANE), f32),
        vmem((PARTS, 4 * block_rows, LANE), f32),
        vmem((all_slices, SUB, LANE), f32),
        vmem((all_slices, SUB, LANE), f32),
        dma((5,)),
        dma((2, PARTS)),
        dma((2, PARTS)),
        dma((PARTS,)),
        dma((PARTS,)),
        dma((3,)),
        dma((chunks, GROUP - 1)),
        dma((chunks, GROUP - 1)),
        dma((4,)),
        dma((4,)),
        dma((2,)),
        dma((2,)),
        dma(()),
        dma(()),
        pltpu.SemaphoreType.REGULAR((max(1, len(far_reaches(groups))),)),
        dma((units,)),
        dma((PAIR,)),
        dma((PAIR, GROUP)),
        dma(()),
        dma((units, GROUP)),
        dma(()),
    ]
    image = pl.pallas_call(
        functools.partial(render_kernel, depth_count, light_count),
        in_specs=[FAR] * 5,
        out_specs=pl.BlockSpec(memory_space=pltpu.VMEM),
        out_shape=jax.ShapeDtypeStruct((4, block_rows * columns), f32),
        scratch_shapes=scratch,
        compiler_params=pltpu.CompilerParams(
            collective_id=0, has_side_effects=True, vmem_limit_bytes=40 * 1024 * 1024
        ),
    )(*(pltpu.with_memory_space_constraint(one, pltpu.HBM) for one in (density, labels, slice_order, extinction, albedo)))
    return image


def solution(mesh):
    return jax.shard_map(
        shards,
        mesh=mesh,
        in_specs=(P("depth", "light", None), P("depth", "light", None), P("depth"), P(), P()),
        out_specs=P(None, ("light", "depth")),
        check_vma=False,
    )
```

```python
import functools

import jax
import jax.numpy as jnp
from jax import lax
from jax.experimental import pallas as pl
from jax.experimental.pallas import tpu as pltpu
from jax.sharding import PartitionSpec as P

SUB, LANE = 8, 128
GROUP, PAIR = 4, 2
PARTS = GROUP * PAIR
CHUNK_TILES = 2
MERGE_AFTER = 12
EDGE = 2 * SUB
MESH = pl.DeviceIdType.MESH
FAR = pl.BlockSpec(memory_space=pltpu.HBM)
ORDER = (3, 1, 2)


def flip(value, mask):
    for bit in (1, 2):
        if mask & bit:
            value = value + bit * (1 - 2 * ((value // bit) % 2))
    return value


def far_reaches(groups):
    reaches, known = [], 1
    while known < groups - 1:
        reaches.append(known)
        known *= 2
    return reaches


def lookup(table, index):
    return jnp.take_along_axis(table, index, axis=1, mode="promise_in_bounds")


def render_kernel(
    depth_count, light_count,
    density_far, labels_far, order_far, extinction_far, albedo_far,
    out,
    density, labels, order, extinction, albedo,
    bricks, strips, labels_out, column_labels, volume, halo_strips, materials,
    smooth, heat, turned, parts_out, parts_mid, parts_merged, parts_last, direct_last, blended, lights_in, lights_out,
    load_sem, brick_send, brick_recv, strip_send, strip_recv, mate_sem, label_send, label_recv,
    halo_send, halo_recv, edge_send, edge_recv, light_send, light_recv, ready_sem,
    mid_send, mid_recv, last_send, last_recv, direct_send, direct_recv,
):
    slices, rows = density.shape[:2]
    half = slices // 2
    groups, pairs = depth_count // GROUP, light_count // PAIR
    all_rows, all_slices = PAIR * rows, GROUP * slices
    block_rows = rows // depth_count
    row_tiles = rows // SUB
    unit_rows = GROUP * block_rows
    units = PAIR * groups
    chunk_tiles = CHUNK_TILES
    chunk_rows = chunk_tiles * SUB
    chunks = all_rows // chunk_rows
    step_rows = max(chunk_rows, unit_rows)
    step_units, step_tiles = step_rows // unit_rows, step_rows // SUB
    direct_from = units // 2
    merged_steps = direct_from // step_units
    merge_at = min(MERGE_AFTER // step_tiles, all_rows // step_rows)
    d = lax.axis_index("depth")
    light = lax.axis_index("light")
    k, j = d // GROUP, d % GROUP
    p, l = light // PAIR, light % PAIR
    q = PAIR * j + l
    has_below, has_above = k > 0, k < groups - 1
    has_before, has_after = p > 0, p < pairs - 1
    lane = lax.broadcasted_iota(jnp.int32, (SUB, LANE), 1)
    sub = lax.broadcasted_iota(jnp.int32, (SUB, LANE), 0)
    zero = jnp.zeros((SUB, LANE), jnp.float32)

    barrier = pltpu.get_barrier_semaphore()

    for m in range(GROUP):
        for e in range(PAIR):
            if (m, e) != (0, 0):
                mate = (GROUP * k + flip(j, m), PAIR * p + (l if e == 0 else 1 - l))
                pl.semaphore_signal(barrier, inc=1, device_id=mate, device_id_type=MESH)
    greeted = PARTS - 1
    for exists, step in ((has_below, -GROUP), (has_above, GROUP)):

        @pl.when(exists)
        def _():
            pl.semaphore_signal(barrier, inc=1, device_id=(d + step, light), device_id_type=MESH)

        greeted = greeted + jnp.where(exists, 1, 0)
    if pairs > 1:
        for exists, step in ((has_before, -PAIR), (has_after, PAIR)):

            @pl.when(exists)
            def _():
                pl.semaphore_signal(barrier, inc=1, device_id=(d, light + step), device_id_type=MESH)

            greeted = greeted + jnp.where(exists, 1, 0)

    loads = [
        pltpu.make_async_copy(source, target, load_sem.at[n])
        for n, (source, target) in enumerate(
            ((order_far, order), (density_far, density), (labels_far, labels), (extinction_far, extinction), (albedo_far, albedo))
        )
    ]
    for one in loads:
        one.start()

    def remote(source, target, send, recv, depth, to_light):
        return pltpu.make_async_remote_copy(
            src_ref=source, dst_ref=target, send_sem=send, recv_sem=recv,
            device_id=(depth, to_light), device_id_type=MESH,
        )

    loads[0].wait()
    loads[1].wait()

    def pack_bricks(part):
        for z in range(half):
            z = half * part + z
            at = lax.rem(order[z], slices)
            for g in range(row_tiles):
                for t in range(PARTS):
                    tile = density[at, g * SUB : (g + 1) * SUB, t * LANE : (t + 1) * LANE]
                    bricks[t, z, g * SUB : (g + 1) * SUB, :] = tile

    pack_bricks(jnp.where(j == GROUP - 1, 1, 0))

    def brick_spot(from_j, from_l, part):
        return volume.at[
            pl.ds(slices + slices * from_j + half * part, half), 0, pl.ds(EDGE + rows * from_l, rows)
        ]

    def brick_copy(m, e, part):
        to_q = PAIR * flip(j, m) + (l if e == 0 else 1 - l)
        source = bricks.at[to_q, pl.ds(half * part, half)]
        slot = PAIR * m + e
        if slot == 0:
            return pltpu.make_async_copy(source, brick_spot(j, l, part), brick_recv.at[part, 0])
        return remote(
            source, brick_spot(j, l, part), brick_send.at[part, slot], brick_recv.at[part, slot],
            GROUP * k + flip(j, m), PAIR * p + to_q % PAIR,
        )

    def strip_copy(m, e):
        to_q = PAIR * flip(j, m) + (l if e == 0 else 1 - l)
        target = halo_strips.at[1 + j, l]
        slot = PAIR * m + e
        if slot == 0:
            return pltpu.make_async_copy(strips.at[to_q], target, strip_recv.at[0])
        return remote(
            strips.at[to_q], target, strip_send.at[slot], strip_recv.at[slot],
            GROUP * k + flip(j, m), PAIR * p + to_q % PAIR,
        )

    every = [(m, e) for m in ORDER + (0,) for e in range(PAIR)]
    early = jnp.where(j == GROUP - 1, 1, 0)
    pl.semaphore_wait(barrier, greeted)
    for m, e in every:
        brick_copy(m, e, early).start()
    pack_bricks(1 - early)

    def pack_strips(z, packed):
        packed = list(packed)
        for g in range(row_tiles):
            i = z * row_tiles + g
            rows_at = slice(g * SUB, (g + 1) * SUB)
            for t in range(PARTS):
                left = bricks[t - 1, z, rows_at, :] if t > 0 else zero
                right = bricks[t + 1, z, rows_at, :] if t < PARTS - 1 else zero
                rims = pltpu.roll(jnp.where(lane < LANE // 2, right, left), lax.rem(4 * i + 2, LANE), 1)
                packed[t] = jnp.where(lane // 4 == i, rims, packed[t])
        return tuple(packed)

    packed = lax.fori_loop(0, slices, pack_strips, (zero,) * PARTS)
    for t in range(PARTS):
        strips[t] = packed[t]
    for m, e in every:
        strip_copy(m, e).start()
    for m, e in every:
        brick_copy(m, e, 1 - early).start()

    @pl.when(jnp.logical_not(has_below))
    def _():
        volume[half : slices, 0] = jnp.zeros((half,) + volume.shape[2:], jnp.float32)
        halo_strips[0] = jnp.zeros(halo_strips.shape[1:], jnp.float32)

    @pl.when(jnp.logical_not(has_above))
    def _():
        volume[slices + all_slices : slices + all_slices + half, 0] = jnp.zeros((half,) + volume.shape[2:], jnp.float32)
        halo_strips[GROUP + 1] = jnp.zeros(halo_strips.shape[1:], jnp.float32)


    def signal_far(number, reach):
        for exists, step in ((k >= reach, -reach), (k + reach < groups, reach)):

            @pl.when(exists)
            def _():
                pl.semaphore_signal(
                    ready_sem.at[number], inc=1, device_id=(d + GROUP * step, light), device_id_type=MESH
                )

    def wait_far(number, reach):
        count = jnp.where(k >= reach, 1, 0) + jnp.where(k + reach < groups, 1, 0)
        pl.semaphore_wait(ready_sem.at[number], count)

    reaches = far_reaches(groups)
    if reaches:
        signal_far(0, reaches[0])

    loads[2].wait()

    def pack_labels(i, carry):
        z, g = i // row_tiles, i % row_tiles
        at = lax.rem(order[z], slices)
        base = pl.multiple_of(g * SUB, SUB)
        spot = pl.multiple_of(g % chunk_tiles * SUB, SUB)
        for t in range(PARTS):
            labels_out[t % PAIR, t // PAIR, g // chunk_tiles, z, pl.ds(spot, SUB), :] = labels[at, pl.ds(base, SUB), t * LANE : (t + 1) * LANE]
        return carry

    lax.fori_loop(0, slices * row_tiles, pack_labels, 0)
    own_rows = column_labels.at[:, pl.ds(chunks // PAIR * l, chunks // PAIR)]
    keep_labels = pltpu.make_async_copy(labels_out.at[l], own_rows, mate_sem.at[0])
    mate_labels = remote(labels_out.at[1 - l], own_rows, mate_sem.at[1], mate_sem.at[2], d, PAIR * p + 1 - l)
    keep_labels.start()
    mate_labels.start()

    def wait_brick(m, e, part):
        to_q = PAIR * flip(j, m) + (l if e == 0 else 1 - l)
        if isinstance(m, int) and PAIR * m + e == 0:
            brick_copy(0, 0, part).wait()
        else:
            spot = brick_spot(flip(j, m), to_q % PAIR, part)
            remote(spot, spot, brick_send.at[part, PAIR * m + e], brick_recv.at[part, PAIR * m + e], d, light).wait_recv()

    def wait_strip(m, e):
        if PAIR * m + e == 0:
            strip_copy(0, 0).wait()
        else:
            strip_copy(m, e).wait_recv()

    halos = []
    for n, (step, own, part, target) in enumerate(
        ((-1, 0, 0, slices + all_slices), (1, GROUP - 1, 1, half))
    ):
        start = slices + slices * own + half * part
        depth = d + GROUP * step
        strip_target = GROUP + 1 if step < 0 else 0
        halos.append((
            remote(
                volume.at[pl.ds(start, half), 0, pl.ds(EDGE, all_rows)],
                volume.at[pl.ds(target, half), 0, pl.ds(EDGE, all_rows)],
                halo_send.at[n], halo_recv.at[n], depth, light,
            ),
            remote(halo_strips.at[1 + own], halo_strips.at[strip_target], halo_send.at[2 + n], halo_recv.at[2 + n], depth, light),
        ))
    for part in range(2):
        first_j = 0 if part == 0 else GROUP - 1
        for m in range(GROUP):

            @pl.when(flip(j, m) == first_j)
            def _():
                for e in range(PAIR):
                    wait_brick(m, e, part)

    for (bulk, thin), exists in zip(halos, (has_below, has_above)):
        pl.when(exists)(bulk.start)
    for number in range(len(reaches) - 1):
        wait_far(number, reaches[number])
        signal_far(number + 1, reaches[number + 1])
    for m, e in every:
        wait_strip(m, e)
    for (bulk, thin), exists in zip(halos, (has_below, has_above)):
        pl.when(exists)(thin.start)

    keep_labels.wait()
    mate_labels.wait_recv()
    def label_copy(c, m):
        return remote(
            column_labels.at[flip(j, m), c], materials.at[c, pl.ds(slices * j, slices)],
            label_send.at[c, m - 1], label_recv.at[c, m - 1], GROUP * k + flip(j, m), light,
        )

    def send_labels(c, carry):
        for m in ORDER:
            label_copy(c, m).start()
        return carry

    lax.fori_loop(0, chunks, send_labels, 0)
    own_labels = pltpu.make_async_copy(column_labels.at[j], materials.at[:, pl.ds(slices * j, slices)], mate_sem.at[0])
    own_labels.start()

    def unpack(b, carry):
        for l_from in range(PAIR):
            strip = halo_strips[b, l_from]
            for z in range(slices):
                for g in range(row_tiles):
                    i = z * row_tiles + g
                    at = EDGE + rows * l_from + SUB * g
                    volume[slices * b + z, 1, at : at + SUB] = pltpu.roll(strip, (2 * LANE - 4 * i - 2) % LANE, 1)
        return carry

    lax.fori_loop(1, GROUP + 1, unpack, 0)

    def zero_edge(at):
        for t in range(2):
            for z in range(half, all_slices + slices + half):
                volume[z, t, at : at + SUB] = zero

    pl.when(jnp.logical_not(has_before))(lambda: zero_edge(EDGE - SUB))
    pl.when(jnp.logical_not(has_after))(lambda: zero_edge(EDGE + all_rows))

    def clear_rim(at):
        for s in range(1, all_slices + 1):
            smooth[s, 0, at : at + SUB] = zero

    def clear_rims():
        pl.when(jnp.logical_not(has_before))(lambda: clear_rim(0))
        pl.when(jnp.logical_not(has_after))(lambda: clear_rim(SUB + all_rows))

    if pairs == 1:
        clear_rims()

    loads[3].wait()
    loads[4].wait()
    tables = [zero for _ in range(4)]
    for n in range(extinction.shape[0]):
        tables[0] = jnp.where(lane == n, extinction[n], tables[0])
        for c in range(3):
            tables[c + 1] = jnp.where(lane == n, albedo[c, n], tables[c + 1])


    for part in range(2):
        first_j = 0 if part == 0 else GROUP - 1
        for m in range(GROUP):

            @pl.when(flip(j, m) != first_j)
            def _():
                for e in range(PAIR):
                    wait_brick(m, e, part)

    for n, exists in ((1, has_below), (0, has_above)):

        @pl.when(exists)
        def _():
            halos[n][0].wait_recv()
            halos[n][1].wait_recv()

    for b in (0, GROUP + 1):
        unpack(b, 0)

    edges = []
    if pairs > 1:
        for n, (step, source, target, exists) in enumerate(
            ((-PAIR, EDGE, EDGE + all_rows, has_before), (PAIR, EDGE + all_rows - SUB, EDGE - SUB, has_after))
        ):
            edges.append((
                remote(
                    volume.at[:, :, pl.ds(source, SUB)], volume.at[:, :, pl.ds(target, SUB)],
                    edge_send.at[n], edge_recv.at[n], d, light + step,
                ),
                exists,
            ))
        for one, exists in edges:
            pl.when(exists)(one.start)

    if pairs > 1:
        for n, exists in ((0, has_after), (1, has_before)):
            pl.when(exists)(edges[n][0].wait_recv)
    below = jnp.where(has_below, 1.0, 0.0)
    above = jnp.where(has_above, 1.0, 0.0)
    inside = jnp.where(lane < LANE // 2, jnp.where(q < PARTS - 1, 1.0, 0.0), jnp.where(q > 0, 1.0, 0.0))
    lane_first, lane_last = lane == 0, lane == LANE - 1

    def smooth_tile(g, carry):
        base = pl.multiple_of(EDGE + g * SUB, SUB)
        target = pl.multiple_of(SUB + g * SUB, SUB)
        at = pl.ds(base, SUB)

        def both(z):
            return [volume[z, t, at] for t in range(2)]

        first = slices - 1
        before, center = both(first - 1), both(first)
        for s in range(all_slices + 2):
            z = first + s
            after = both(z + 1)
            for t in range(2 if 0 < s <= all_slices else 1):
                own, other = center[t], center[1 - t]
                low = pltpu.roll(jnp.where(lane_last, other, own), 1, 1)
                high = pltpu.roll(jnp.where(lane_first, other, own), LANE - 1, 1)
                up = volume[z, t, pl.ds(base - 1, SUB)]
                down = volume[z, t, pl.ds(base + 1, SUB)]
                value = 0.4 * own + 0.1 * ((before[t] + after[t]) + (up + down) + (low + high))
                if s == 0:
                    value = value * below
                if s == all_slices + 1:
                    value = value * above
                if t == 1:
                    value = value * inside
                smooth[s, t, pl.ds(target, SUB)] = value
            before, center = center, after
        return carry

    ends = 1 if pairs > 1 else 0
    lax.fori_loop(-ends, all_rows // SUB + ends, smooth_tile, 0)

    if pairs > 1:
        clear_rims()

    def slope_tile(g, carry):
        base = pl.multiple_of(SUB + g * SUB, SUB)
        target = pl.ds(pl.multiple_of(g * SUB, SUB), SUB)
        at = pl.ds(base, SUB)
        before, center = smooth[0, 0, at], smooth[1, 0, at]
        for z in range(all_slices):
            after = smooth[z + 2, 0, at]
            beside = smooth[z + 1, 1, at]
            low = pltpu.roll(jnp.where(lane_last, beside, center), 1, 1)
            high = pltpu.roll(jnp.where(lane_first, beside, center), LANE - 1, 1)
            up = smooth[z + 1, 0, pl.ds(base - 1, SUB)]
            down = smooth[z + 1, 0, pl.ds(base + 1, SUB)]
            grad_z, grad_x, grad_y = after - before, down - up, high - low
            facing = grad_x * lax.rsqrt(grad_z * grad_z + grad_x * grad_x + grad_y * grad_y + 0.2)
            heat[z, target] = jnp.exp(center)
            turned[z, target] = 0.5 + 0.5 * facing
            before, center = center, after
        return carry

    lax.fori_loop(0, all_rows // SUB, slope_tile, 0)

    def unit_copy(u):
        return remote(
            parts_out.at[pl.ds(GROUP * u, GROUP)], parts_mid.at[u // groups, k],
            mid_send.at[u], mid_recv.at[u // groups], GROUP * (u % groups) + j, light,
        )

    def send_unit(u):
        @pl.when(u % groups != k)
        def _():
            unit_copy(u).start()

        @pl.when(u % groups == k)
        def _():
            pltpu.make_async_copy(
                parts_out.at[pl.ds(GROUP * u, GROUP)], parts_mid.at[u // groups, k], mid_recv.at[u // groups]
            ).start()

    def owned_here(u, i):
        return (u % groups == k) & (u // groups == l) & (j == i)

    def owner_copy(source, target, send, recv, u, i):
        return remote(source, target, send, recv, GROUP * (u % groups) + i, PAIR * p + u // groups)

    def send_owner(source, target, send, recv, u, i):
        own = owned_here(u, i)

        @pl.when(jnp.logical_not(own))
        def _():
            owner_copy(source, target, send, recv, u, i).start()

        @pl.when(own)
        def _():
            pltpu.make_async_copy(source, target, recv).start()

    def direct_parts(u, i):
        send = direct_send.at[u - direct_from, i]
        return parts_out.at[GROUP * u + i], direct_last.at[k, q], send, direct_recv, u, i

    def merged_parts(to_l, i):
        send = last_send.at[to_l, i]
        return parts_merged.at[to_l, i], parts_last.at[q], send, last_recv, to_l * groups + k, i

    paired = 2 * block_rows == SUB
    top = sub < SUB // 2

    def turn(value):
        return pltpu.roll(value, SUB // 2, 0)

    def fetch(ref, at):
        if paired:
            return [ref[at + (pl.ds(SUB * n, SUB),)] for n in range(2)]
        return [ref[at + (pl.ds(block_rows * c, block_rows),)] for c in range(4)]

    def keep(ref, at, values):
        size = SUB if paired else block_rows
        for n, value in enumerate(values):
            ref[at + (pl.ds(size * n, size),)] = value

    def over(fronts):
        back = fronts[-1]
        for front in reversed(fronts[:-1]):
            shade = jnp.where(top, turn(front[-1]), front[-1]) if paired else front[-1]
            clear = 1.0 - shade
            back = [one + clear * other for one, other in zip(front, back)]
        return back

    per_tile = SUB // block_rows

    def shade_tile(g, lights):
        at = pl.ds(pl.multiple_of(g * SUB, SUB), SUB)
        spot = pl.ds(pl.multiple_of(g % chunk_tiles * SUB, SUB), SUB)
        lights = list(lights)
        remaining = jnp.ones((SUB, LANE), jnp.float32)
        colours = [zero] * 3
        for z in range(all_slices):
            index = materials[g // chunk_tiles, z, spot]
            passed = jnp.exp(-(lookup(tables[0], index) * heat[z, at]))
            ahead = jnp.where(sub >= 1, pltpu.roll(passed, 1, 0), lights[z])
            for step in (1, 2, 4):
                ahead = ahead * jnp.where(sub >= step, pltpu.roll(ahead, step, 0), 1.0)
            lights[z] = jnp.broadcast_to((ahead * passed)[SUB - 1 :], (SUB, LANE))
            weight = (1.0 - passed) * remaining * (0.2 + ahead * turned[z, at])
            for c in range(3):
                colours[c] = colours[c] + lookup(tables[c + 1], index) * weight
            remaining = remaining * passed
        values = colours + [1.0 - remaining]
        for b in range(per_tile):
            if paired and b == 0:
                block = [jnp.where(top, values[n], turn(values[n + 1])) for n in (0, 2)]
            elif paired:
                block = [jnp.where(top, turn(values[n]), values[n + 1]) for n in (0, 2)]
            else:
                block = [value[b * block_rows : (b + 1) * block_rows] for value in values]
            keep(parts_out, (g * per_tile + b,), block)
        return tuple(lights)

    lights = (jnp.ones((SUB, LANE), jnp.float32),) * all_slices
    if pairs > 1:
        light_copy = remote(lights_out, lights_in, light_send, light_recv, d, light + PAIR)

        @pl.when(has_before)
        def _():
            light_copy.wait_recv()

        @pl.when(jnp.logical_not(has_before))
        def _():
            for z in range(all_slices):
                lights_in[z] = jnp.ones((SUB, LANE), jnp.float32)

        lights = tuple(lights_in[z] for z in range(all_slices))

    if reaches:
        wait_far(len(reaches) - 1, reaches[-1])
    own_labels.wait()

    def shade_wait(g, n, lights):
        if n % chunk_tiles == 0:
            for m in ORDER:
                label_copy(g // chunk_tiles, m).wait_recv()
        return shade_tile(g, lights)

    def merged_step(step, lights):
        for n in range(step_tiles):
            lights = shade_wait(step * step_tiles + n, n, lights)
        for n in range(step_units):
            send_unit(step * step_units + n)
        return lights

    def direct_step(step, lights):
        for n in range(step_tiles):
            g = step * step_tiles + n
            lights = shade_wait(g, n, lights)
            for b in range(per_tile):
                block = g * per_tile + b
                send_owner(*direct_parts(block // GROUP, block % GROUP))
        return lights

    def bytes_of(ref, sem):
        pltpu.make_async_copy(ref, ref, sem).wait()

    def merge(to_l):
        bytes_of(parts_mid.at[to_l], mid_recv.at[to_l])
        for i in range(GROUP):
            keep(parts_merged, (to_l, i), over([fetch(parts_mid, (to_l, front, i)) for front in range(groups)]))
        for i in range(GROUP):
            send_owner(*merged_parts(to_l, i))

    def merges_far(to_l):
        return to_l * groups + k < direct_from

    lights = lax.fori_loop(0, merged_steps, merged_step, lights)
    lights = lax.fori_loop(merged_steps, merge_at, direct_step, lights)
    merge(0)
    lights = lax.fori_loop(merge_at, all_rows // step_rows, direct_step, lights)
    if pairs > 1:
        for z in range(all_slices):
            lights_out[z] = lights[z]
        pl.when(has_after)(light_copy.start)

    for part in range(2):
        for m, e in every:
            if (m, e) != (0, 0):
                brick_copy(m, e, part).wait_send()
    for m, e in every:
        if (m, e) != (0, 0):
            strip_copy(m, e).wait_send()
    mate_labels.wait_send()
    for (bulk, thin), exists in zip(halos, (has_below, has_above)):

        @pl.when(exists)
        def _():
            bulk.wait_send()
            thin.wait_send()

    def sent_labels(c, carry):
        for m in ORDER:
            label_copy(c, m).wait_send()
        return carry

    lax.fori_loop(0, chunks, sent_labels, 0)

    def sent_unit(u, carry):
        @pl.when(u % groups != k)
        def _():
            unit_copy(u).wait_send()

        return carry

    lax.fori_loop(0, direct_from, sent_unit, 0)

    def sent_direct(u, carry):
        for i in range(GROUP):

            @pl.when(jnp.logical_not(owned_here(u, i)))
            def _():
                owner_copy(*direct_parts(u, i)).wait_send()

        return carry

    lax.fori_loop(direct_from, units, sent_direct, 0)
    for to_l in range(PAIR):
        for i in range(GROUP):

            @pl.when(merges_far(to_l) & jnp.logical_not(owned_here(to_l * groups + k, i)))
            def _():
                owner_copy(*merged_parts(to_l, i)).wait_send()

    for one, exists in edges:
        pl.when(exists)(one.wait_send)
    if pairs > 1:
        pl.when(has_after)(light_copy.wait_send)

    own_far = l * groups + k < direct_from

    @pl.when(own_far)
    def _():
        bytes_of(parts_last, last_recv)
        for n in range(PARTS):
            keep(blended, (n,), fetch(parts_last, (n,)))

    @pl.when(jnp.logical_not(own_far))
    def _():
        bytes_of(direct_last, direct_recv)
        for n in range(PARTS):
            keep(blended, (n,), over([fetch(direct_last, (front, n)) for front in range(groups)]))

    for n in range(PARTS):
        for r in range(block_rows):
            at = r * PARTS * LANE + n * LANE
            out[:, at : at + LANE] = blended[n, pl.ds(r, 4, stride=block_rows), :]


def shards(density, labels, slice_order, extinction, albedo):
    depth_count = lax.axis_size("depth")
    light_count = lax.axis_size("light")
    slices, rows, columns = density.shape
    groups = depth_count // GROUP
    block_rows = rows // depth_count
    all_rows, all_slices = PAIR * rows, GROUP * slices
    units = PAIR * groups
    chunk_rows = CHUNK_TILES * SUB
    chunks = all_rows // chunk_rows
    f32, i32 = jnp.float32, jnp.int32
    vmem, smem, dma = pltpu.VMEM, pltpu.SMEM, pltpu.SemaphoreType.DMA
    scratch = [
        vmem(density.shape, f32),
        vmem(labels.shape, i32),
        smem(slice_order.shape, i32),
        smem(extinction.shape, f32),
        smem(albedo.shape, f32),
        vmem((PARTS, slices, rows, LANE), f32),
        vmem((PARTS, SUB, LANE), f32),
        vmem((PAIR, GROUP, chunks // PAIR, slices, chunk_rows, LANE), i32),
        vmem((GROUP, chunks, slices, chunk_rows, LANE), i32),
        vmem((all_slices + 2 * slices, 2, all_rows + 2 * EDGE, LANE), f32),
        vmem((GROUP + 2, PAIR, SUB, LANE), f32),
        vmem((chunks, all_slices, chunk_rows, LANE), i32),
        vmem((all_slices + 2, 2, all_rows + 2 * SUB, LANE), f32),
        vmem((all_slices, all_rows, LANE), f32),
        vmem((all_slices, all_rows, LANE), f32),
        vmem((PAIR * depth_count, 4 * block_rows, LANE), f32),
        vmem((PAIR, groups, GROUP, 4 * block_rows, LANE), f32),
        vmem((PAIR, GROUP, 4 * block_rows, LANE), f32),
        vmem((PARTS, 4 * block_rows, LANE), f32),
        vmem((groups, PARTS, 4 * block_rows, LANE), f32),
        vmem((PARTS, SUB * block_rows, LANE), f32),
        vmem((all_slices, SUB, LANE), f32),
        vmem((all_slices, SUB, LANE), f32),
        dma((5,)),
        dma((2, PARTS)),
        dma((2, PARTS)),
        dma((PARTS,)),
        dma((PARTS,)),
        dma((3,)),
        dma((chunks, GROUP - 1)),
        dma((chunks, GROUP - 1)),
        dma((4,)),
        dma((4,)),
        dma((2,)),
        dma((2,)),
        dma(()),
        dma(()),
        pltpu.SemaphoreType.REGULAR((max(1, len(far_reaches(groups))),)),
        dma((units,)),
        dma((PAIR,)),
        dma((PAIR, GROUP)),
        dma(()),
        dma((units, GROUP)),
        dma(()),
    ]
    image = pl.pallas_call(
        functools.partial(render_kernel, depth_count, light_count),
        in_specs=[FAR] * 5,
        out_specs=pl.BlockSpec(memory_space=pltpu.VMEM),
        out_shape=jax.ShapeDtypeStruct((4, block_rows * columns), f32),
        scratch_shapes=scratch,
        compiler_params=pltpu.CompilerParams(
            collective_id=0, has_side_effects=True, vmem_limit_bytes=40 * 1024 * 1024
        ),
    )(*(pltpu.with_memory_space_constraint(one, pltpu.HBM) for one in (density, labels, slice_order, extinction, albedo)))
    return image


def solution(mesh):
    return jax.shard_map(
        shards,
        mesh=mesh,
        in_specs=(P("depth", "light", None), P("depth", "light", None), P("depth"), P(), P()),
        out_specs=P(None, ("light", "depth")),
        check_vma=False,
    )
```

```python
import functools

import jax
import jax.numpy as jnp
from jax import lax
from jax.experimental import pallas as pl
from jax.experimental.pallas import tpu as pltpu
from jax.sharding import PartitionSpec as P

SUB, LANE = 8, 128
GROUP, PAIR = 4, 2
PARTS = GROUP * PAIR
CHUNK_TILES = 2
MERGE_AFTER = 12
EDGE = 2 * SUB
MESH = pl.DeviceIdType.MESH
FAR = pl.BlockSpec(memory_space=pltpu.HBM)
ORDER = (3, 1, 2)


def flip(value, mask):
    for bit in (1, 2):
        if mask & bit:
            value = value + bit * (1 - 2 * ((value // bit) % 2))
    return value


def far_reaches(groups):
    reaches, known = [], 1
    while known < groups - 1:
        reaches.append(known)
        known *= 2
    return reaches


def lookup(table, index):
    return jnp.take_along_axis(table, index, axis=1, mode="promise_in_bounds")


def render_kernel(
    depth_count, light_count,
    density_far, labels_far, order_far, extinction_far, albedo_far,
    out,
    density, labels, order, extinction, albedo,
    bricks, strips, labels_out, column_labels, volume, halo_strips, materials,
    smooth, heat, turned, parts_out, parts_mid, parts_merged, parts_last, direct_last, blended, lights_in, lights_out,
    load_sem, brick_send, brick_recv, strip_send, strip_recv, mate_sem, label_send, label_recv,
    halo_send, halo_recv, edge_send, edge_recv, light_send, light_recv, ready_sem,
    mid_send, mid_recv, last_send, last_recv, direct_send, direct_recv,
):
    slices, rows = density.shape[:2]
    half = slices // 2
    groups, pairs = depth_count // GROUP, light_count // PAIR
    all_rows, all_slices = PAIR * rows, GROUP * slices
    block_rows = rows // depth_count
    row_tiles = rows // SUB
    unit_rows = GROUP * block_rows
    units = PAIR * groups
    chunk_tiles = CHUNK_TILES
    chunk_rows = chunk_tiles * SUB
    chunks = all_rows // chunk_rows
    step_rows = max(chunk_rows, unit_rows)
    step_units, step_tiles = step_rows // unit_rows, step_rows // SUB
    direct_from = units // 2
    merged_steps = direct_from // step_units
    merge_at = min(MERGE_AFTER // step_tiles, all_rows // step_rows)
    d = lax.axis_index("depth")
    light = lax.axis_index("light")
    k, j = d // GROUP, d % GROUP
    p, l = light // PAIR, light % PAIR
    q = PAIR * j + l
    has_below, has_above = k > 0, k < groups - 1
    has_before, has_after = p > 0, p < pairs - 1
    lane = lax.broadcasted_iota(jnp.int32, (SUB, LANE), 1)
    sub = lax.broadcasted_iota(jnp.int32, (SUB, LANE), 0)
    zero = jnp.zeros((SUB, LANE), jnp.float32)

    barrier = pltpu.get_barrier_semaphore()

    for m in range(GROUP):
        for e in range(PAIR):
            if (m, e) != (0, 0):
                mate = (GROUP * k + flip(j, m), PAIR * p + (l if e == 0 else 1 - l))
                pl.semaphore_signal(barrier, inc=1, device_id=mate, device_id_type=MESH)
    greeted = PARTS - 1
    for exists, step in ((has_below, -GROUP), (has_above, GROUP)):

        @pl.when(exists)
        def _():
            pl.semaphore_signal(barrier, inc=1, device_id=(d + step, light), device_id_type=MESH)

        greeted = greeted + jnp.where(exists, 1, 0)
    if pairs > 1:
        for exists, step in ((has_before, -PAIR), (has_after, PAIR)):

            @pl.when(exists)
            def _():
                pl.semaphore_signal(barrier, inc=1, device_id=(d, light + step), device_id_type=MESH)

            greeted = greeted + jnp.where(exists, 1, 0)

    loads = [
        pltpu.make_async_copy(source, target, load_sem.at[n])
        for n, (source, target) in enumerate(
            ((order_far, order), (density_far, density), (labels_far, labels), (extinction_far, extinction), (albedo_far, albedo))
        )
    ]
    for one in loads:
        one.start()

    def remote(source, target, send, recv, depth, to_light):
        return pltpu.make_async_remote_copy(
            src_ref=source, dst_ref=target, send_sem=send, recv_sem=recv,
            device_id=(depth, to_light), device_id_type=MESH,
        )

    loads[0].wait()
    loads[1].wait()

    def pack_bricks(part):
        for z in range(half):
            z = half * part + z
            at = lax.rem(order[z], slices)
            for g in range(row_tiles):
                for t in range(PARTS):
                    tile = density[at, g * SUB : (g + 1) * SUB, t * LANE : (t + 1) * LANE]
                    bricks[t, z, g * SUB : (g + 1) * SUB, :] = tile

    pack_bricks(jnp.where(j == GROUP - 1, 1, 0))

    def brick_spot(from_j, from_l, part):
        return volume.at[
            pl.ds(slices + slices * from_j + half * part, half), 0, pl.ds(EDGE + rows * from_l, rows)
        ]

    def brick_copy(m, e, part):
        to_q = PAIR * flip(j, m) + (l if e == 0 else 1 - l)
        source = bricks.at[to_q, pl.ds(half * part, half)]
        slot = PAIR * m + e
        if slot == 0:
            return pltpu.make_async_copy(source, brick_spot(j, l, part), brick_recv.at[part, 0])
        return remote(
            source, brick_spot(j, l, part), brick_send.at[part, slot], brick_recv.at[part, slot],
            GROUP * k + flip(j, m), PAIR * p + to_q % PAIR,
        )

    def strip_copy(m, e):
        to_q = PAIR * flip(j, m) + (l if e == 0 else 1 - l)
        target = halo_strips.at[1 + j, l]
        slot = PAIR * m + e
        if slot == 0:
            return pltpu.make_async_copy(strips.at[to_q], target, strip_recv.at[0])
        return remote(
            strips.at[to_q], target, strip_send.at[slot], strip_recv.at[slot],
            GROUP * k + flip(j, m), PAIR * p + to_q % PAIR,
        )

    every = [(m, e) for m in ORDER + (0,) for e in range(PAIR)]
    early = jnp.where(j == GROUP - 1, 1, 0)
    pl.semaphore_wait(barrier, greeted)
    for m, e in every:
        brick_copy(m, e, early).start()
    pack_bricks(1 - early)

    def pack_strips(z, packed):
        packed = list(packed)
        for g in range(row_tiles):
            i = z * row_tiles + g
            rows_at = slice(g * SUB, (g + 1) * SUB)
            for t in range(PARTS):
                left = bricks[t - 1, z, rows_at, :] if t > 0 else zero
                right = bricks[t + 1, z, rows_at, :] if t < PARTS - 1 else zero
                rims = pltpu.roll(jnp.where(lane < LANE // 2, right, left), lax.rem(4 * i + 2, LANE), 1)
                packed[t] = jnp.where(lane // 4 == i, rims, packed[t])
        return tuple(packed)

    packed = lax.fori_loop(0, slices, pack_strips, (zero,) * PARTS)
    for t in range(PARTS):
        strips[t] = packed[t]
    for m, e in every:
        strip_copy(m, e).start()
    for m, e in every:
        brick_copy(m, e, 1 - early).start()

    @pl.when(jnp.logical_not(has_below))
    def _():
        volume[half : slices, 0] = jnp.zeros((half,) + volume.shape[2:], jnp.float32)
        halo_strips[0] = jnp.zeros(halo_strips.shape[1:], jnp.float32)

    @pl.when(jnp.logical_not(has_above))
    def _():
        volume[slices + all_slices : slices + all_slices + half, 0] = jnp.zeros((half,) + volume.shape[2:], jnp.float32)
        halo_strips[GROUP + 1] = jnp.zeros(halo_strips.shape[1:], jnp.float32)


    def signal_far(number, reach):
        for exists, step in ((k >= reach, -reach), (k + reach < groups, reach)):

            @pl.when(exists)
            def _():
                pl.semaphore_signal(
                    ready_sem.at[number], inc=1, device_id=(d + GROUP * step, light), device_id_type=MESH
                )

    def wait_far(number, reach):
        count = jnp.where(k >= reach, 1, 0) + jnp.where(k + reach < groups, 1, 0)
        pl.semaphore_wait(ready_sem.at[number], count)

    reaches = far_reaches(groups)
    if reaches:
        signal_far(0, reaches[0])

    loads[2].wait()

    def pack_labels(i, carry):
        z, g = i // row_tiles, i % row_tiles
        at = lax.rem(order[z], slices)
        base = pl.multiple_of(g * SUB, SUB)
        spot = pl.multiple_of(g % chunk_tiles * SUB, SUB)
        for t in range(PARTS):
            labels_out[t % PAIR, t // PAIR, g // chunk_tiles, z, pl.ds(spot, SUB), :] = labels[at, pl.ds(base, SUB), t * LANE : (t + 1) * LANE]
        return carry

    lax.fori_loop(0, slices * row_tiles, pack_labels, 0)
    own_rows = column_labels.at[:, pl.ds(chunks // PAIR * l, chunks // PAIR)]
    keep_labels = pltpu.make_async_copy(labels_out.at[l], own_rows, mate_sem.at[0])
    mate_labels = remote(labels_out.at[1 - l], own_rows, mate_sem.at[1], mate_sem.at[2], d, PAIR * p + 1 - l)
    keep_labels.start()
    mate_labels.start()

    def wait_brick(m, e, part):
        to_q = PAIR * flip(j, m) + (l if e == 0 else 1 - l)
        if isinstance(m, int) and PAIR * m + e == 0:
            brick_copy(0, 0, part).wait()
        else:
            spot = brick_spot(flip(j, m), to_q % PAIR, part)
            remote(spot, spot, brick_send.at[part, PAIR * m + e], brick_recv.at[part, PAIR * m + e], d, light).wait_recv()

    def wait_strip(m, e):
        if PAIR * m + e == 0:
            strip_copy(0, 0).wait()
        else:
            strip_copy(m, e).wait_recv()

    halos = []
    for n, (step, own, part, target) in enumerate(
        ((-1, 0, 0, slices + all_slices), (1, GROUP - 1, 1, half))
    ):
        start = slices + slices * own + half * part
        depth = d + GROUP * step
        strip_target = GROUP + 1 if step < 0 else 0
        halos.append((
            remote(
                volume.at[pl.ds(start, half), 0, pl.ds(EDGE, all_rows)],
                volume.at[pl.ds(target, half), 0, pl.ds(EDGE, all_rows)],
                halo_send.at[n], halo_recv.at[n], depth, light,
            ),
            remote(halo_strips.at[1 + own], halo_strips.at[strip_target], halo_send.at[2 + n], halo_recv.at[2 + n], depth, light),
        ))
    for part in range(2):
        first_j = 0 if part == 0 else GROUP - 1
        for m in range(GROUP):

            @pl.when(flip(j, m) == first_j)
            def _():
                for e in range(PAIR):
                    wait_brick(m, e, part)

    for (bulk, thin), exists in zip(halos, (has_below, has_above)):
        pl.when(exists)(bulk.start)
    for number in range(len(reaches) - 1):
        wait_far(number, reaches[number])
        signal_far(number + 1, reaches[number + 1])

    keep_labels.wait()
    mate_labels.wait_recv()
    def label_copy(c, m):
        return remote(
            column_labels.at[flip(j, m), c], materials.at[c, pl.ds(slices * j, slices)],
            label_send.at[c, m - 1], label_recv.at[c, m - 1], GROUP * k + flip(j, m), light,
        )

    def send_labels(c, carry):
        for m in ORDER:
            label_copy(c, m).start()
        return carry

    lax.fori_loop(0, chunks, send_labels, 0)
    own_labels = pltpu.make_async_copy(column_labels.at[j], materials.at[:, pl.ds(slices * j, slices)], mate_sem.at[0])
    own_labels.start()
    for m, e in every:
        wait_strip(m, e)
    for (bulk, thin), exists in zip(halos, (has_below, has_above)):
        pl.when(exists)(thin.start)

    def unpack(b, carry):
        for l_from in range(PAIR):
            strip = halo_strips[b, l_from]
            for z in range(slices):
                for g in range(row_tiles):
                    i = z * row_tiles + g
                    at = EDGE + rows * l_from + SUB * g
                    volume[slices * b + z, 1, at : at + SUB] = pltpu.roll(strip, (2 * LANE - 4 * i - 2) % LANE, 1)
        return carry

    lax.fori_loop(1, GROUP + 1, unpack, 0)

    def zero_edge(at):
        for t in range(2):
            for z in range(half, all_slices + slices + half):
                volume[z, t, at : at + SUB] = zero

    pl.when(jnp.logical_not(has_before))(lambda: zero_edge(EDGE - SUB))
    pl.when(jnp.logical_not(has_after))(lambda: zero_edge(EDGE + all_rows))

    def clear_rim(at):
        for s in range(1, all_slices + 1):
            smooth[s, 0, at : at + SUB] = zero

    def clear_rims():
        pl.when(jnp.logical_not(has_before))(lambda: clear_rim(0))
        pl.when(jnp.logical_not(has_after))(lambda: clear_rim(SUB + all_rows))

    if pairs == 1:
        clear_rims()

    loads[3].wait()
    loads[4].wait()
    tables = [zero for _ in range(4)]
    for n in range(extinction.shape[0]):
        tables[0] = jnp.where(lane == n, extinction[n], tables[0])
        for c in range(3):
            tables[c + 1] = jnp.where(lane == n, albedo[c, n], tables[c + 1])


    for part in range(2):
        first_j = 0 if part == 0 else GROUP - 1
        for m in range(GROUP):

            @pl.when(flip(j, m) != first_j)
            def _():
                for e in range(PAIR):
                    wait_brick(m, e, part)

    for n, exists in ((1, has_below), (0, has_above)):

        @pl.when(exists)
        def _():
            halos[n][0].wait_recv()
            halos[n][1].wait_recv()

    for b in (0, GROUP + 1):
        unpack(b, 0)

    edges = []
    if pairs > 1:
        for n, (step, source, target, exists) in enumerate(
            ((-PAIR, EDGE, EDGE + all_rows, has_before), (PAIR, EDGE + all_rows - SUB, EDGE - SUB, has_after))
        ):
            edges.append((
                remote(
                    volume.at[:, :, pl.ds(source, SUB)], volume.at[:, :, pl.ds(target, SUB)],
                    edge_send.at[n], edge_recv.at[n], d, light + step,
                ),
                exists,
            ))
        for one, exists in edges:
            pl.when(exists)(one.start)

    if pairs > 1:
        for n, exists in ((0, has_after), (1, has_before)):
            pl.when(exists)(edges[n][0].wait_recv)
    below = jnp.where(has_below, 1.0, 0.0)
    above = jnp.where(has_above, 1.0, 0.0)
    inside = jnp.where(lane < LANE // 2, jnp.where(q < PARTS - 1, 1.0, 0.0), jnp.where(q > 0, 1.0, 0.0))
    lane_first, lane_last = lane == 0, lane == LANE - 1

    def smooth_tile(g, carry):
        base = pl.multiple_of(EDGE + g * SUB, SUB)
        target = pl.multiple_of(SUB + g * SUB, SUB)
        at = pl.ds(base, SUB)

        def both(z):
            return [volume[z, t, at] for t in range(2)]

        first = slices - 1
        before, center = both(first - 1), both(first)
        for s in range(all_slices + 2):
            z = first + s
            after = both(z + 1)
            for t in range(2 if 0 < s <= all_slices else 1):
                own, other = center[t], center[1 - t]
                low = pltpu.roll(jnp.where(lane_last, other, own), 1, 1)
                high = pltpu.roll(jnp.where(lane_first, other, own), LANE - 1, 1)
                up = volume[z, t, pl.ds(base - 1, SUB)]
                down = volume[z, t, pl.ds(base + 1, SUB)]
                value = 0.4 * own + 0.1 * ((before[t] + after[t]) + (up + down) + (low + high))
                if s == 0:
                    value = value * below
                if s == all_slices + 1:
                    value = value * above
                if t == 1:
                    value = value * inside
                smooth[s, t, pl.ds(target, SUB)] = value
            before, center = center, after
        return carry

    ends = 1 if pairs > 1 else 0
    lax.fori_loop(-ends, all_rows // SUB + ends, smooth_tile, 0)

    if pairs > 1:
        clear_rims()

    def slope_tile(g, carry):
        base = pl.multiple_of(SUB + g * SUB, SUB)
        target = pl.ds(pl.multiple_of(g * SUB, SUB), SUB)
        at = pl.ds(base, SUB)
        before, center = smooth[0, 0, at], smooth[1, 0, at]
        for z in range(all_slices):
            after = smooth[z + 2, 0, at]
            beside = smooth[z + 1, 1, at]
            low = pltpu.roll(jnp.where(lane_last, beside, center), 1, 1)
            high = pltpu.roll(jnp.where(lane_first, beside, center), LANE - 1, 1)
            up = smooth[z + 1, 0, pl.ds(base - 1, SUB)]
            down = smooth[z + 1, 0, pl.ds(base + 1, SUB)]
            grad_z, grad_x, grad_y = after - before, down - up, high - low
            facing = grad_x * lax.rsqrt(grad_z * grad_z + grad_x * grad_x + grad_y * grad_y + 0.2)
            heat[z, target] = jnp.exp(center)
            turned[z, target] = 0.5 + 0.5 * facing
            before, center = center, after
        return carry

    lax.fori_loop(0, all_rows // SUB, slope_tile, 0)

    def unit_copy(u):
        return remote(
            parts_out.at[pl.ds(GROUP * u, GROUP)], parts_mid.at[u // groups, k],
            mid_send.at[u], mid_recv.at[u // groups], GROUP * (u % groups) + j, light,
        )

    def send_unit(u):
        @pl.when(u % groups != k)
        def _():
            unit_copy(u).start()

        @pl.when(u % groups == k)
        def _():
            pltpu.make_async_copy(
                parts_out.at[pl.ds(GROUP * u, GROUP)], parts_mid.at[u // groups, k], mid_recv.at[u // groups]
            ).start()

    def owned_here(u, i):
        return (u % groups == k) & (u // groups == l) & (j == i)

    def owner_copy(source, target, send, recv, u, i):
        return remote(source, target, send, recv, GROUP * (u % groups) + i, PAIR * p + u // groups)

    def send_owner(source, target, send, recv, u, i):
        own = owned_here(u, i)

        @pl.when(jnp.logical_not(own))
        def _():
            owner_copy(source, target, send, recv, u, i).start()

        @pl.when(own)
        def _():
            pltpu.make_async_copy(source, target, recv).start()

    def direct_parts(u, i):
        send = direct_send.at[u - direct_from, i]
        return parts_out.at[GROUP * u + i], direct_last.at[k, q], send, direct_recv, u, i

    def merged_parts(to_l, i):
        send = last_send.at[to_l, i]
        return parts_merged.at[to_l, i], parts_last.at[q], send, last_recv, to_l * groups + k, i

    paired = 2 * block_rows == SUB
    top = sub < SUB // 2

    def turn(value):
        return pltpu.roll(value, SUB // 2, 0)

    def fetch(ref, at):
        if paired:
            return [ref[at + (pl.ds(SUB * n, SUB),)] for n in range(2)]
        return [ref[at + (pl.ds(block_rows * c, block_rows),)] for c in range(4)]

    def keep(ref, at, values):
        size = SUB if paired else block_rows
        for n, value in enumerate(values):
            ref[at + (pl.ds(size * n, size),)] = value

    def over(fronts):
        back = fronts[-1]
        for front in reversed(fronts[:-1]):
            shade = jnp.where(top, turn(front[-1]), front[-1]) if paired else front[-1]
            clear = 1.0 - shade
            back = [one + clear * other for one, other in zip(front, back)]
        return back

    per_tile = SUB // block_rows

    def shade_tile(g, lights):
        at = pl.ds(pl.multiple_of(g * SUB, SUB), SUB)
        spot = pl.ds(pl.multiple_of(g % chunk_tiles * SUB, SUB), SUB)
        lights = list(lights)
        remaining = jnp.ones((SUB, LANE), jnp.float32)
        colours = [zero] * 3
        for z in range(all_slices):
            index = materials[g // chunk_tiles, z, spot]
            passed = jnp.exp(-(lookup(tables[0], index) * heat[z, at]))
            ahead = jnp.where(sub >= 1, pltpu.roll(passed, 1, 0), lights[z])
            for step in (1, 2, 4):
                ahead = ahead * jnp.where(sub >= step, pltpu.roll(ahead, step, 0), 1.0)
            lights[z] = jnp.broadcast_to((ahead * passed)[SUB - 1 :], (SUB, LANE))
            weight = (1.0 - passed) * remaining * (0.2 + ahead * turned[z, at])
            for c in range(3):
                colours[c] = colours[c] + lookup(tables[c + 1], index) * weight
            remaining = remaining * passed
        values = colours + [1.0 - remaining]
        for b in range(per_tile):
            if paired and b == 0:
                block = [jnp.where(top, values[n], turn(values[n + 1])) for n in (0, 2)]
            elif paired:
                block = [jnp.where(top, turn(values[n]), values[n + 1]) for n in (0, 2)]
            else:
                block = [value[b * block_rows : (b + 1) * block_rows] for value in values]
            keep(parts_out, (g * per_tile + b,), block)
        return tuple(lights)

    lights = (jnp.ones((SUB, LANE), jnp.float32),) * all_slices
    if pairs > 1:
        light_copy = remote(lights_out, lights_in, light_send, light_recv, d, light + PAIR)

        @pl.when(has_before)
        def _():
            light_copy.wait_recv()

        @pl.when(jnp.logical_not(has_before))
        def _():
            for z in range(all_slices):
                lights_in[z] = jnp.ones((SUB, LANE), jnp.float32)

        lights = tuple(lights_in[z] for z in range(all_slices))

    if reaches:
        wait_far(len(reaches) - 1, reaches[-1])
    own_labels.wait()

    def shade_wait(g, n, lights):
        if n % chunk_tiles == 0:
            for m in ORDER:
                label_copy(g // chunk_tiles, m).wait_recv()
        return shade_tile(g, lights)

    def merged_step(step, lights):
        for n in range(step_tiles):
            lights = shade_wait(step * step_tiles + n, n, lights)
        for n in range(step_units):
            send_unit(step * step_units + n)
        return lights

    def direct_step(step, lights):
        for n in range(step_tiles):
            g = step * step_tiles + n
            lights = shade_wait(g, n, lights)
            for b in range(per_tile):
                block = g * per_tile + b
                send_owner(*direct_parts(block // GROUP, block % GROUP))
        return lights

    def bytes_of(ref, sem):
        pltpu.make_async_copy(ref, ref, sem).wait()

    def merge(to_l):
        bytes_of(parts_mid.at[to_l], mid_recv.at[to_l])
        for i in range(GROUP):
            keep(parts_merged, (to_l, i), over([fetch(parts_mid, (to_l, front, i)) for front in range(groups)]))
        for i in range(GROUP):
            send_owner(*merged_parts(to_l, i))

    def merges_far(to_l):
        return to_l * groups + k < direct_from

    lights = lax.fori_loop(0, merged_steps, merged_step, lights)
    lights = lax.fori_loop(merged_steps, merge_at, direct_step, lights)
    merge(0)
    lights = lax.fori_loop(merge_at, all_rows // step_rows, direct_step, lights)
    if pairs > 1:
        for z in range(all_slices):
            lights_out[z] = lights[z]
        pl.when(has_after)(light_copy.start)

    for part in range(2):
        for m, e in every:
            if (m, e) != (0, 0):
                brick_copy(m, e, part).wait_send()
    for m, e in every:
        if (m, e) != (0, 0):
            strip_copy(m, e).wait_send()
    mate_labels.wait_send()
    for (bulk, thin), exists in zip(halos, (has_below, has_above)):

        @pl.when(exists)
        def _():
            bulk.wait_send()
            thin.wait_send()

    def sent_labels(c, carry):
        for m in ORDER:
            label_copy(c, m).wait_send()
        return carry

    lax.fori_loop(0, chunks, sent_labels, 0)

    def sent_unit(u, carry):
        @pl.when(u % groups != k)
        def _():
            unit_copy(u).wait_send()

        return carry

    lax.fori_loop(0, direct_from, sent_unit, 0)

    def sent_direct(u, carry):
        for i in range(GROUP):

            @pl.when(jnp.logical_not(owned_here(u, i)))
            def _():
                owner_copy(*direct_parts(u, i)).wait_send()

        return carry

    lax.fori_loop(direct_from, units, sent_direct, 0)
    for to_l in range(PAIR):
        for i in range(GROUP):

            @pl.when(merges_far(to_l) & jnp.logical_not(owned_here(to_l * groups + k, i)))
            def _():
                owner_copy(*merged_parts(to_l, i)).wait_send()

    for one, exists in edges:
        pl.when(exists)(one.wait_send)
    if pairs > 1:
        pl.when(has_after)(light_copy.wait_send)

    own_far = l * groups + k < direct_from

    @pl.when(own_far)
    def _():
        bytes_of(parts_last, last_recv)
        for n in range(PARTS):
            keep(blended, (n,), fetch(parts_last, (n,)))

    @pl.when(jnp.logical_not(own_far))
    def _():
        bytes_of(direct_last, direct_recv)
        for n in range(PARTS):
            keep(blended, (n,), over([fetch(direct_last, (front, n)) for front in range(groups)]))

    for n in range(PARTS):
        for r in range(block_rows):
            at = r * PARTS * LANE + n * LANE
            out[:, at : at + LANE] = blended[n, pl.ds(r, 4, stride=block_rows), :]


def shards(density, labels, slice_order, extinction, albedo):
    depth_count = lax.axis_size("depth")
    light_count = lax.axis_size("light")
    slices, rows, columns = density.shape
    groups = depth_count // GROUP
    block_rows = rows // depth_count
    all_rows, all_slices = PAIR * rows, GROUP * slices
    units = PAIR * groups
    chunk_rows = CHUNK_TILES * SUB
    chunks = all_rows // chunk_rows
    f32, i32 = jnp.float32, jnp.int32
    vmem, smem, dma = pltpu.VMEM, pltpu.SMEM, pltpu.SemaphoreType.DMA
    scratch = [
        vmem(density.shape, f32),
        vmem(labels.shape, i32),
        smem(slice_order.shape, i32),
        smem(extinction.shape, f32),
        smem(albedo.shape, f32),
        vmem((PARTS, slices, rows, LANE), f32),
        vmem((PARTS, SUB, LANE), f32),
        vmem((PAIR, GROUP, chunks // PAIR, slices, chunk_rows, LANE), i32),
        vmem((GROUP, chunks, slices, chunk_rows, LANE), i32),
        vmem((all_slices + 2 * slices, 2, all_rows + 2 * EDGE, LANE), f32),
        vmem((GROUP + 2, PAIR, SUB, LANE), f32),
        vmem((chunks, all_slices, chunk_rows, LANE), i32),
        vmem((all_slices + 2, 2, all_rows + 2 * SUB, LANE), f32),
        vmem((all_slices, all_rows, LANE), f32),
        vmem((all_slices, all_rows, LANE), f32),
        vmem((PAIR * depth_count, 4 * block_rows, LANE), f32),
        vmem((PAIR, groups, GROUP, 4 * block_rows, LANE), f32),
        vmem((PAIR, GROUP, 4 * block_rows, LANE), f32),
        vmem((PARTS, 4 * block_rows, LANE), f32),
        vmem((groups, PARTS, 4 * block_rows, LANE), f32),
        vmem((PARTS, SUB * block_rows, LANE), f32),
        vmem((all_slices, SUB, LANE), f32),
        vmem((all_slices, SUB, LANE), f32),
        dma((5,)),
        dma((2, PARTS)),
        dma((2, PARTS)),
        dma((PARTS,)),
        dma((PARTS,)),
        dma((3,)),
        dma((chunks, GROUP - 1)),
        dma((chunks, GROUP - 1)),
        dma((4,)),
        dma((4,)),
        dma((2,)),
        dma((2,)),
        dma(()),
        dma(()),
        pltpu.SemaphoreType.REGULAR((max(1, len(far_reaches(groups))),)),
        dma((units,)),
        dma((PAIR,)),
        dma((PAIR, GROUP)),
        dma(()),
        dma((units, GROUP)),
        dma(()),
    ]
    image = pl.pallas_call(
        functools.partial(render_kernel, depth_count, light_count),
        in_specs=[FAR] * 5,
        out_specs=pl.BlockSpec(memory_space=pltpu.VMEM),
        out_shape=jax.ShapeDtypeStruct((4, block_rows * columns), f32),
        scratch_shapes=scratch,
        compiler_params=pltpu.CompilerParams(
            collective_id=0, has_side_effects=True, vmem_limit_bytes=40 * 1024 * 1024
        ),
    )(*(pltpu.with_memory_space_constraint(one, pltpu.HBM) for one in (density, labels, slice_order, extinction, albedo)))
    return image


def solution(mesh):
    return jax.shard_map(
        shards,
        mesh=mesh,
        in_specs=(P("depth", "light", None), P("depth", "light", None), P("depth"), P(), P()),
        out_specs=P(None, ("light", "depth")),
        check_vma=False,
    )
```

```python
import functools

import jax
import jax.numpy as jnp
from jax import lax
from jax.experimental import pallas as pl
from jax.experimental.pallas import tpu as pltpu
from jax.sharding import PartitionSpec as P

SUB, LANE = 8, 128
GROUP, PAIR = 4, 2
PARTS = GROUP * PAIR
CHUNK_TILES = 2
MERGE_STEP, MERGE_SPREAD = 6, 2
EDGE = 2 * SUB
MESH = pl.DeviceIdType.MESH
FAR = pl.BlockSpec(memory_space=pltpu.HBM)
ORDER = (3, 1, 2)


def flip(value, mask):
    for bit in (1, 2):
        if mask & bit:
            value = value + bit * (1 - 2 * ((value // bit) % 2))
    return value


def far_reaches(groups):
    reaches, known = [], 1
    while known < groups - 1:
        reaches.append(known)
        known *= 2
    return reaches


def lookup(table, index):
    return jnp.take_along_axis(table, index, axis=1, mode="promise_in_bounds")


def render_kernel(
    depth_count, light_count,
    density_far, labels_far, order_far, extinction_far, albedo_far,
    out,
    density, labels, order, extinction, albedo,
    bricks, strips, labels_out, column_labels, volume, halo_strips, materials,
    smooth, heat, turned, parts_out, parts_mid, parts_merged, parts_last, direct_last, blended, lights_in, lights_out,
    load_sem, brick_send, brick_recv, strip_send, strip_recv, mate_sem, label_send, label_recv,
    halo_send, halo_recv, edge_send, edge_recv, light_send, light_recv, ready_sem,
    mid_send, mid_recv, last_send, last_recv, direct_send, direct_recv,
):
    slices, rows = density.shape[:2]
    half = slices // 2
    groups, pairs = depth_count // GROUP, light_count // PAIR
    all_rows, all_slices = PAIR * rows, GROUP * slices
    block_rows = rows // depth_count
    row_tiles = rows // SUB
    unit_rows = GROUP * block_rows
    units = PAIR * groups
    chunk_tiles = CHUNK_TILES
    chunk_rows = chunk_tiles * SUB
    chunks = all_rows // chunk_rows
    step_rows = max(chunk_rows, unit_rows)
    step_units, step_tiles = step_rows // unit_rows, step_rows // SUB
    direct_from = units // 2
    merged_steps = direct_from // step_units
    steps = all_rows // step_rows
    d = lax.axis_index("depth")
    light = lax.axis_index("light")
    k, j = d // GROUP, d % GROUP
    p, l = light // PAIR, light % PAIR
    q = PAIR * j + l
    has_below, has_above = k > 0, k < groups - 1
    merge_step = MERGE_STEP * steps // 8 + (groups - 1 - k) * MERGE_SPREAD * steps // (8 * groups)
    merge_step = jnp.minimum(jnp.maximum(merge_step, merged_steps), steps)
    has_before, has_after = p > 0, p < pairs - 1
    lane = lax.broadcasted_iota(jnp.int32, (SUB, LANE), 1)
    sub = lax.broadcasted_iota(jnp.int32, (SUB, LANE), 0)
    zero = jnp.zeros((SUB, LANE), jnp.float32)

    loads = [
        pltpu.make_async_copy(source, target, load_sem.at[n])
        for n, (source, target) in enumerate(
            ((order_far, order), (density_far, density), (labels_far, labels), (extinction_far, extinction), (albedo_far, albedo))
        )
    ]
    for one in loads:
        one.start()

    barrier = pltpu.get_barrier_semaphore()

    for m in range(GROUP):
        for e in range(PAIR):
            if (m, e) != (0, 0):
                mate = (GROUP * k + flip(j, m), PAIR * p + (l if e == 0 else 1 - l))
                pl.semaphore_signal(barrier, inc=1, device_id=mate, device_id_type=MESH)
    greeted = PARTS - 1
    for exists, step in ((has_below, -GROUP), (has_above, GROUP)):

        @pl.when(exists)
        def _():
            pl.semaphore_signal(barrier, inc=1, device_id=(d + step, light), device_id_type=MESH)

        greeted = greeted + jnp.where(exists, 1, 0)
    if pairs > 1:
        for exists, step in ((has_before, -PAIR), (has_after, PAIR)):

            @pl.when(exists)
            def _():
                pl.semaphore_signal(barrier, inc=1, device_id=(d, light + step), device_id_type=MESH)

            greeted = greeted + jnp.where(exists, 1, 0)

    def remote(source, target, send, recv, depth, to_light):
        return pltpu.make_async_remote_copy(
            src_ref=source, dst_ref=target, send_sem=send, recv_sem=recv,
            device_id=(depth, to_light), device_id_type=MESH,
        )

    loads[0].wait()
    loads[1].wait()

    def pack_bricks(part):
        for z in range(half):
            z = half * part + z
            at = lax.rem(order[z], slices)
            for g in range(row_tiles):
                for t in range(PARTS):
                    tile = density[at, g * SUB : (g + 1) * SUB, t * LANE : (t + 1) * LANE]
                    bricks[t, z, g * SUB : (g + 1) * SUB, :] = tile

    pack_bricks(jnp.where(j == GROUP - 1, 1, 0))

    def brick_spot(from_j, from_l, part):
        return volume.at[
            pl.ds(slices + slices * from_j + half * part, half), 0, pl.ds(EDGE + rows * from_l, rows)
        ]

    def brick_copy(m, e, part):
        to_q = PAIR * flip(j, m) + (l if e == 0 else 1 - l)
        source = bricks.at[to_q, pl.ds(half * part, half)]
        slot = PAIR * m + e
        if slot == 0:
            return pltpu.make_async_copy(source, brick_spot(j, l, part), brick_recv.at[part, 0])
        return remote(
            source, brick_spot(j, l, part), brick_send.at[part, slot], brick_recv.at[part, slot],
            GROUP * k + flip(j, m), PAIR * p + to_q % PAIR,
        )

    def strip_copy(m, e):
        to_q = PAIR * flip(j, m) + (l if e == 0 else 1 - l)
        target = halo_strips.at[1 + j, l]
        slot = PAIR * m + e
        if slot == 0:
            return pltpu.make_async_copy(strips.at[to_q], target, strip_recv.at[0])
        return remote(
            strips.at[to_q], target, strip_send.at[slot], strip_recv.at[slot],
            GROUP * k + flip(j, m), PAIR * p + to_q % PAIR,
        )

    every = [(m, e) for m in ORDER + (0,) for e in range(PAIR)]
    early = jnp.where(j == GROUP - 1, 1, 0)
    pl.semaphore_wait(barrier, greeted)
    for m, e in every:
        brick_copy(m, e, early).start()
    pack_bricks(1 - early)

    def pack_strips(z, packed):
        packed = list(packed)
        for g in range(row_tiles):
            i = z * row_tiles + g
            rows_at = slice(g * SUB, (g + 1) * SUB)
            for t in range(PARTS):
                left = bricks[t - 1, z, rows_at, :] if t > 0 else zero
                right = bricks[t + 1, z, rows_at, :] if t < PARTS - 1 else zero
                rims = pltpu.roll(jnp.where(lane < LANE // 2, right, left), lax.rem(4 * i + 2, LANE), 1)
                packed[t] = jnp.where(lane // 4 == i, rims, packed[t])
        return tuple(packed)

    packed = lax.fori_loop(0, slices, pack_strips, (zero,) * PARTS)
    for t in range(PARTS):
        strips[t] = packed[t]
    for m, e in every:
        strip_copy(m, e).start()
    for m, e in every:
        brick_copy(m, e, 1 - early).start()

    @pl.when(jnp.logical_not(has_below))
    def _():
        volume[half : slices, 0] = jnp.zeros((half,) + volume.shape[2:], jnp.float32)
        halo_strips[0] = jnp.zeros(halo_strips.shape[1:], jnp.float32)

    @pl.when(jnp.logical_not(has_above))
    def _():
        volume[slices + all_slices : slices + all_slices + half, 0] = jnp.zeros((half,) + volume.shape[2:], jnp.float32)
        halo_strips[GROUP + 1] = jnp.zeros(halo_strips.shape[1:], jnp.float32)


    def signal_far(number, reach):
        for exists, step in ((k >= reach, -reach), (k + reach < groups, reach)):

            @pl.when(exists)
            def _():
                pl.semaphore_signal(
                    ready_sem.at[number], inc=1, device_id=(d + GROUP * step, light), device_id_type=MESH
                )

    def wait_far(number, reach):
        count = jnp.where(k >= reach, 1, 0) + jnp.where(k + reach < groups, 1, 0)
        pl.semaphore_wait(ready_sem.at[number], count)

    reaches = far_reaches(groups)
    if reaches:
        signal_far(0, reaches[0])

    loads[2].wait()

    def pack_labels(i, carry):
        z, g = i // row_tiles, i % row_tiles
        at = lax.rem(order[z], slices)
        base = pl.multiple_of(g * SUB, SUB)
        spot = pl.multiple_of(g % chunk_tiles * SUB, SUB)
        for t in range(PARTS):
            labels_out[t % PAIR, t // PAIR, g // chunk_tiles, z, pl.ds(spot, SUB), :] = labels[at, pl.ds(base, SUB), t * LANE : (t + 1) * LANE]
        return carry

    lax.fori_loop(0, slices * row_tiles, pack_labels, 0)
    own_rows = column_labels.at[:, pl.ds(chunks // PAIR * l, chunks // PAIR)]
    keep_labels = pltpu.make_async_copy(labels_out.at[l], own_rows, mate_sem.at[0])
    mate_labels = remote(labels_out.at[1 - l], own_rows, mate_sem.at[1], mate_sem.at[2], d, PAIR * p + 1 - l)
    keep_labels.start()
    mate_labels.start()

    def wait_brick(m, e, part):
        to_q = PAIR * flip(j, m) + (l if e == 0 else 1 - l)
        if isinstance(m, int) and PAIR * m + e == 0:
            brick_copy(0, 0, part).wait()
        else:
            spot = brick_spot(flip(j, m), to_q % PAIR, part)
            remote(spot, spot, brick_send.at[part, PAIR * m + e], brick_recv.at[part, PAIR * m + e], d, light).wait_recv()

    def wait_strip(m, e):
        if PAIR * m + e == 0:
            strip_copy(0, 0).wait()
        else:
            strip_copy(m, e).wait_recv()

    halos = []
    for n, (step, own, part, target) in enumerate(
        ((-1, 0, 0, slices + all_slices), (1, GROUP - 1, 1, half))
    ):
        start = slices + slices * own + half * part
        depth = d + GROUP * step
        strip_target = GROUP + 1 if step < 0 else 0
        halos.append((
            remote(
                volume.at[pl.ds(start, half), 0, pl.ds(EDGE, all_rows)],
                volume.at[pl.ds(target, half), 0, pl.ds(EDGE, all_rows)],
                halo_send.at[n], halo_recv.at[n], depth, light,
            ),
            remote(halo_strips.at[1 + own], halo_strips.at[strip_target], halo_send.at[2 + n], halo_recv.at[2 + n], depth, light),
        ))
    for part in range(2):
        first_j = 0 if part == 0 else GROUP - 1
        for m in range(GROUP):

            @pl.when(flip(j, m) == first_j)
            def _():
                for e in range(PAIR):
                    wait_brick(m, e, part)

    for (bulk, thin), exists in zip(halos, (has_below, has_above)):
        pl.when(exists)(bulk.start)
    for number in range(len(reaches) - 1):
        wait_far(number, reaches[number])
        signal_far(number + 1, reaches[number + 1])
    for m, e in every:
        wait_strip(m, e)
    for (bulk, thin), exists in zip(halos, (has_below, has_above)):
        pl.when(exists)(thin.start)

    keep_labels.wait()
    mate_labels.wait_recv()
    def label_copy(c, m):
        return remote(
            column_labels.at[flip(j, m), c], materials.at[c, pl.ds(slices * j, slices)],
            label_send.at[c, m - 1], label_recv.at[c, m - 1], GROUP * k + flip(j, m), light,
        )

    def send_labels(c, carry):
        for m in ORDER:
            label_copy(c, m).start()
        return carry

    lax.fori_loop(0, chunks, send_labels, 0)
    own_labels = pltpu.make_async_copy(column_labels.at[j], materials.at[:, pl.ds(slices * j, slices)], mate_sem.at[0])
    own_labels.start()

    def unpack(b, carry):
        for l_from in range(PAIR):
            strip = halo_strips[b, l_from]
            for z in range(slices):
                for g in range(row_tiles):
                    i = z * row_tiles + g
                    at = EDGE + rows * l_from + SUB * g
                    volume[slices * b + z, 1, at : at + SUB] = pltpu.roll(strip, (2 * LANE - 4 * i - 2) % LANE, 1)
        return carry

    lax.fori_loop(1, GROUP + 1, unpack, 0)

    def zero_edge(at):
        for t in range(2):
            for z in range(half, all_slices + slices + half):
                volume[z, t, at : at + SUB] = zero

    pl.when(jnp.logical_not(has_before))(lambda: zero_edge(EDGE - SUB))
    pl.when(jnp.logical_not(has_after))(lambda: zero_edge(EDGE + all_rows))

    def clear_rim(at):
        for s in range(1, all_slices + 1):
            smooth[s, 0, at : at + SUB] = zero

    def clear_rims():
        pl.when(jnp.logical_not(has_before))(lambda: clear_rim(0))
        pl.when(jnp.logical_not(has_after))(lambda: clear_rim(SUB + all_rows))

    if pairs == 1:
        clear_rims()

    loads[3].wait()
    loads[4].wait()
    tables = [zero for _ in range(4)]
    for n in range(extinction.shape[0]):
        tables[0] = jnp.where(lane == n, extinction[n], tables[0])
        for c in range(3):
            tables[c + 1] = jnp.where(lane == n, albedo[c, n], tables[c + 1])


    for part in range(2):
        first_j = 0 if part == 0 else GROUP - 1
        for m in range(GROUP):

            @pl.when(flip(j, m) != first_j)
            def _():
                for e in range(PAIR):
                    wait_brick(m, e, part)

    for n, exists in ((1, has_below), (0, has_above)):

        @pl.when(exists)
        def _():
            halos[n][0].wait_recv()
            halos[n][1].wait_recv()

    for b in (0, GROUP + 1):
        unpack(b, 0)

    edges = []
    if pairs > 1:
        for n, (step, source, target, exists) in enumerate(
            ((-PAIR, EDGE, EDGE + all_rows, has_before), (PAIR, EDGE + all_rows - SUB, EDGE - SUB, has_after))
        ):
            edges.append((
                remote(
                    volume.at[:, :, pl.ds(source, SUB)], volume.at[:, :, pl.ds(target, SUB)],
                    edge_send.at[n], edge_recv.at[n], d, light + step,
                ),
                exists,
            ))
        for one, exists in edges:
            pl.when(exists)(one.start)

    if pairs > 1:
        for n, exists in ((0, has_after), (1, has_before)):
            pl.when(exists)(edges[n][0].wait_recv)
    below = jnp.where(has_below, 1.0, 0.0)
    above = jnp.where(has_above, 1.0, 0.0)
    inside = jnp.where(lane < LANE // 2, jnp.where(q < PARTS - 1, 1.0, 0.0), jnp.where(q > 0, 1.0, 0.0))
    lane_first, lane_last = lane == 0, lane == LANE - 1

    def smooth_tile(g, carry):
        base = pl.multiple_of(EDGE + g * SUB, SUB)
        target = pl.multiple_of(SUB + g * SUB, SUB)
        at = pl.ds(base, SUB)

        def both(z):
            return [volume[z, t, at] for t in range(2)]

        first = slices - 1
        before, center = both(first - 1), both(first)
        for s in range(all_slices + 2):
            z = first + s
            after = both(z + 1)
            for t in range(2 if 0 < s <= all_slices else 1):
                own, other = center[t], center[1 - t]
                low = pltpu.roll(jnp.where(lane_last, other, own), 1, 1)
                high = pltpu.roll(jnp.where(lane_first, other, own), LANE - 1, 1)
                up = volume[z, t, pl.ds(base - 1, SUB)]
                down = volume[z, t, pl.ds(base + 1, SUB)]
                value = 0.4 * own + 0.1 * ((before[t] + after[t]) + (up + down) + (low + high))
                if s == 0:
                    value = value * below
                if s == all_slices + 1:
                    value = value * above
                if t == 1:
                    value = value * inside
                smooth[s, t, pl.ds(target, SUB)] = value
            before, center = center, after
        return carry

    ends = 1 if pairs > 1 else 0
    lax.fori_loop(-ends, all_rows // SUB + ends, smooth_tile, 0)

    if pairs > 1:
        clear_rims()

    def slope_tile(g, carry):
        base = pl.multiple_of(SUB + g * SUB, SUB)
        target = pl.ds(pl.multiple_of(g * SUB, SUB), SUB)
        at = pl.ds(base, SUB)
        before, center = smooth[0, 0, at], smooth[1, 0, at]
        for z in range(all_slices):
            after = smooth[z + 2, 0, at]
            beside = smooth[z + 1, 1, at]
            low = pltpu.roll(jnp.where(lane_last, beside, center), 1, 1)
            high = pltpu.roll(jnp.where(lane_first, beside, center), LANE - 1, 1)
            up = smooth[z + 1, 0, pl.ds(base - 1, SUB)]
            down = smooth[z + 1, 0, pl.ds(base + 1, SUB)]
            grad_z, grad_x, grad_y = after - before, down - up, high - low
            facing = grad_x * lax.rsqrt(grad_z * grad_z + grad_x * grad_x + grad_y * grad_y + 0.2)
            heat[z, target] = jnp.exp(center)
            turned[z, target] = 0.5 + 0.5 * facing
            before, center = center, after
        return carry

    lax.fori_loop(0, all_rows // SUB, slope_tile, 0)

    def unit_copy(u):
        return remote(
            parts_out.at[pl.ds(GROUP * u, GROUP)], parts_mid.at[u // groups, k],
            mid_send.at[u], mid_recv.at[u // groups], GROUP * (u % groups) + j, light,
        )

    def send_unit(u):
        @pl.when(u % groups != k)
        def _():
            unit_copy(u).start()

        @pl.when(u % groups == k)
        def _():
            pltpu.make_async_copy(
                parts_out.at[pl.ds(GROUP * u, GROUP)], parts_mid.at[u // groups, k], mid_recv.at[u // groups]
            ).start()

    def owned_here(u, i):
        return (u % groups == k) & (u // groups == l) & (j == i)

    def owner_copy(source, target, send, recv, u, i):
        return remote(source, target, send, recv, GROUP * (u % groups) + i, PAIR * p + u // groups)

    def send_owner(source, target, send, recv, u, i):
        own = owned_here(u, i)

        @pl.when(jnp.logical_not(own))
        def _():
            owner_copy(source, target, send, recv, u, i).start()

        @pl.when(own)
        def _():
            pltpu.make_async_copy(source, target, recv).start()

    def direct_parts(u, i):
        send = direct_send.at[u - direct_from, i]
        return parts_out.at[GROUP * u + i], direct_last.at[k, q], send, direct_recv, u, i

    def merged_parts(to_l, i):
        send = last_send.at[to_l, i]
        return parts_merged.at[to_l, i], parts_last.at[q], send, last_recv, to_l * groups + k, i

    paired = 2 * block_rows == SUB
    top = sub < SUB // 2

    def turn(value):
        return pltpu.roll(value, SUB // 2, 0)

    def fetch(ref, at):
        if paired:
            return [ref[at + (pl.ds(SUB * n, SUB),)] for n in range(2)]
        return [ref[at + (pl.ds(block_rows * c, block_rows),)] for c in range(4)]

    def keep(ref, at, values):
        size = SUB if paired else block_rows
        for n, value in enumerate(values):
            ref[at + (pl.ds(size * n, size),)] = value

    def over(fronts):
        back = fronts[-1]
        for front in reversed(fronts[:-1]):
            shade = jnp.where(top, turn(front[-1]), front[-1]) if paired else front[-1]
            clear = 1.0 - shade
            back = [one + clear * other for one, other in zip(front, back)]
        return back

    per_tile = SUB // block_rows

    def shade_tile(g, lights):
        at = pl.ds(pl.multiple_of(g * SUB, SUB), SUB)
        spot = pl.ds(pl.multiple_of(g % chunk_tiles * SUB, SUB), SUB)
        lights = list(lights)
        remaining = jnp.ones((SUB, LANE), jnp.float32)
        colours = [zero] * 3
        for z in range(all_slices):
            index = materials[g // chunk_tiles, z, spot]
            passed = jnp.exp(-(lookup(tables[0], index) * heat[z, at]))
            ahead = jnp.where(sub >= 1, pltpu.roll(passed, 1, 0), lights[z])
            for step in (1, 2, 4):
                ahead = ahead * jnp.where(sub >= step, pltpu.roll(ahead, step, 0), 1.0)
            lights[z] = jnp.broadcast_to((ahead * passed)[SUB - 1 :], (SUB, LANE))
            weight = (1.0 - passed) * remaining * (0.2 + ahead * turned[z, at])
            for c in range(3):
                colours[c] = colours[c] + lookup(tables[c + 1], index) * weight
            remaining = remaining * passed
        values = colours + [1.0 - remaining]
        for b in range(per_tile):
            if paired and b == 0:
                block = [jnp.where(top, values[n], turn(values[n + 1])) for n in (0, 2)]
            elif paired:
                block = [jnp.where(top, turn(values[n]), values[n + 1]) for n in (0, 2)]
            else:
                block = [value[b * block_rows : (b + 1) * block_rows] for value in values]
            keep(parts_out, (g * per_tile + b,), block)
        return tuple(lights)

    lights = (jnp.ones((SUB, LANE), jnp.float32),) * all_slices
    if pairs > 1:
        light_copy = remote(lights_out, lights_in, light_send, light_recv, d, light + PAIR)

        @pl.when(has_before)
        def _():
            light_copy.wait_recv()

        @pl.when(jnp.logical_not(has_before))
        def _():
            for z in range(all_slices):
                lights_in[z] = jnp.ones((SUB, LANE), jnp.float32)

        lights = tuple(lights_in[z] for z in range(all_slices))

    if reaches:
        wait_far(len(reaches) - 1, reaches[-1])
    own_labels.wait()

    def shade_wait(g, n, lights):
        if n % chunk_tiles == 0:
            for m in ORDER:
                label_copy(g // chunk_tiles, m).wait_recv()
        return shade_tile(g, lights)

    def merged_step(step, lights):
        for n in range(step_tiles):
            lights = shade_wait(step * step_tiles + n, n, lights)
        for n in range(step_units):
            send_unit(step * step_units + n)
        return lights

    def direct_step(step, lights):
        for n in range(step_tiles):
            g = step * step_tiles + n
            lights = shade_wait(g, n, lights)
            for b in range(per_tile):
                block = g * per_tile + b
                send_owner(*direct_parts(block // GROUP, block % GROUP))
        return lights

    def bytes_of(ref, sem):
        pltpu.make_async_copy(ref, ref, sem).wait()

    def merge(to_l):
        bytes_of(parts_mid.at[to_l], mid_recv.at[to_l])
        for i in range(GROUP):
            keep(parts_merged, (to_l, i), over([fetch(parts_mid, (to_l, front, i)) for front in range(groups)]))
        for i in range(GROUP):
            send_owner(*merged_parts(to_l, i))

    def merges_far(to_l):
        return to_l * groups + k < direct_from

    def late_step(step, lights):
        pl.when(step == merge_step)(lambda: merge(0))
        return direct_step(step, lights)

    lights = lax.fori_loop(0, merged_steps, merged_step, lights)
    lights = lax.fori_loop(merged_steps, steps, late_step, lights)
    pl.when(merge_step == steps)(lambda: merge(0))
    if pairs > 1:
        for z in range(all_slices):
            lights_out[z] = lights[z]
        pl.when(has_after)(light_copy.start)

    for part in range(2):
        for m, e in every:
            if (m, e) != (0, 0):
                brick_copy(m, e, part).wait_send()
    for m, e in every:
        if (m, e) != (0, 0):
            strip_copy(m, e).wait_send()
    mate_labels.wait_send()
    for (bulk, thin), exists in zip(halos, (has_below, has_above)):

        @pl.when(exists)
        def _():
            bulk.wait_send()
            thin.wait_send()

    def sent_labels(c, carry):
        for m in ORDER:
            label_copy(c, m).wait_send()
        return carry

    lax.fori_loop(0, chunks, sent_labels, 0)

    def sent_unit(u, carry):
        @pl.when(u % groups != k)
        def _():
            unit_copy(u).wait_send()

        return carry

    lax.fori_loop(0, direct_from, sent_unit, 0)

    def sent_direct(u, carry):
        for i in range(GROUP):

            @pl.when(jnp.logical_not(owned_here(u, i)))
            def _():
                owner_copy(*direct_parts(u, i)).wait_send()

        return carry

    lax.fori_loop(direct_from, units, sent_direct, 0)
    for to_l in range(PAIR):
        for i in range(GROUP):

            @pl.when(merges_far(to_l) & jnp.logical_not(owned_here(to_l * groups + k, i)))
            def _():
                owner_copy(*merged_parts(to_l, i)).wait_send()

    for one, exists in edges:
        pl.when(exists)(one.wait_send)
    if pairs > 1:
        pl.when(has_after)(light_copy.wait_send)

    own_far = l * groups + k < direct_from

    @pl.when(own_far)
    def _():
        bytes_of(parts_last, last_recv)
        for n in range(PARTS):
            keep(blended, (n,), fetch(parts_last, (n,)))

    @pl.when(jnp.logical_not(own_far))
    def _():
        bytes_of(direct_last, direct_recv)
        for n in range(PARTS):
            keep(blended, (n,), over([fetch(direct_last, (front, n)) for front in range(groups)]))

    for n in range(PARTS):
        for r in range(block_rows):
            at = r * PARTS * LANE + n * LANE
            out[:, at : at + LANE] = blended[n, pl.ds(r, 4, stride=block_rows), :]


def shards(density, labels, slice_order, extinction, albedo):
    depth_count = lax.axis_size("depth")
    light_count = lax.axis_size("light")
    slices, rows, columns = density.shape
    groups = depth_count // GROUP
    block_rows = rows // depth_count
    all_rows, all_slices = PAIR * rows, GROUP * slices
    units = PAIR * groups
    chunk_rows = CHUNK_TILES * SUB
    chunks = all_rows // chunk_rows
    f32, i32 = jnp.float32, jnp.int32
    vmem, smem, dma = pltpu.VMEM, pltpu.SMEM, pltpu.SemaphoreType.DMA
    scratch = [
        vmem(density.shape, f32),
        vmem(labels.shape, i32),
        smem(slice_order.shape, i32),
        smem(extinction.shape, f32),
        smem(albedo.shape, f32),
        vmem((PARTS, slices, rows, LANE), f32),
        vmem((PARTS, SUB, LANE), f32),
        vmem((PAIR, GROUP, chunks // PAIR, slices, chunk_rows, LANE), i32),
        vmem((GROUP, chunks, slices, chunk_rows, LANE), i32),
        vmem((all_slices + 2 * slices, 2, all_rows + 2 * EDGE, LANE), f32),
        vmem((GROUP + 2, PAIR, SUB, LANE), f32),
        vmem((chunks, all_slices, chunk_rows, LANE), i32),
        vmem((all_slices + 2, 2, all_rows + 2 * SUB, LANE), f32),
        vmem((all_slices, all_rows, LANE), f32),
        vmem((all_slices, all_rows, LANE), f32),
        vmem((PAIR * depth_count, 4 * block_rows, LANE), f32),
        vmem((PAIR, groups, GROUP, 4 * block_rows, LANE), f32),
        vmem((PAIR, GROUP, 4 * block_rows, LANE), f32),
        vmem((PARTS, 4 * block_rows, LANE), f32),
        vmem((groups, PARTS, 4 * block_rows, LANE), f32),
        vmem((PARTS, SUB * block_rows, LANE), f32),
        vmem((all_slices, SUB, LANE), f32),
        vmem((all_slices, SUB, LANE), f32),
        dma((5,)),
        dma((2, PARTS)),
        dma((2, PARTS)),
        dma((PARTS,)),
        dma((PARTS,)),
        dma((3,)),
        dma((chunks, GROUP - 1)),
        dma((chunks, GROUP - 1)),
        dma((4,)),
        dma((4,)),
        dma((2,)),
        dma((2,)),
        dma(()),
        dma(()),
        pltpu.SemaphoreType.REGULAR((max(1, len(far_reaches(groups))),)),
        dma((units,)),
        dma((PAIR,)),
        dma((PAIR, GROUP)),
        dma(()),
        dma((units, GROUP)),
        dma(()),
    ]
    image = pl.pallas_call(
        functools.partial(render_kernel, depth_count, light_count),
        in_specs=[FAR] * 5,
        out_specs=pl.BlockSpec(memory_space=pltpu.VMEM),
        out_shape=jax.ShapeDtypeStruct((4, block_rows * columns), f32),
        scratch_shapes=scratch,
        compiler_params=pltpu.CompilerParams(
            collective_id=0, has_side_effects=True, vmem_limit_bytes=40 * 1024 * 1024
        ),
    )(*(pltpu.with_memory_space_constraint(one, pltpu.HBM) for one in (density, labels, slice_order, extinction, albedo)))
    return image


def solution(mesh):
    return jax.shard_map(
        shards,
        mesh=mesh,
        in_specs=(P("depth", "light", None), P("depth", "light", None), P("depth"), P(), P()),
        out_specs=P(None, ("light", "depth")),
        check_vma=False,
    )
```
